128 devices in a mesh: req: 128 (over y, x, z, core).
Axes of the slice: x: 4, y: 4, z: 4, core: 2. Of those that a mesh axis runs over, the one named last changes fastest.
Arguments:
- prefill_hidden: bfloat16 [32768, 1280], P('req'), may hold values from -6 to 6
- decode_hidden: bfloat16 [256, 1280], P('req'), may hold values from -6 to 6
- attn_gain: float32 [1280], replicated, may hold values from 0.1 to 1.9
- w_qkv: bfloat16 [1280, 1920], replicated
- w_out: bfloat16 [1280, 1280], replicated, may hold values from -0.15625 to 0.15625
- ffn_gain: float32 [1280], replicated, may hold values from 0.1 to 1.9
- w_gate_up: bfloat16 [128, 1280, 448], P('req'), as said below
- w_down: bfloat16 [128, 224, 1280], P('req'), as said below
- key_value_cache: bfloat16 [512, 1024, 640], P('req'), may hold values from -6 to 6
- cache_len: int32 [512], P('req'), may hold values from 64 to 1024, as said below
- slot_of_request: int32 [256], replicated, may hold values from 0 to 511, as said below
- held_hidden: bfloat16 [131072, 1280], P('req'), may hold values from -6 to 6
- recomputed_index: int32 [131072], P('req'), may hold values from 0 to 4095, as said below
- recomp_count: int32 [128], P('req'), may hold values from 512 to 1024, as said below
Outputs:
- prefill_out: bfloat16 [32768, 1280], P('req')
- decode_out: bfloat16 [256, 1280], P('req')
The draws below stay inside these ranges and needn't reach their ends.
Inputs may be any that keep to these rules, and one draw needn't show every extreme that they name: `slot_of_request`: distinct slot numbers; slot s belongs to device s div 4; some device holds 4 requests. `cache_len`: some slot that holds a request has length 1024. `recomputed_index`: within one device's list the entries are distinct. Only the first recomp_count[d] entries of device d's list are live; some device has 1024. `w_gate_up`: copy n equals copy n mod 16. `w_down`: copy n equals copy n mod 16.
All inputs are finite; a program needn't handle non-finite values.
Results may differ from the reference program's by a relative error of at most 0.015.
Values may be sent and summed in bfloat16 or wider, within the bound.
No kernel may reach another device: no remote copies, remote signals or barrier semaphores. Data moves between devices by JAX's collectives and lax.ppermute only.
A program may use at most 192 MiB of HBM per device.

```python
import math
import jax
import jax.numpy as jnp
from jax import lax

MODEL_WIDTH = 1280
QUERY_HEADS = 20
KEY_VALUE_HEADS = 5
HEAD_SIZE = 64
FF = 3584
GROUP = 16
PRE_DEV = 256
PREFILL_TOKENS = 1024
SLOTS = 4
CACHE_POSITIONS = 1024
RECOMP = 1024
PREFILLS = 32
DECODES = 256
SLOT_TOTAL = 512
N_REQ = 128


def favoured(key):
    return jax.random.randint(jax.random.fold_in(key, 41), (), 0, N_REQ)


def draw_w_qkv(key, part):
    query_width = QUERY_HEADS * HEAD_SIZE
    key_value_width = KEY_VALUE_HEADS * HEAD_SIZE
    rotary_base = jax.random.normal(jax.random.fold_in(key, 31), (MODEL_WIDTH, query_width + 2 * key_value_width), jnp.float32) / math.sqrt(MODEL_WIDTH)
    query_rows = rotary_base[:, :query_width]
    random_noise = rotary_base[:, query_width:query_width + key_value_width].reshape(MODEL_WIDTH, KEY_VALUE_HEADS, HEAD_SIZE)
    value_rows = rotary_base[:, query_width + key_value_width:]
    mean_square = query_rows.reshape(MODEL_WIDTH, KEY_VALUE_HEADS, QUERY_HEADS // KEY_VALUE_HEADS, HEAD_SIZE).mean(axis=2)
    noise_strength = jax.random.uniform(jax.random.fold_in(key, 37), (KEY_VALUE_HEADS,), jnp.float32, 1.5, 3.5)
    key_rows = noise_strength[None, :, None] * mean_square + random_noise
    return jnp.concatenate([query_rows, key_rows.reshape(MODEL_WIDTH, key_value_width), value_rows], axis=1).astype(jnp.bfloat16)


def draw_w_gate_up(key, part):
    rotary_base = jax.random.normal(jax.random.fold_in(key, 71), (GROUP, MODEL_WIDTH, 2 * FF // GROUP), jnp.float32) / math.sqrt(MODEL_WIDTH)
    return jnp.tile(rotary_base, (N_REQ // GROUP, 1, 1)).astype(jnp.bfloat16)


def draw_w_down(key, part):
    rotary_base = jax.random.normal(jax.random.fold_in(key, 73), (GROUP, FF // GROUP, MODEL_WIDTH), jnp.float32) / math.sqrt(FF)
    return jnp.tile(rotary_base, (N_REQ // GROUP, 1, 1)).astype(jnp.bfloat16)


def draw_slot_of_request(key, part):
    total_slots = SLOTS * N_REQ
    ranking = jax.random.permutation(jax.random.fold_in(key, 43), total_slots).astype(jnp.int32)
    holder = jnp.arange(total_slots, dtype=jnp.int32) // SLOTS
    score = jnp.where(holder == favoured(key), ranking - total_slots, ranking)
    chosen = jnp.argsort(score, stable=True)[:DECODES].astype(jnp.int32)
    shuffle = jax.random.permutation(jax.random.fold_in(key, 47), DECODES)
    return chosen[shuffle].astype(jnp.int32)


def draw_cache_len(key, part):
    lengths = jax.random.randint(jax.random.fold_in(key, 53), (SLOTS * N_REQ,), CACHE_POSITIONS // 16, CACHE_POSITIONS + 1)
    return lengths.at[favoured(key) * SLOTS].set(CACHE_POSITIONS).astype(jnp.int32)


def draw_recomputed_index(key, part):
    subkeys = jax.random.split(jax.random.fold_in(key, 59), N_REQ)

    def pick_positions(subkey):
        return jax.random.permutation(subkey, SLOTS * CACHE_POSITIONS)[:RECOMP]
    return jax.vmap(pick_positions)(subkeys).reshape(-1).astype(jnp.int32)


def draw_recomp_count(key, part):
    counts = jax.random.randint(jax.random.fold_in(key, 61), (N_REQ,), RECOMP // 2, RECOMP + 1)
    full_device = jax.random.randint(jax.random.fold_in(key, 67), (), 0, N_REQ)
    return counts.at[full_device].set(RECOMP).astype(jnp.int32)


def steps_of(key, dims, cuts, low, top_value):
    factor_of, own = 1.0, jax.random.fold_in(key, 6)
    for position, shards_of in cuts:
        steps = jnp.exp(jax.random.uniform(jax.random.fold_in(own, position), (shards_of,), jnp.float32, low / len(cuts), top_value / len(cuts)))
        factor_of = factor_of * jnp.repeat(steps, dims[position] // shards_of).reshape([-1 if axis == position else 1 for axis in range(len(dims))])
    return factor_of


def gaussian(own_key, extent, scale, most, pieces=(), kind=jnp.bfloat16):
    level = steps_of(own_key, extent, pieces, -0.22, 0.18) if pieces else 1.0
    values = jax.random.normal(own_key, extent, jnp.float32) * scale * level
    return jnp.minimum(jnp.maximum(values, -most), most).astype(kind)


def setup_inputs(seed: int = 0) -> dict:
    splits = jax.random.split(jax.random.key(seed), 15)
    prefill_hidden = gaussian(splits[0], (PREFILLS * PREFILL_TOKENS, MODEL_WIDTH), 1.0, 6.0, ((0, 128),))
    decode_hidden = gaussian(splits[1], (DECODES, MODEL_WIDTH), 1.0, 6.0, ((0, 128),))
    attn_gain = jnp.clip(1.0 + 0.18 * jax.random.normal(splits[2], (MODEL_WIDTH,), jnp.float32), 0.1, 1.9)
    w_qkv = draw_w_qkv(jax.random.fold_in(splits[14], 71), 0)
    w_out = gaussian(splits[4], (MODEL_WIDTH, MODEL_WIDTH), MODEL_WIDTH ** -0.5, 0.15625)
    ffn_gain = jnp.clip(1.0 + 0.18 * jax.random.normal(splits[5], (MODEL_WIDTH,), jnp.float32), 0.1, 1.9)
    w_gate_up = draw_w_gate_up(jax.random.fold_in(splits[14], 71), 0)
    w_down = draw_w_down(jax.random.fold_in(splits[14], 71), 0)
    key_value_cache = gaussian(splits[8], (SLOT_TOTAL, CACHE_POSITIONS, 2 * KEY_VALUE_HEADS * HEAD_SIZE), 1.0, 6.0, ((0, 128),))
    cache_len = draw_cache_len(jax.random.fold_in(splits[14], 71), 0)
    slot_of_request = draw_slot_of_request(jax.random.fold_in(splits[14], 71), 0)
    held_hidden = gaussian(splits[11], (RECOMP * N_REQ, MODEL_WIDTH), 1.0, 6.0, ((0, 128),))
    recomputed_index = draw_recomputed_index(jax.random.fold_in(splits[14], 71), 0)
    recomp_count = draw_recomp_count(jax.random.fold_in(splits[14], 71), 0)
    return {"prefill_hidden": prefill_hidden, "decode_hidden": decode_hidden, "attn_gain": attn_gain, "w_qkv": w_qkv, "w_out": w_out, "ffn_gain": ffn_gain, "w_gate_up": w_gate_up, "w_down": w_down, "key_value_cache": key_value_cache, "cache_len": cache_len, "slot_of_request": slot_of_request, "held_hidden": held_hidden, "recomputed_index": recomputed_index, "recomp_count": recomp_count}


eps = 1e-05
theta = 10000.0
masked_score = -1e+30

def rms_scale(value_rows, gain):
    as_float = value_rows.astype(jnp.float32)
    return as_float * lax.rsqrt(lax.optimization_barrier(jnp.mean(as_float * as_float, axis=-1, keepdims=True)) + eps) * gain

def apply_rotary(heads, token_positions):
    half = heads.shape[-1] // 2
    frequency = theta ** (-(jnp.arange(half).astype(jnp.float32) * 2.0 / heads.shape[-1]))
    angle = token_positions.astype(jnp.float32)[:, None] * frequency[None, :]
    cosine = jnp.cos(angle)[:, None, :]
    sine = jnp.sin(angle)[:, None, :]
    first = heads[..., :half]
    second = heads[..., half:]
    return jnp.concatenate([first * cosine - second * sine, second * cosine + first * sine], axis=-1)

def attend(query, key_rows, value_rows, mask):
    query_len = query.shape[0]
    heads_kv = key_rows.shape[1]
    group = query.shape[1] // heads_kv
    query_groups = query.reshape(query_len, heads_kv, group, key_rows.shape[2]).astype(jnp.float32)
    scores = jnp.einsum('qhgd,khd->hgqk', query_groups, key_rows.astype(jnp.float32)) * key_rows.shape[2] ** (-0.5)
    scores = jnp.where(mask[None, None], scores, masked_score)
    top = lax.optimization_barrier(jnp.max(scores, axis=-1, keepdims=True))
    weights = jnp.where(mask[None, None], jnp.exp(scores - top), 0.0)
    total = lax.optimization_barrier(jnp.sum(weights, axis=-1))
    rounded = lax.optimization_barrier(weights.astype(jnp.bfloat16)).astype(jnp.float32)
    mixed = jnp.einsum('hgqk,khd->qhgd', rounded, value_rows.astype(jnp.float32))
    mixed = mixed / jnp.transpose(total, (2, 0, 1))[..., None]
    return mixed.reshape(query_len, -1).astype(jnp.bfloat16)

def finish(hidden, mixed, w_out, ffn_gain, w_gate_up, w_down):
    projection = jnp.dot(mixed, w_out, preferred_element_type=jnp.float32)
    resid = (hidden.astype(jnp.float32) + projection).astype(jnp.bfloat16)
    normed = rms_scale(resid, ffn_gain).astype(jnp.bfloat16)
    gated = jnp.dot(normed, w_gate_up, preferred_element_type=jnp.float32)
    hidden_units = w_down.shape[0]
    act = (jax.nn.silu(gated[:, :hidden_units]) * gated[:, hidden_units:]).astype(jnp.bfloat16)
    down = jnp.dot(act, w_down, preferred_element_type=jnp.float32)
    return (resid.astype(jnp.float32) + down).astype(jnp.bfloat16)

def reference(prefill_hidden, decode_hidden, attn_gain, w_qkv, w_out, ffn_gain, w_gate_up, w_down, key_value_cache, cache_len, slot_of_request, held_hidden, recomputed_index, recomp_count):
    query_width = QUERY_HEADS * HEAD_SIZE
    key_value_width = KEY_VALUE_HEADS * HEAD_SIZE
    share = FF // GROUP
    block_span = PREFILL_TOKENS // PRE_DEV
    shards = w_gate_up[:GROUP]
    gate_full = jnp.transpose(shards[:, :, :share], (1, 0, 2)).reshape(MODEL_WIDTH, FF)
    up_full = jnp.transpose(shards[:, :, share:], (1, 0, 2)).reshape(MODEL_WIDTH, FF)
    gate_up_full = jnp.concatenate([gate_full, up_full], axis=1)
    down_full = w_down[:GROUP].reshape(FF, MODEL_WIDTH)

    def one_prefill(prefill_block_rows):
        normed = rms_scale(prefill_block_rows, attn_gain).astype(jnp.bfloat16)
        projected_rows = jnp.dot(normed, w_qkv, preferred_element_type=jnp.float32)
        stored = jnp.arange(PREFILL_TOKENS).astype(jnp.int32)
        token_positions = (stored % PRE_DEV * block_span + stored // PRE_DEV).astype(jnp.int32)
        query = apply_rotary(projected_rows[:, :query_width].reshape(PREFILL_TOKENS, QUERY_HEADS, HEAD_SIZE), token_positions).astype(jnp.bfloat16)
        key_rows = apply_rotary(projected_rows[:, query_width:query_width + key_value_width].reshape(PREFILL_TOKENS, KEY_VALUE_HEADS, HEAD_SIZE), token_positions).astype(jnp.bfloat16)
        value_rows = projected_rows[:, query_width + key_value_width:].astype(jnp.bfloat16).reshape(PREFILL_TOKENS, KEY_VALUE_HEADS, HEAD_SIZE)
        mask = token_positions[None, :] <= token_positions[:, None]
        mixed = attend(query, key_rows, value_rows, mask)
        return finish(prefill_block_rows, mixed, w_out, ffn_gain, gate_up_full, down_full)
    prefill_out = lax.map(one_prefill, prefill_hidden.reshape(PREFILLS, PREFILL_TOKENS, MODEL_WIDTH)).reshape(PREFILLS * PREFILL_TOKENS, MODEL_WIDTH)
    normed_decode = rms_scale(decode_hidden, attn_gain).astype(jnp.bfloat16)
    decode_projected = jnp.dot(normed_decode, w_qkv, preferred_element_type=jnp.float32).astype(jnp.bfloat16)
    normed_held = rms_scale(held_hidden, attn_gain).astype(jnp.bfloat16)
    kept_key_value = jnp.dot(normed_held, w_qkv[:, query_width:], preferred_element_type=jnp.float32)
    kept_positions = (recomputed_index % CACHE_POSITIONS).astype(jnp.int32)
    kept_keys = apply_rotary(kept_key_value[:, :key_value_width].reshape(-1, KEY_VALUE_HEADS, HEAD_SIZE), kept_positions).reshape(-1, key_value_width)
    recomputed = jnp.concatenate([kept_keys, kept_key_value[:, key_value_width:]], axis=1).astype(jnp.bfloat16)
    order = jnp.arange(RECOMP).astype(jnp.int32)

    def one_decode(inputs):
        row_number, slot = inputs
        device = (slot // SLOTS).astype(jnp.int32)
        local = (slot % SLOTS).astype(jnp.int32)
        length = lax.dynamic_index_in_dim(cache_len, slot, 0, keepdims=False)
        slot_cache = lax.dynamic_index_in_dim(key_value_cache, slot, 0, keepdims=False)
        start = (device * RECOMP).astype(jnp.int32)
        fresh_rows = lax.dynamic_slice_in_dim(recomputed, start, RECOMP, 0)
        index = lax.dynamic_slice_in_dim(recomputed_index, start, RECOMP, 0)
        count = lax.dynamic_index_in_dim(recomp_count, device, 0, keepdims=False)
        valid = (index // CACHE_POSITIONS == local) & (order < count)
        target = jnp.where(valid, index % CACHE_POSITIONS, CACHE_POSITIONS).astype(jnp.int32)
        slot_cache = slot_cache.at[target].set(fresh_rows, mode='drop')
        token_position = length.reshape(1)
        query = apply_rotary(row_number[:query_width].astype(jnp.float32).reshape(1, QUERY_HEADS, HEAD_SIZE), token_position).astype(jnp.bfloat16)
        newest_key = apply_rotary(row_number[query_width:query_width + key_value_width].astype(jnp.float32).reshape(1, KEY_VALUE_HEADS, HEAD_SIZE), token_position).astype(jnp.bfloat16)
        key_rows = jnp.concatenate([slot_cache[:, :key_value_width].reshape(CACHE_POSITIONS, KEY_VALUE_HEADS, HEAD_SIZE), newest_key], axis=0)
        value_rows = jnp.concatenate([slot_cache[:, key_value_width:].reshape(CACHE_POSITIONS, KEY_VALUE_HEADS, HEAD_SIZE), row_number[query_width + key_value_width:].reshape(1, KEY_VALUE_HEADS, HEAD_SIZE)], axis=0)
        places = jnp.arange(CACHE_POSITIONS + 1).astype(jnp.int32)
        mask = ((places < length) | (places == CACHE_POSITIONS))[None, :]
        return attend(query, key_rows, value_rows, mask)[0]
    decode_mixed = lax.map(one_decode, (decode_projected, slot_of_request))
    decode_out = finish(decode_hidden, decode_mixed, w_out, ffn_gain, gate_up_full, down_full)
    return (prefill_out, decode_out)
```

```python
import functools

import jax
import jax.numpy as jnp
from jax import lax
from jax.experimental import pallas as pl
from jax.experimental.pallas import tpu as pltpu
from jax.sharding import PartitionSpec as P

WIDTH = 1280
QUERY_HEADS = 20
HEAD = 64
QW = 1280
KVW = 640
SHARE = 224
GROUP = 16
SIDE = 4
SLOTS = 4
POSITIONS = 1024
ROWS = 256
HALF = 144
EPS = 1e-05
THETA = 10000.0
NEG = -1e30
F32 = jnp.float32
BF = jnp.bfloat16
NT = (((1,), (1,)), ((), ()))
VMEM_LIMIT = 56 << 20


def place(y, x, z, core):
    return (((y % SIDE) * SIDE + x % SIDE) * SIDE + z % SIDE) * 2 + core


def moves(step):
    pairs = []
    for y in range(SIDE):
        for x in range(SIDE):
            for z in range(SIDE):
                for core in range(2):
                    pairs.append((place(y, x, z, core), place(*step(y, x, z, core))))
    return pairs


def send(array, step):
    return lax.ppermute(array, "req", moves(step))


def other_core(y, x, z, core):
    return y, x, z, 1 - core


def next_x(y, x, z, core):
    return y, x + 1, z, core


def last_x(y, x, z, core):
    return y, x - 1, z, core


def pair_z(y, x, z, core):
    return y, x, z ^ 1, core


def norm_rows(rows, gain):
    rows = rows.astype(F32)
    mean = jnp.mean(rows * rows, axis=-1, keepdims=True)
    return (rows * lax.rsqrt(mean + EPS) * gain).astype(BF)


def lanes(shape):
    return lax.broadcasted_iota(jnp.int32, shape, len(shape) - 1)


def sublanes(shape):
    return lax.broadcasted_iota(jnp.int32, shape, len(shape) - 2)


def rope_tables(position, frequency):
    angle = position * frequency
    sine = jnp.sin(angle)
    low = lanes(angle.shape) % HEAD < HEAD // 2
    return jnp.cos(angle), jnp.where(low, -sine, sine)


def rope(chunk, cosine, sine):
    low = lanes(chunk.shape) % HEAD < HEAD // 2
    other = jnp.where(low, pltpu.roll(chunk, 96, 1), pltpu.roll(chunk, 32, 1))
    return chunk * cosine + other * sine


def pack_kernel(gate_up_ref, down_ref, packed_ref):
    packed_ref[: 2 * SHARE, :] = gate_up_ref[...].astype(F32).T.astype(BF)
    packed_ref[2 * SHARE :, :] = down_ref[...]


def pack_weights(w_gate_up, w_down):
    return pl.pallas_call(
        pack_kernel,
        out_shape=jax.ShapeDtypeStruct((3 * SHARE, WIDTH), BF),
        grid=(1,),
        in_specs=[
            pl.BlockSpec((None, WIDTH, 2 * SHARE), lambda i: (0, 0, 0)),
            pl.BlockSpec((None, SHARE, WIDTH), lambda i: (0, 0, 0)),
        ],
        out_specs=pl.BlockSpec((3 * SHARE, WIDTH), lambda i: (0, 0)),
        compiler_params=pltpu.CompilerParams(vmem_limit_bytes=VMEM_LIMIT),
        cost_estimate=pl.CostEstimate(flops=10**8, transcendentals=0, bytes_accessed=3500000),
        name="pack",
    )(w_gate_up, w_down)


def qkv_kernel(rank_ref, hidden_ref, gain_ref, freq_ref, w_ref, query_ref, kv_ref, normed, cos, sin):
    step = pl.program_id(0)

    @pl.when(step == 0)
    def _():
        normed[...] = norm_rows(hidden_ref[...], gain_ref[...])
        position = (sublanes((ROWS, 128)) * 4 + rank_ref[0]).astype(F32)
        cos[...], sin[...] = rope_tables(position, freq_ref[...])

    projected = jnp.dot(normed[...], w_ref[...], preferred_element_type=F32)
    chunks = [projected[:, i * 128 : (i + 1) * 128] for i in range(5)]

    @pl.when(step < 2)
    def _():
        for i in range(5):
            roped = rope(chunks[i], cos[...], sin[...]).astype(BF)
            query_ref[:, i * 128 : (i + 1) * 128] = roped * jnp.asarray(0.125, BF)

    @pl.when(step == 2)
    def _():
        low = lanes((ROWS, 128)) < HEAD
        first = rope(chunks[0], cos[...], sin[...])
        second = rope(chunks[1], cos[...], sin[...])
        third = jnp.where(low, rope(chunks[2], cos[...], sin[...]), chunks[2])
        swap = lambda value: pltpu.roll(value, 64, 1)
        out = [
            jnp.where(low, first, third),
            jnp.where(low, swap(first), swap(chunks[3])),
            jnp.where(low, second, chunks[3]),
            jnp.where(low, swap(second), swap(chunks[4])),
            jnp.where(low, third, chunks[4]),
        ]
        for i in range(5):
            kv_ref[:, i * 128 : (i + 1) * 128] = out[i].astype(BF)


def prefill_qkv(rank, hidden, gain, freq, w_qkv):
    return pl.pallas_call(
        qkv_kernel,
        out_shape=(
            jax.ShapeDtypeStruct((ROWS, QW), BF),
            jax.ShapeDtypeStruct((ROWS, KVW), BF),
        ),
        grid=(3,),
        in_specs=[
            pl.BlockSpec(memory_space=pltpu.SMEM),
            pl.BlockSpec((ROWS, WIDTH), lambda j: (0, 0)),
            pl.BlockSpec((1, WIDTH), lambda j: (0, 0)),
            pl.BlockSpec((1, 128), lambda j: (0, 0)),
            pl.BlockSpec((WIDTH, KVW), lambda j: (0, j)),
        ],
        out_specs=(
            pl.BlockSpec((ROWS, KVW), lambda j: (0, jnp.minimum(j, 1))),
            pl.BlockSpec((ROWS, KVW), lambda j: (0, 0)),
        ),
        scratch_shapes=[
            pltpu.VMEM((ROWS, WIDTH), BF),
            pltpu.VMEM((ROWS, 128), F32),
            pltpu.VMEM((ROWS, 128), F32),
        ],
        compiler_params=pltpu.CompilerParams(vmem_limit_bytes=VMEM_LIMIT),
        cost_estimate=pl.CostEstimate(flops=4 * 10**9, transcendentals=0, bytes_accessed=7000000),
        name="prefill_qkv",
    )(rank, hidden, gain, freq, w_qkv)


def column(row):
    return jnp.broadcast_to(row, (128, 128)).T


def held_kernel(index_ref, hidden_ref, gain_ref, freq_ref, w_ref, out_ref):
    step = pl.program_id(0)
    normed = norm_rows(hidden_ref[...], gain_ref[...])
    projected = jnp.dot(normed, w_ref[...], preferred_element_type=F32)
    position = (index_ref[pl.ds(step * 2, 2), :] % POSITIONS).astype(F32)
    position = jnp.concatenate([column(position[0:1]), column(position[1:2])], axis=0)
    cosine, sine = rope_tables(position, freq_ref[...])
    low = lanes((256, 128)) < HEAD
    for i in range(5):
        chunk = projected[:, i * 128 : (i + 1) * 128]
        if i < 2:
            chunk = rope(chunk, cosine, sine)
        elif i == 2:
            chunk = jnp.where(low, rope(chunk, cosine, sine), chunk)
        out_ref[:, i * 128 : (i + 1) * 128] = chunk.astype(BF)


def held_rows(index, hidden, gain, freq, w_qkv):
    rows = hidden.shape[0]
    return pl.pallas_call(
        held_kernel,
        out_shape=jax.ShapeDtypeStruct((rows, KVW), BF),
        grid=(rows // 256,),
        in_specs=[
            pl.BlockSpec((8, 128), lambda i: (0, 0)),
            pl.BlockSpec((256, WIDTH), lambda i: (i, 0)),
            pl.BlockSpec((1, WIDTH), lambda i: (0, 0)),
            pl.BlockSpec((1, 128), lambda i: (0, 0)),
            pl.BlockSpec((WIDTH, KVW), lambda i: (0, 2)),
        ],
        out_specs=pl.BlockSpec((256, KVW), lambda i: (i, 0)),
        compiler_params=pltpu.CompilerParams(vmem_limit_bytes=VMEM_LIMIT),
        cost_estimate=pl.CostEstimate(flops=6 * 10**9, transcendentals=0, bytes_accessed=7000000),
        name="held",
    )(index, hidden, gain, freq, w_qkv)


def decode_kernel(
    device_ref,
    length_ref,
    count_ref,
    slot_ref,
    index_ref,
    rows_ref,
    gain_ref,
    freq_ref,
    w_ref,
    cache_ref,
    held_ref,
    out_ref,
    spread,
    query,
    fresh_key,
    fresh_value,
    over,
    result,
):
    step = pl.program_id(0)
    first_slot = device_ref[0] * SLOTS
    index_rows = [index_ref[i : i + 1, :] for i in range(8)]

    @pl.when(step == 0)
    def _():
        spread[...] = (
            sublanes((QW, 384)) % HEAD == lanes((QW, 384)) % HEAD
        ).astype(F32).astype(BF)
        wanted = jnp.broadcast_to(slot_ref[...], (8, 256))
        slot = sublanes((8, 256))
        chosen = ((wanted == first_slot + slot) & (slot < SLOTS)).astype(F32).astype(BF)
        rows = jnp.dot(chosen, rows_ref[...], preferred_element_type=F32)
        normed = norm_rows(rows, gain_ref[...])
        projected = jnp.dot(normed, w_ref[...], preferred_element_type=F32)
        projected = projected.astype(BF).astype(F32)
        row = sublanes((8, 128))
        position = jnp.zeros((8, 128), F32)
        for j in range(SLOTS):
            position = jnp.where(row == j, length_ref[j].astype(F32), position)
        cosine, sine = rope_tables(position, freq_ref[...])
        chunks = [projected[:, i * 128 : (i + 1) * 128] for i in range(15)]
        roped = [rope(chunks[i], cosine, sine).astype(BF) for i in range(13)]
        whole = jnp.concatenate(roped[:10], axis=1).astype(F32) * 0.125
        head_of = sublanes((32, QW))
        keep = lanes((32, QW)) // HEAD == head_of
        group = sublanes((32, 384))
        block = (lanes((32, 384)) // HEAD == group // 4) & (group < QUERY_HEADS)
        for j in range(SLOTS):
            placed = jnp.where(keep, jnp.broadcast_to(whole[j : j + 1], (32, QW)), 0.0)
            turned = jnp.dot(placed.astype(BF), spread[...], preferred_element_type=F32)
            query[j * 32 : (j + 1) * 32, :] = jnp.where(block, turned, 0.0).astype(BF)
        fresh_key[...] = jnp.concatenate(roped[10:13], axis=1).astype(F32)
        fresh_value[...] = jnp.concatenate(chunks[12:15], axis=1)
        counts = jnp.zeros((32, 128), F32)
        for i in range(8):
            entry = i * 128 + lanes((32, 128))
            live = entry < count_ref[0]
            upper = jnp.broadcast_to(index_rows[i] // 128, (32, 128)) == sublanes((32, 128))
            upper = (upper & live).astype(F32).astype(BF)
            lower = jnp.broadcast_to(index_rows[i] % 128, (128, 128)) == sublanes((128, 128))
            lower = lower.astype(F32).astype(BF)
            counts = counts + lax.dot_general(upper, lower, NT, preferred_element_type=F32)
        over[...] = counts

    length = length_ref[step]
    queries = query[pl.ds(pl.multiple_of(step * 32, 32), 32), :]
    taken = over[pl.ds(pl.multiple_of(step * 8, 8), 8), :]
    taken = jnp.concatenate([taken[i : i + 1, :] for i in range(8)], axis=1)
    cache_live = (lanes((1, POSITIONS)) < length) & (taken < 0.5)
    index = jnp.concatenate(index_rows, axis=1)
    held_live = (
        (lanes((1, 1024)) < count_ref[0])
        & (index // POSITIONS == step)
        & (index % POSITIONS < length)
    )
    cache_score = lax.dot_general(queries, cache_ref[:, :384], NT, preferred_element_type=F32)
    held_score = lax.dot_general(queries, held_ref[:, :384], NT, preferred_element_type=F32)
    own_score = jnp.sum(
        queries.astype(F32) * fresh_key[pl.ds(step, 1), :], axis=-1, keepdims=True
    )
    cache_live = jnp.broadcast_to(cache_live, cache_score.shape)
    held_live = jnp.broadcast_to(held_live, held_score.shape)
    cache_score = jnp.where(cache_live, cache_score, NEG)
    held_score = jnp.where(held_live, held_score, NEG)
    top = jnp.maximum(
        jnp.maximum(
            jnp.max(cache_score, axis=-1, keepdims=True), jnp.max(held_score, axis=-1, keepdims=True)
        ),
        own_score,
    )
    cache_weight = jnp.where(cache_live, jnp.exp(cache_score - top), 0.0)
    held_weight = jnp.where(held_live, jnp.exp(held_score - top), 0.0)
    own_weight = jnp.exp(own_score - top)
    total = (
        jnp.sum(cache_weight, axis=-1, keepdims=True)
        + jnp.sum(held_weight, axis=-1, keepdims=True)
        + own_weight
    )
    mixed = jnp.dot(cache_weight.astype(BF), cache_ref[:, 256:], preferred_element_type=F32)
    mixed += jnp.dot(held_weight.astype(BF), held_ref[:, 256:], preferred_element_type=F32)
    mixed += own_weight.astype(BF).astype(F32) * fresh_value[pl.ds(step, 1), :]
    group = sublanes((32, 384))
    block = (lanes((32, 384)) // HEAD == group // 4 + 1) & (group < QUERY_HEADS)
    mixed = jnp.where(block, mixed / total, 0.0).astype(BF)
    turned = lax.dot_general(mixed, spread[...], NT, preferred_element_type=F32)
    keep = lanes((32, QW)) // HEAD == sublanes((32, QW))
    result[pl.ds(step, 1), :] = jnp.sum(jnp.where(keep, turned, 0.0), axis=0, keepdims=True)

    @pl.when(step == SLOTS - 1)
    def _():
        wanted = jnp.broadcast_to(slot_ref[...], (8, 256))
        slot = sublanes((8, 256))
        chosen = ((wanted == first_slot + slot) & (slot < SLOTS)).astype(F32).astype(BF)
        good = jnp.where(sublanes((8, QW)) < SLOTS, result[...], 0.0).astype(BF)
        out_ref[...] = lax.dot_general(
            chosen, good, (((0,), (0,)), ((), ())), preferred_element_type=F32
        ).astype(BF)


def decode_attention(
    device, length, count, slots, index, rows, gain, freq, w_qkv, cache, held
):
    smem = pl.BlockSpec(memory_space=pltpu.SMEM)
    full = lambda shape: pl.BlockSpec(shape, lambda j: (0,) * len(shape))
    return pl.pallas_call(
        decode_kernel,
        out_shape=jax.ShapeDtypeStruct((256, QW), BF),
        grid=(SLOTS,),
        in_specs=[
            smem,
            smem,
            smem,
            full((1, 256)),
            full((8, 128)),
            full((256, WIDTH)),
            full((1, WIDTH)),
            full((1, 128)),
            full((WIDTH, QW + KVW)),
            pl.BlockSpec((None, POSITIONS, KVW), lambda j: (j, 0, 0)),
            full((1024, KVW)),
        ],
        out_specs=full((256, QW)),
        scratch_shapes=[
            pltpu.VMEM((QW, 384), BF),
            pltpu.VMEM((128, 384), BF),
            pltpu.VMEM((8, 384), F32),
            pltpu.VMEM((8, 384), F32),
            pltpu.VMEM((32, 128), F32),
            pltpu.VMEM((8, QW), F32),
        ],
        compiler_params=pltpu.CompilerParams(vmem_limit_bytes=VMEM_LIMIT),
        cost_estimate=pl.CostEstimate(flops=8 * 10**9, transcendentals=0, bytes_accessed=13000000),
        name="decode",
    )(device, length, count, slots, index, rows, gain, freq, w_qkv, cache, held)


def attention_kernel(
    rank_ref,
    query_ref,
    own_ref,
    core_ref,
    zed_ref,
    far_ref,
    w_ref,
    hidden_ref,
    decode_ref,
    back_ref,
    gain_ref,
    resid_ref,
    normed_ref,
    lower_ref,
    upper_ref,
    total,
    decode_mixed,
    mask,
):
    group = pl.program_id(0)

    @pl.when(group == 0)
    def _():
        total[...] = jnp.zeros_like(total)
        source = lanes((32, 256)) % 2
        row = sublanes((32, 256))
        pick = ((row == 0) & (source == 0)) | ((row == 16) & (source == 1))
        pick = pick.astype(F32).astype(BF)
        decode_mixed[...] = jnp.dot(
            pick, back_ref[...], preferred_element_type=F32
        ).astype(BF)
        rank = rank_ref[0]
        row = sublanes((128, 128))
        col = lanes((128, 128))
        for piece in range(4):
            other = rank ^ piece
            bound = jnp.where(other <= rank, 0, 1)
            mask[:, piece * 128 : (piece + 1) * 128] = jnp.where(col + bound <= row, 0.0, NEG)

    pieces = [own_ref, core_ref, zed_ref, far_ref]
    keys = jnp.concatenate(
        [ref[h * 128 : (h + 1) * 128, :] for h in range(2) for ref in pieces], axis=0
    )
    low = lanes((1024, 128)) < HEAD
    wide = keys.astype(F32)
    values = jnp.where(low, pltpu.roll(wide, 64, 1), wide).astype(BF)
    values = jnp.concatenate([values, jnp.ones((1024, 128), BF)], axis=1)
    low = lanes((128, 128)) < HEAD
    blocked = mask[...]
    mixed = []
    for tile in range(2):
        heads = []
        for pair in range(2):
            two = query_ref[tile * 128 : (tile + 1) * 128, pair * 128 : (pair + 1) * 128].astype(F32)
            heads.append(jnp.where(low, two, 0.0).astype(BF))
            heads.append(jnp.where(low, pltpu.roll(two, 64, 1), 0.0).astype(BF))
        out = []
        for head in heads:
            count = 512 * (tile + 1)
            score = lax.dot_general(head, keys[:count], NT, preferred_element_type=F32)
            if tile == 0:
                score = score + blocked
            else:
                score = jnp.concatenate([score[:, :512], score[:, 512:] + blocked], axis=1)
            top = jnp.max(score, axis=-1, keepdims=True)
            weight = jnp.exp(score - top).astype(BF)
            both = jnp.dot(weight, values[:count], preferred_element_type=F32)
            out.append(both[:, :128] / both[:, 128:])
        mixed.append(
            jnp.concatenate(
                [jnp.where(low, out[0], out[1]), jnp.where(low, out[2], out[3])], axis=1
            ).astype(BF)
        )
    extra = decode_mixed[:, pl.ds(pl.multiple_of(group * 256, 256), 256)]
    rows = jnp.concatenate([mixed[0], extra[:16], mixed[1], extra[16:]], axis=0)
    total[...] += jnp.dot(rows, w_ref[...], preferred_element_type=F32)

    @pl.when(group == 4)
    def _():
        first = sublanes((16, WIDTH)) == 0
        single = decode_ref[...].astype(F32)
        for part in range(2):
            alone = jnp.where(first, jnp.broadcast_to(single[part : part + 1], (16, WIDTH)), 0.0)
            hidden = jnp.concatenate(
                [hidden_ref[part * 128 : (part + 1) * 128, :].astype(F32), alone], axis=0
            )
            resid = (hidden + total[part * HALF : (part + 1) * HALF, :]).astype(BF)
            normed = norm_rows(resid, gain_ref[...])
            resid_ref[part * HALF : (part + 1) * HALF, :] = resid
            normed_ref[part * HALF : (part + 1) * HALF, :] = normed
            (lower_ref, upper_ref)[part][...] = normed


def attention(rank, query, own, core, zed, far, w_out, hidden, decode, back, gain):
    full = lambda shape: pl.BlockSpec(shape, lambda g: (0,) * len(shape))
    side = pl.BlockSpec((ROWS, 128), lambda g: (0, g))
    return pl.pallas_call(
        attention_kernel,
        out_shape=(
            jax.ShapeDtypeStruct((2 * HALF, WIDTH), BF),
            jax.ShapeDtypeStruct((2 * HALF, WIDTH), BF),
            jax.ShapeDtypeStruct((HALF, WIDTH), BF),
            jax.ShapeDtypeStruct((HALF, WIDTH), BF),
        ),
        grid=(5,),
        in_specs=[
            pl.BlockSpec(memory_space=pltpu.SMEM),
            pl.BlockSpec((ROWS, 256), lambda g: (0, g)),
            side,
            side,
            side,
            side,
            pl.BlockSpec((256, WIDTH), lambda g: (g, 0)),
            full((ROWS, WIDTH)),
            full((2, WIDTH)),
            full((256, WIDTH)),
            full((1, WIDTH)),
        ],
        out_specs=(
            full((2 * HALF, WIDTH)),
            full((2 * HALF, WIDTH)),
            full((HALF, WIDTH)),
            full((HALF, WIDTH)),
        ),
        scratch_shapes=[
            pltpu.VMEM((2 * HALF, WIDTH), F32),
            pltpu.VMEM((32, WIDTH), BF),
            pltpu.VMEM((128, 512), F32),
        ],
        compiler_params=pltpu.CompilerParams(vmem_limit_bytes=VMEM_LIMIT),
        cost_estimate=pl.CostEstimate(flops=12 * 10**9, transcendentals=0, bytes_accessed=8000000),
        name="attention",
    )(rank, query, own, core, zed, far, w_out, hidden, decode, back, gain)


def feed_kernel(mine_ref, other_ref, w_ref, mine_out, other_out, total):
    step = pl.program_id(0)
    rows = jnp.concatenate([mine_ref[...], other_ref[...]], axis=0)
    gate = lax.dot_general(rows, w_ref[:SHARE, :], NT, preferred_element_type=F32)
    up = lax.dot_general(rows, w_ref[SHARE : 2 * SHARE, :], NT, preferred_element_type=F32)
    act = (gate / (1.0 + jnp.exp(-gate)) * up).astype(BF)
    down = jnp.dot(act, w_ref[2 * SHARE :, :], preferred_element_type=F32)

    @pl.when(step == 0)
    def _():
        total[...] = down

    @pl.when((step > 0) & (step < SIDE - 1))
    def _():
        total[...] += down

    @pl.when(step == SIDE - 1)
    def _():
        done = total[...] + down
        mine_out[...] = done[: 2 * HALF]
        other_out[...] = done[2 * HALF :].astype(BF)


def feed_forward(mine, other, weights, name):
    full = pl.BlockSpec((2 * HALF, WIDTH), lambda i: (0, 0))
    return pl.pallas_call(
        feed_kernel,
        out_shape=(
            jax.ShapeDtypeStruct((2 * HALF, WIDTH), F32),
            jax.ShapeDtypeStruct((2 * HALF, WIDTH), BF),
        ),
        grid=(SIDE,),
        in_specs=[
            full,
            full,
            pl.BlockSpec((None, 3 * SHARE, WIDTH), lambda i: (i, 0, 0)),
        ],
        out_specs=(full, full),
        scratch_shapes=[pltpu.VMEM((4 * HALF, WIDTH), F32)],
        compiler_params=pltpu.CompilerParams(vmem_limit_bytes=VMEM_LIMIT),
        cost_estimate=pl.CostEstimate(flops=6 * 10**9, transcendentals=0, bytes_accessed=11000000),
        name=name,
    )(mine, other, weights)


def add_kernel(mine_ref, other_ref, first_ref, second_ref):
    whole = mine_ref[...] + other_ref[...].astype(F32)
    first_ref[...] = whole[:HALF].astype(BF)
    second_ref[...] = whole[HALF:].astype(BF)


def add_halves(mine, other):
    half = jax.ShapeDtypeStruct((HALF, WIDTH), BF)
    return pl.pallas_call(
        add_kernel,
        out_shape=(half, half),
        compiler_params=pltpu.CompilerParams(vmem_limit_bytes=VMEM_LIMIT),
        cost_estimate=pl.CostEstimate(flops=10**6, transcendentals=0, bytes_accessed=3000000),
        name="add",
    )(mine, other)


def final_kernel(resid_ref, mine_ref, other_ref, first_ref, second_ref, prefill_ref, decode_ref):
    decode = []
    for part, ref in ((0, first_ref), (1, second_ref)):
        cut = slice(part * HALF, (part + 1) * HALF)
        whole = resid_ref[cut, :].astype(F32) + (
            mine_ref[cut, :] + other_ref[cut, :].astype(F32) + ref[...].astype(F32)
        )
        prefill_ref[part * 128 : (part + 1) * 128, :] = whole[:128].astype(BF)
        decode.append(whole[128:129])
    decode_ref[...] = jnp.concatenate(decode, axis=0).astype(BF)


def final_sum(resid, mine, other, first, second):
    return pl.pallas_call(
        final_kernel,
        out_shape=(
            jax.ShapeDtypeStruct((ROWS, WIDTH), BF),
            jax.ShapeDtypeStruct((2, WIDTH), BF),
        ),
        compiler_params=pltpu.CompilerParams(vmem_limit_bytes=VMEM_LIMIT),
        cost_estimate=pl.CostEstimate(flops=10**6, transcendentals=0, bytes_accessed=5000000),
        name="final",
    )(resid, mine, other, first, second)


def body(
    prefill_hidden,
    decode_hidden,
    attn_gain,
    w_qkv,
    w_out,
    ffn_gain,
    w_gate_up,
    w_down,
    key_value_cache,
    cache_len,
    slot_of_request,
    held_hidden,
    recomputed_index,
    recomp_count,
):
    device = lax.axis_index("req").astype(jnp.int32).reshape(1)
    rank = device % 4
    gain = attn_gain.reshape(1, WIDTH)
    gain2 = ffn_gain.reshape(1, WIDTH)
    half = HEAD // 2
    frequency = THETA ** (-(jnp.arange(half).astype(F32) * 2.0 / HEAD))
    freq = jnp.tile(frequency, 4).reshape(1, 128)
    index = recomputed_index.reshape(8, 128)

    packed = pack_weights(w_gate_up, w_down)
    columns = [
        [place(y, x, z, core) for z in range(SIDE)]
        for y in range(SIDE)
        for x in range(SIDE)
        for core in range(2)
    ]
    weights = lax.all_gather(packed, "req", axis_index_groups=columns)

    total = 2 * SIDE**3
    spread = jnp.broadcast_to(decode_hidden[None], (total, 2, WIDTH))
    every_row = lax.all_to_all(spread, "req", 0, 0).reshape(256, WIDTH)

    query, kv = prefill_qkv(rank, prefill_hidden, gain, freq, w_qkv)
    zed = send(kv, pair_z)
    core = send(kv, other_core)
    held = held_rows(index, held_hidden, gain, freq, w_qkv)
    far = send(zed, other_core)

    outgoing = decode_attention(
        device,
        cache_len,
        recomp_count,
        slot_of_request.reshape(1, 256),
        index,
        every_row,
        gain,
        freq,
        w_qkv,
        key_value_cache,
        held,
    )
    back = lax.all_to_all(outgoing.reshape(total, 2, WIDTH), "req", 0, 0).reshape(256, WIDTH)

    resid, normed, lower, upper = attention(
        rank, query, kv, core, zed, far, w_out, prefill_hidden, decode_hidden, back, gain2
    )
    from_last = send(lower, next_x)
    from_next = send(upper, last_x)
    across = send(normed, other_core)
    mine, given = feed_forward(normed, across, weights, "feed_own")
    given = send(given, other_core)
    guests = jnp.concatenate([from_last, from_next], axis=0)
    guests_across = send(guests, other_core)
    guest_mine, guest_given = feed_forward(guests, guests_across, weights, "feed_guest")
    guest_given = send(guest_given, other_core)
    to_last, to_next = add_halves(guest_mine, guest_given)
    first = send(to_last, last_x)
    second = send(to_next, next_x)
    return final_sum(resid, mine, given, first, second)


def solution(mesh):
    return jax.shard_map(
        body,
        mesh=mesh,
        in_specs=(
            P("req", None),
            P("req", None),
            P(),
            P(),
            P(),
            P(),
            P("req", None, None),
            P("req", None, None),
            P("req", None, None),
            P("req"),
            P(),
            P("req", None),
            P("req"),
            P("req"),
        ),
        out_specs=(P("req", None), P("req", None)),
        check_vma=False,
    )
```

```python
import functools

import jax
import jax.numpy as jnp
import numpy as np
from jax import lax
from jax.experimental import pallas as pl
from jax.experimental.pallas import tpu as pltpu
from jax.sharding import PartitionSpec as P

WIDTH = 1280
QUERY_HEADS = 20
HEAD = 64
QW = 1280
KVW = 640
SHARE = 224
GROUP = 16
SIDE = 4
SLOTS = 4
POSITIONS = 1024
ROWS = 256
HALF = 144
EPS = 1e-05
THETA = 10000.0
NEG = -1e30
F32 = jnp.float32
BF = jnp.bfloat16
NT = (((1,), (1,)), ((), ()))
VMEM_LIMIT = 56 << 20


def place(y, x, z, core):
    return (((y % SIDE) * SIDE + x % SIDE) * SIDE + z % SIDE) * 2 + core


def moves(step):
    pairs = []
    for y in range(SIDE):
        for x in range(SIDE):
            for z in range(SIDE):
                for core in range(2):
                    pairs.append((place(y, x, z, core), place(*step(y, x, z, core))))
    return pairs


def send(array, step):
    return lax.ppermute(array, "req", moves(step))


def other_core(y, x, z, core):
    return y, x, z, 1 - core


def next_x(y, x, z, core):
    return y, x + 1, z, core


def last_x(y, x, z, core):
    return y, x - 1, z, core


def next_z(y, x, z, core):
    return y, x, z + 1, core


def last_z(y, x, z, core):
    return y, x, z - 1, core


def pair_z(y, x, z, core):
    return y, x, z ^ 1, core


def norm_rows(rows, gain):
    rows = rows.astype(F32)
    mean = jnp.mean(rows * rows, axis=-1, keepdims=True)
    return (rows * lax.rsqrt(mean + EPS) * gain).astype(BF)


def lanes(shape):
    return lax.broadcasted_iota(jnp.int32, shape, len(shape) - 1)


def sublanes(shape):
    return lax.broadcasted_iota(jnp.int32, shape, len(shape) - 2)


def rope_tables(position, frequency):
    angle = position * frequency
    sine = jnp.sin(angle)
    low = lanes(angle.shape) % HEAD < HEAD // 2
    return jnp.cos(angle), jnp.where(low, -sine, sine)


def rope(chunk, cosine, sine):
    low = lanes(chunk.shape) % HEAD < HEAD // 2
    other = jnp.where(low, pltpu.roll(chunk, 96, 1), pltpu.roll(chunk, 32, 1))
    return chunk * cosine + other * sine


def qkv_kernel(rank_ref, hidden_ref, gain_ref, freq_ref, w_ref, query_ref, kv_ref, normed, cos, sin):
    step = pl.program_id(0)

    @pl.when(step == 0)
    def _():
        normed[...] = norm_rows(hidden_ref[...], gain_ref[...])
        position = (sublanes((ROWS, 128)) * 4 + rank_ref[0]).astype(F32)
        cos[...], sin[...] = rope_tables(position, freq_ref[...])

    projected = jnp.dot(normed[...], w_ref[...], preferred_element_type=F32)
    chunks = [projected[:, i * 128 : (i + 1) * 128] for i in range(5)]

    @pl.when(step < 2)
    def _():
        for i in range(5):
            roped = rope(chunks[i], cos[...], sin[...]).astype(BF)
            query_ref[:, i * 128 : (i + 1) * 128] = roped * jnp.asarray(0.125, BF)

    @pl.when(step == 2)
    def _():
        low = lanes((ROWS, 128)) < HEAD
        first = rope(chunks[0], cos[...], sin[...])
        second = rope(chunks[1], cos[...], sin[...])
        third = jnp.where(low, rope(chunks[2], cos[...], sin[...]), chunks[2])
        swap = lambda value: pltpu.roll(value, 64, 1)
        out = [
            jnp.where(low, first, third),
            jnp.where(low, swap(first), swap(chunks[3])),
            jnp.where(low, second, chunks[3]),
            jnp.where(low, swap(second), swap(chunks[4])),
            jnp.where(low, third, chunks[4]),
        ]
        for i in range(5):
            kv_ref[:, i * 128 : (i + 1) * 128] = out[i].astype(BF)


def prefill_qkv(rank, hidden, gain, freq, w_qkv):
    return pl.pallas_call(
        qkv_kernel,
        out_shape=(
            jax.ShapeDtypeStruct((ROWS, QW), BF),
            jax.ShapeDtypeStruct((ROWS, KVW), BF),
        ),
        grid=(3,),
        in_specs=[
            pl.BlockSpec(memory_space=pltpu.SMEM),
            pl.BlockSpec((ROWS, WIDTH), lambda j: (0, 0)),
            pl.BlockSpec((1, WIDTH), lambda j: (0, 0)),
            pl.BlockSpec((1, 128), lambda j: (0, 0)),
            pl.BlockSpec((WIDTH, KVW), lambda j: (0, j)),
        ],
        out_specs=(
            pl.BlockSpec((ROWS, KVW), lambda j: (0, jnp.minimum(j, 1))),
            pl.BlockSpec((ROWS, KVW), lambda j: (0, 0)),
        ),
        scratch_shapes=[
            pltpu.VMEM((ROWS, WIDTH), BF),
            pltpu.VMEM((ROWS, 128), F32),
            pltpu.VMEM((ROWS, 128), F32),
        ],
        compiler_params=pltpu.CompilerParams(vmem_limit_bytes=VMEM_LIMIT),
        cost_estimate=pl.CostEstimate(flops=4 * 10**9, transcendentals=0, bytes_accessed=7000000),
        name="prefill_qkv",
    )(rank, hidden, gain, freq, w_qkv)


def column(row):
    return jnp.broadcast_to(row, (128, 128)).T


def decode_kernel(
    device_ref,
    length_ref,
    count_ref,
    slot_ref,
    index_ref,
    rows_ref,
    gain_ref,
    freq_ref,
    w_ref,
    cache_ref,
    hidden_ref,
    out_ref,
    held_ref,
    spread,
    query,
    fresh_key,
    fresh_value,
    over,
    result,
):
    tick = pl.program_id(0)
    step = tick - SLOTS
    first_slot = device_ref[0] * SLOTS

    @pl.when(tick < SLOTS)
    def _():
        normed = norm_rows(hidden_ref[...], gain_ref[...])
        projected = jnp.dot(normed, w_ref[:, QW:], preferred_element_type=F32)
        position = (index_ref[pl.ds(tick * 2, 2), :] % POSITIONS).astype(F32)
        position = jnp.concatenate([column(position[0:1]), column(position[1:2])], axis=0)
        cosine, sine = rope_tables(position, freq_ref[...])
        low = lanes((256, 128)) < HEAD
        rows = pl.ds(pl.multiple_of(tick * 256, 256), 256)
        for i in range(5):
            chunk = projected[:, i * 128 : (i + 1) * 128]
            if i < 2:
                chunk = rope(chunk, cosine, sine)
            elif i == 2:
                chunk = jnp.where(low, rope(chunk, cosine, sine), chunk)
            held_ref[rows, i * 128 : (i + 1) * 128] = chunk.astype(BF)

    index_rows = [index_ref[i : i + 1, :] for i in range(8)]

    @pl.when(step == 0)
    def _():
        spread[...] = (
            sublanes((QW, 384)) % HEAD == lanes((QW, 384)) % HEAD
        ).astype(F32).astype(BF)
        wanted = jnp.broadcast_to(slot_ref[...], (8, 256))
        slot = sublanes((8, 256))
        chosen = ((wanted == first_slot + slot) & (slot < SLOTS)).astype(F32).astype(BF)
        rows = jnp.dot(chosen, rows_ref[...], preferred_element_type=F32)
        normed = norm_rows(rows, gain_ref[...])
        projected = jnp.dot(normed, w_ref[...], preferred_element_type=F32)
        projected = projected.astype(BF).astype(F32)
        row = sublanes((8, 128))
        position = jnp.zeros((8, 128), F32)
        for j in range(SLOTS):
            position = jnp.where(row == j, length_ref[j].astype(F32), position)
        cosine, sine = rope_tables(position, freq_ref[...])
        chunks = [projected[:, i * 128 : (i + 1) * 128] for i in range(15)]
        roped = [rope(chunks[i], cosine, sine).astype(BF) for i in range(13)]
        whole = jnp.concatenate(roped[:10], axis=1).astype(F32) * 0.125
        head_of = sublanes((32, QW))
        keep = lanes((32, QW)) // HEAD == head_of
        group = sublanes((32, 384))
        block = (lanes((32, 384)) // HEAD == group // 4) & (group < QUERY_HEADS)
        for j in range(SLOTS):
            placed = jnp.where(keep, jnp.broadcast_to(whole[j : j + 1], (32, QW)), 0.0)
            turned = jnp.dot(placed.astype(BF), spread[...], preferred_element_type=F32)
            query[j * 32 : (j + 1) * 32, :] = jnp.where(block, turned, 0.0).astype(BF)
        fresh_key[...] = jnp.concatenate(roped[10:13], axis=1).astype(F32)
        fresh_value[...] = jnp.concatenate(chunks[12:15], axis=1)
        counts = jnp.zeros((32, 128), F32)
        for i in range(8):
            entry = i * 128 + lanes((32, 128))
            live = entry < count_ref[0]
            upper = jnp.broadcast_to(index_rows[i] // 128, (32, 128)) == sublanes((32, 128))
            upper = (upper & live).astype(F32).astype(BF)
            lower = jnp.broadcast_to(index_rows[i] % 128, (128, 128)) == sublanes((128, 128))
            lower = lower.astype(F32).astype(BF)
            counts = counts + lax.dot_general(upper, lower, NT, preferred_element_type=F32)
        over[...] = counts

    @pl.when(step >= 0)
    def _():
        length = length_ref[step]
        queries = query[pl.ds(pl.multiple_of(step * 32, 32), 32), :]
        taken = over[pl.ds(pl.multiple_of(step * 8, 8), 8), :]
        taken = jnp.concatenate([taken[i : i + 1, :] for i in range(8)], axis=1)
        cache_live = (lanes((1, POSITIONS)) < length) & (taken < 0.5)
        index = jnp.concatenate(index_rows, axis=1)
        held_live = (
            (lanes((1, 1024)) < count_ref[0])
            & (index // POSITIONS == step)
            & (index % POSITIONS < length)
        )
        cache_score = lax.dot_general(queries, cache_ref[:, :384], NT, preferred_element_type=F32)
        held_score = lax.dot_general(queries, held_ref[:, :384], NT, preferred_element_type=F32)
        own_score = jnp.sum(
            queries.astype(F32) * fresh_key[pl.ds(step, 1), :], axis=-1, keepdims=True
        )
        cache_live = jnp.broadcast_to(cache_live, cache_score.shape)
        held_live = jnp.broadcast_to(held_live, held_score.shape)
        cache_score = jnp.where(cache_live, cache_score, NEG)
        held_score = jnp.where(held_live, held_score, NEG)
        top = jnp.maximum(
            jnp.maximum(
                jnp.max(cache_score, axis=-1, keepdims=True), jnp.max(held_score, axis=-1, keepdims=True)
            ),
            own_score,
        )
        cache_weight = jnp.where(cache_live, jnp.exp(cache_score - top), 0.0)
        held_weight = jnp.where(held_live, jnp.exp(held_score - top), 0.0)
        own_weight = jnp.exp(own_score - top)
        total = (
            jnp.sum(cache_weight, axis=-1, keepdims=True)
            + jnp.sum(held_weight, axis=-1, keepdims=True)
            + own_weight
        )
        mixed = jnp.dot(cache_weight.astype(BF), cache_ref[:, 256:], preferred_element_type=F32)
        mixed += jnp.dot(held_weight.astype(BF), held_ref[:, 256:], preferred_element_type=F32)
        mixed += own_weight.astype(BF).astype(F32) * fresh_value[pl.ds(step, 1), :]
        group = sublanes((32, 384))
        block = (lanes((32, 384)) // HEAD == group // 4 + 1) & (group < QUERY_HEADS)
        mixed = jnp.where(block, mixed / total, 0.0).astype(BF)
        turned = lax.dot_general(mixed, spread[...], NT, preferred_element_type=F32)
        keep = lanes((32, QW)) // HEAD == sublanes((32, QW))
        result[pl.ds(step, 1), :] = jnp.sum(jnp.where(keep, turned, 0.0), axis=0, keepdims=True)

    @pl.when(step == SLOTS - 1)
    def _():
        wanted = jnp.broadcast_to(slot_ref[...], (8, 256))
        slot = sublanes((8, 256))
        chosen = ((wanted == first_slot + slot) & (slot < SLOTS)).astype(F32).astype(BF)
        good = jnp.where(sublanes((8, QW)) < SLOTS, result[...], 0.0).astype(BF)
        out_ref[...] = lax.dot_general(
            chosen, good, (((0,), (0,)), ((), ())), preferred_element_type=F32
        ).astype(BF)


def decode_attention(
    device, length, count, slots, index, rows, gain, freq, w_qkv, cache, hidden
):
    smem = pl.BlockSpec(memory_space=pltpu.SMEM)
    full = lambda shape: pl.BlockSpec(shape, lambda j: (0,) * len(shape))
    return pl.pallas_call(
        decode_kernel,
        out_shape=jax.ShapeDtypeStruct((256, QW), BF),
        grid=(2 * SLOTS,),
        in_specs=[
            smem,
            smem,
            smem,
            full((1, 256)),
            full((8, 128)),
            full((256, WIDTH)),
            full((1, WIDTH)),
            full((1, 128)),
            full((WIDTH, QW + KVW)),
            pl.BlockSpec((None, POSITIONS, KVW), lambda j: (jnp.maximum(j - SLOTS, 0), 0, 0)),
            pl.BlockSpec((256, WIDTH), lambda j: (jnp.minimum(j, SLOTS - 1), 0)),
        ],
        out_specs=full((256, QW)),
        scratch_shapes=[
            pltpu.VMEM((1024, KVW), BF),
            pltpu.VMEM((QW, 384), BF),
            pltpu.VMEM((128, 384), BF),
            pltpu.VMEM((8, 384), F32),
            pltpu.VMEM((8, 384), F32),
            pltpu.VMEM((32, 128), F32),
            pltpu.VMEM((8, QW), F32),
        ],
        compiler_params=pltpu.CompilerParams(vmem_limit_bytes=VMEM_LIMIT),
        cost_estimate=pl.CostEstimate(flops=12 * 10**9, transcendentals=0, bytes_accessed=15000000),
        name="decode",
    )(device, length, count, slots, index, rows, gain, freq, w_qkv, cache, hidden)


def attention_kernel(
    rank_ref,
    query_ref,
    own_ref,
    core_ref,
    zed_ref,
    far_ref,
    w_ref,
    hidden_ref,
    gain_ref,
    resid_ref,
    lower_ref,
    upper_ref,
    total,
    mask,
):
    group = pl.program_id(0)

    @pl.when(group == 0)
    def _():
        total[...] = jnp.zeros_like(total)
        rank = rank_ref[0]
        row = sublanes((128, 128))
        col = lanes((128, 128))
        for piece in range(4):
            other = rank ^ piece
            bound = jnp.where(other <= rank, 0, 1)
            mask[:, piece * 128 : (piece + 1) * 128] = jnp.where(col + bound <= row, 0.0, NEG)

    pieces = [own_ref, core_ref, zed_ref, far_ref]
    keys = jnp.concatenate(
        [ref[h * 128 : (h + 1) * 128, :] for h in range(2) for ref in pieces], axis=0
    )
    low = lanes((1024, 128)) < HEAD
    wide = keys.astype(F32)
    values = jnp.where(low, pltpu.roll(wide, 64, 1), wide).astype(BF)
    values = jnp.concatenate([values, jnp.ones((1024, 128), BF)], axis=1)
    low = lanes((128, 128)) < HEAD
    blocked = mask[...]
    mixed = []
    for tile in range(2):
        heads = []
        for pair in range(2):
            two = query_ref[tile * 128 : (tile + 1) * 128, pair * 128 : (pair + 1) * 128].astype(F32)
            heads.append(jnp.where(low, two, 0.0).astype(BF))
            heads.append(jnp.where(low, pltpu.roll(two, 64, 1), 0.0).astype(BF))
        out = []
        for head in heads:
            count = 512 * (tile + 1)
            score = lax.dot_general(head, keys[:count], NT, preferred_element_type=F32)
            if tile == 0:
                score = score + blocked
            else:
                score = jnp.concatenate([score[:, :512], score[:, 512:] + blocked], axis=1)
            top = jnp.max(score, axis=-1, keepdims=True)
            weight = jnp.exp(score - top).astype(BF)
            both = jnp.dot(weight, values[:count], preferred_element_type=F32)
            out.append(both[:, :128] / both[:, 128:])
        mixed.append(
            jnp.concatenate(
                [jnp.where(low, out[0], out[1]), jnp.where(low, out[2], out[3])], axis=1
            ).astype(BF)
        )
    rows = jnp.concatenate(mixed, axis=0)
    total[...] += jnp.dot(rows, w_ref[...], preferred_element_type=F32)

    @pl.when(group == 4)
    def _():
        for part in range(2):
            cut = slice(part * 128, (part + 1) * 128)
            resid = (hidden_ref[cut, :].astype(F32) + total[cut, :]).astype(BF)
            resid_ref[cut, :] = resid
            (lower_ref, upper_ref)[part][:128, :] = norm_rows(resid, gain_ref[...])


def attention(rank, query, own, core, zed, far, w_out, hidden, gain):
    full = lambda shape: pl.BlockSpec(shape, lambda g: (0,) * len(shape))
    side = pl.BlockSpec((ROWS, 128), lambda g: (0, g))
    return pl.pallas_call(
        attention_kernel,
        out_shape=(
            jax.ShapeDtypeStruct((ROWS, WIDTH), BF),
            jax.ShapeDtypeStruct((HALF, WIDTH), BF),
            jax.ShapeDtypeStruct((HALF, WIDTH), BF),
        ),
        grid=(5,),
        in_specs=[
            pl.BlockSpec(memory_space=pltpu.SMEM),
            pl.BlockSpec((ROWS, 256), lambda g: (0, g)),
            side,
            side,
            side,
            side,
            pl.BlockSpec((256, WIDTH), lambda g: (g, 0)),
            full((ROWS, WIDTH)),
            full((1, WIDTH)),
        ],
        out_specs=(
            full((ROWS, WIDTH)),
            full((HALF, WIDTH)),
            full((HALF, WIDTH)),
        ),
        scratch_shapes=[
            pltpu.VMEM((ROWS, WIDTH), F32),
            pltpu.VMEM((128, 512), F32),
        ],
        compiler_params=pltpu.CompilerParams(vmem_limit_bytes=VMEM_LIMIT),
        cost_estimate=pl.CostEstimate(flops=12 * 10**9, transcendentals=0, bytes_accessed=8000000),
        name="attention",
    )(rank, query, own, core, zed, far, w_out, hidden, gain)


def decode_rows_kernel(back_ref, w_ref, decode_ref, gain_ref, lower_in, upper_in, resid_ref, lower_ref, upper_ref):
    del lower_in, upper_in
    source = lanes((32, 256)) % 2
    row = sublanes((32, 256))
    pick = ((row == 0) & (source == 0)) | ((row == 16) & (source == 1))
    pick = pick.astype(F32).astype(BF)
    mixed = jnp.dot(pick, back_ref[...], preferred_element_type=F32).astype(BF)
    projection = jnp.dot(mixed, w_ref[...], preferred_element_type=F32)
    first = sublanes((16, WIDTH)) == 0
    single = decode_ref[...].astype(F32)
    for part in range(2):
        cut = slice(part * 16, (part + 1) * 16)
        alone = jnp.where(first, jnp.broadcast_to(single[part : part + 1], (16, WIDTH)), 0.0)
        resid = (alone + projection[cut]).astype(BF)
        resid_ref[cut, :] = resid
        (lower_ref, upper_ref)[part][...] = norm_rows(resid, gain_ref[...])


def decode_rows(back, w_out, decode, gain, lower, upper):
    full = lambda shape: pl.BlockSpec(shape, lambda g: (0,) * len(shape))
    tail = pl.BlockSpec((16, WIDTH), lambda g: (8, 0))
    return pl.pallas_call(
        decode_rows_kernel,
        out_shape=(
            jax.ShapeDtypeStruct((32, WIDTH), BF),
            jax.ShapeDtypeStruct((HALF, WIDTH), BF),
            jax.ShapeDtypeStruct((HALF, WIDTH), BF),
        ),
        grid=(1,),
        in_specs=[
            full((256, WIDTH)),
            full((WIDTH, WIDTH)),
            full((2, WIDTH)),
            full((1, WIDTH)),
            tail,
            tail,
        ],
        out_specs=(full((32, WIDTH)), tail, tail),
        input_output_aliases={4: 1, 5: 2},
        compiler_params=pltpu.CompilerParams(vmem_limit_bytes=VMEM_LIMIT),
        cost_estimate=pl.CostEstimate(flops=10**8, transcendentals=0, bytes_accessed=4000000),
        name="decode_rows",
    )(back, w_out, decode, gain, lower, upper)


def feed_kernel(*refs):
    pieces, gate_ups, downs = refs[:4], refs[4:8], refs[8:12]
    mine_out, other_out, rows, gate_up, down, act, row_sem, gate_sem, down_sem = refs[12:]
    row_copies = [
        pltpu.make_async_copy(pieces[i], rows.at[pl.ds(i * HALF, HALF)], row_sem.at[i])
        for i in range(4)
    ]
    gate_copies = [
        pltpu.make_async_copy(gate_ups[k].at[0], gate_up.at[k], gate_sem.at[k]) for k in range(4)
    ]
    down_copies = [
        pltpu.make_async_copy(downs[k].at[0], down.at[pl.ds(k * SHARE, SHARE)], down_sem.at[k])
        for k in range(4)
    ]
    for copy in row_copies + gate_copies + down_copies:
        copy.start()
    for copy in row_copies:
        copy.wait()
    for k in range(4):
        gate_copies[k].wait()
        gate = lax.dot_general(
            rows[...], gate_up[k, :SHARE, :], NT, preferred_element_type=F32
        )
        up = lax.dot_general(rows[...], gate_up[k, SHARE:, :], NT, preferred_element_type=F32)
        act[:, k * SHARE : (k + 1) * SHARE] = (gate / (1.0 + jnp.exp(-gate)) * up).astype(BF)
    for copy in down_copies:
        copy.wait()
    mine_out[...] = jnp.dot(
        act[: 2 * HALF], down[...], preferred_element_type=F32
    ).astype(BF)
    other_out[...] = jnp.dot(
        act[2 * HALF :], down[...], preferred_element_type=F32
    ).astype(BF)


def feed_forward(pieces, gate_ups, downs, name):
    whole = jax.ShapeDtypeStruct((2 * HALF, WIDTH), BF)
    return pl.pallas_call(
        feed_kernel,
        out_shape=(whole, whole),
        in_specs=[pl.BlockSpec(memory_space=pl.ANY)] * 12,
        scratch_shapes=[
            pltpu.VMEM((4 * HALF, WIDTH), BF),
            pltpu.VMEM((4, 2 * SHARE, WIDTH), BF),
            pltpu.VMEM((4 * SHARE, WIDTH), BF),
            pltpu.VMEM((4 * HALF, 4 * SHARE), BF),
            pltpu.SemaphoreType.DMA((4,)),
            pltpu.SemaphoreType.DMA((4,)),
            pltpu.SemaphoreType.DMA((4,)),
        ],
        compiler_params=pltpu.CompilerParams(vmem_limit_bytes=VMEM_LIMIT),
        cost_estimate=pl.CostEstimate(flops=6 * 10**9, transcendentals=0, bytes_accessed=11000000),
        name=name,
    )(*pieces, *gate_ups, *downs)


def add_kernel(mine_ref, other_ref, out_ref):
    out_ref[...] = (mine_ref[...].astype(F32) + other_ref[...].astype(F32)).astype(BF)


def add_half(mine, other, part):
    block = pl.BlockSpec((HALF, WIDTH), lambda i: (part, 0))
    return pl.pallas_call(
        add_kernel,
        out_shape=jax.ShapeDtypeStruct((HALF, WIDTH), BF),
        grid=(1,),
        in_specs=[block, block],
        out_specs=pl.BlockSpec((HALF, WIDTH), lambda i: (0, 0)),
        compiler_params=pltpu.CompilerParams(vmem_limit_bytes=VMEM_LIMIT),
        cost_estimate=pl.CostEstimate(flops=10**6, transcendentals=0, bytes_accessed=1000000),
        name=("add_first", "add_second")[part],
    )(mine, other)


def start_kernel(resid_ref, extra_ref, mine_ref, other_ref, out_ref):
    for part in range(2):
        cut = slice(part * HALF, part * HALF + 128)
        out_ref[cut, :] = resid_ref[part * 128 : (part + 1) * 128, :].astype(F32) + (
            mine_ref[cut, :].astype(F32) + other_ref[cut, :].astype(F32)
        )
        cut = slice(part * HALF + 128, (part + 1) * HALF)
        out_ref[cut, :] = extra_ref[part * 16 : (part + 1) * 16, :].astype(F32) + (
            mine_ref[cut, :].astype(F32) + other_ref[cut, :].astype(F32)
        )


def start_sum(resid, extra, mine, other):
    return pl.pallas_call(
        start_kernel,
        out_shape=jax.ShapeDtypeStruct((2 * HALF, WIDTH), F32),
        compiler_params=pltpu.CompilerParams(vmem_limit_bytes=VMEM_LIMIT),
        cost_estimate=pl.CostEstimate(flops=10**6, transcendentals=0, bytes_accessed=5000000),
        name="start_sum",
    )(resid, extra, mine, other)


def final_kernel(start_ref, first_ref, second_ref, prefill_ref, decode_ref):
    decode = []
    for part, ref in ((0, first_ref), (1, second_ref)):
        whole = start_ref[part * HALF : (part + 1) * HALF, :] + ref[...].astype(F32)
        prefill_ref[part * 128 : (part + 1) * 128, :] = whole[:128].astype(BF)
        decode.append(whole[128:129])
    decode_ref[...] = jnp.concatenate(decode, axis=0).astype(BF)


def final_sum(start, first, second):
    return pl.pallas_call(
        final_kernel,
        out_shape=(
            jax.ShapeDtypeStruct((ROWS, WIDTH), BF),
            jax.ShapeDtypeStruct((2, WIDTH), BF),
        ),
        compiler_params=pltpu.CompilerParams(vmem_limit_bytes=VMEM_LIMIT),
        cost_estimate=pl.CostEstimate(flops=10**6, transcendentals=0, bytes_accessed=4000000),
        name="final",
    )(start, first, second)


def body(
    prefill_hidden,
    decode_hidden,
    attn_gain,
    w_qkv,
    w_out,
    ffn_gain,
    w_gate_up,
    w_down,
    key_value_cache,
    cache_len,
    slot_of_request,
    held_hidden,
    recomputed_index,
    recomp_count,
):
    device = lax.axis_index("req").astype(jnp.int32).reshape(1)
    rank = device % 4
    gain = attn_gain.reshape(1, WIDTH)
    gain2 = ffn_gain.reshape(1, WIDTH)
    exponent = np.arange(HEAD // 2) * (2.0 / HEAD)
    freq = jnp.asarray(np.tile(THETA**-exponent, 4).reshape(1, 128), F32)
    index = recomputed_index.reshape(8, 128)

    gate_up = jnp.swapaxes(w_gate_up, 1, 2)
    gate_below = send(gate_up, next_z)
    gate_above = send(gate_up, last_z)
    down_below = send(w_down, next_z)
    down_above = send(w_down, last_z)
    gate_far = send(gate_above, last_z)
    down_far = send(down_below, next_z)
    gate_ups = (gate_up, gate_below, gate_above, gate_far)
    downs = (w_down, down_below, down_above, down_far)

    total = 2 * SIDE**3
    spread = jnp.broadcast_to(decode_hidden[None], (total, 2, WIDTH))
    every_row = lax.all_to_all(spread, "req", 0, 0).reshape(256, WIDTH)

    query, kv = prefill_qkv(rank, prefill_hidden, gain, freq, w_qkv)
    zed = send(kv, pair_z)
    core = send(kv, other_core)
    far = send(zed, other_core)

    outgoing = decode_attention(
        device,
        cache_len,
        recomp_count,
        slot_of_request.reshape(1, 256),
        index,
        every_row,
        gain,
        freq,
        w_qkv,
        key_value_cache,
        held_hidden,
    )
    back = lax.all_to_all(outgoing.reshape(total, 2, WIDTH), "req", 0, 0).reshape(256, WIDTH)

    resid, lower, upper = attention(
        rank, query, kv, core, zed, far, w_out, prefill_hidden, gain2
    )
    extra, lower, upper = decode_rows(back, w_out, decode_hidden, gain2, lower, upper)
    from_last = send(lower, next_x)
    from_next = send(upper, last_x)
    lower_across = send(lower, other_core)
    upper_across = send(upper, other_core)
    mine, given = feed_forward(
        (lower, upper, lower_across, upper_across), gate_ups, downs, "feed_own"
    )
    from_last, from_next, mine, given = lax.optimization_barrier(
        (from_last, from_next, mine, given)
    )
    last_across = send(from_last, other_core)
    next_across = send(from_next, other_core)
    given = send(given, other_core)
    guest_mine, guest_given = feed_forward(
        (from_last, from_next, last_across, next_across), gate_ups, downs, "feed_guest"
    )
    guest_given = send(guest_given, other_core)
    first = send(add_half(guest_mine, guest_given, 0), last_x)
    second = send(add_half(guest_mine, guest_given, 1), next_x)
    start = start_sum(resid, extra, mine, given)
    return final_sum(start, first, second)


def solution(mesh):
    return jax.shard_map(
        body,
        mesh=mesh,
        in_specs=(
            P("req", None),
            P("req", None),
            P(),
            P(),
            P(),
            P(),
            P("req", None, None),
            P("req", None, None),
            P("req", None, None),
            P("req"),
            P(),
            P("req", None),
            P("req"),
            P("req"),
        ),
        out_specs=(P("req", None), P("req", None)),
        check_vma=False,
    )
```

```python
import functools

import jax
import jax.numpy as jnp
import numpy as np
from jax import lax
from jax.experimental import pallas as pl
from jax.experimental.pallas import tpu as pltpu
from jax.sharding import PartitionSpec as P

WIDTH = 1280
QUERY_HEADS = 20
HEAD = 64
QW = 1280
KVW = 640
SHARE = 224
GROUP = 16
SIDE = 4
SLOTS = 4
POSITIONS = 1024
ROWS = 256
HALF = 144
EPS = 1e-05
THETA = 10000.0
NEG = -1e30
F32 = jnp.float32
BF = jnp.bfloat16
NT = (((1,), (1,)), ((), ()))
VMEM_LIMIT = 24 << 20


def cost(microseconds):
    return pl.CostEstimate(
        flops=int(microseconds * 10**9), transcendentals=0, bytes_accessed=int(microseconds * 3000000)
    )


def place(y, x, z, core):
    return (((y % SIDE) * SIDE + x % SIDE) * SIDE + z % SIDE) * 2 + core


def moves(step):
    pairs = []
    for y in range(SIDE):
        for x in range(SIDE):
            for z in range(SIDE):
                for core in range(2):
                    pairs.append((place(y, x, z, core), place(*step(y, x, z, core))))
    return pairs


def send(array, step):
    return lax.ppermute(array, "req", moves(step))


def in_hbm(*arrays):
    return [pltpu.with_memory_space_constraint(a, pltpu.MemorySpace.HBM) for a in arrays]


def other_core(y, x, z, core):
    return y, x, z, 1 - core


def next_x(y, x, z, core):
    return y, x + 1, z, core


def last_x(y, x, z, core):
    return y, x - 1, z, core


def next_z(y, x, z, core):
    return y, x, z + 1, core


def last_z(y, x, z, core):
    return y, x, z - 1, core


def pair_z(y, x, z, core):
    return y, x, z ^ 1, core


def norm_rows(rows, gain):
    rows = rows.astype(F32)
    mean = jnp.mean(rows * rows, axis=-1, keepdims=True)
    return (rows * lax.rsqrt(mean + EPS) * gain).astype(BF)


def lanes(shape):
    return lax.broadcasted_iota(jnp.int32, shape, len(shape) - 1)


def sublanes(shape):
    return lax.broadcasted_iota(jnp.int32, shape, len(shape) - 2)


def sine_cosine(angle):
    turns = jnp.floor(angle * (2.0 / np.pi) + 0.5)
    rest = angle - turns * 1.5703125
    rest = rest - turns * 4.837512969970703125e-4
    rest = rest - turns * 7.54978995489188216e-8
    square = rest * rest
    sine = 8.3321608736e-3 + square * -1.9515295891e-4
    sine = rest + rest * square * (-1.6666654611e-1 + square * sine)
    cosine = -1.388731625493765e-3 + square * 2.443315711809948e-5
    cosine = 4.166664568298827e-2 + square * cosine
    cosine = 1.0 - 0.5 * square + square * square * cosine
    quarter = turns.astype(jnp.int32) & 3
    odd = (quarter & 1) == 1
    out_sine = jnp.where(odd, cosine, sine)
    out_cosine = jnp.where(odd, sine, cosine)
    out_sine = jnp.where(quarter >= 2, -out_sine, out_sine)
    out_cosine = jnp.where((quarter == 1) | (quarter == 2), -out_cosine, out_cosine)
    return out_sine, out_cosine


def rope_tables(position, frequency):
    sine, cosine = sine_cosine(position * frequency)
    low = lanes(sine.shape) % HEAD < HEAD // 2
    return cosine, jnp.where(low, -sine, sine)


def rope(chunk, cosine, sine):
    low = lanes(chunk.shape) % HEAD < HEAD // 2
    other = jnp.where(low, pltpu.roll(chunk, 96, 1), pltpu.roll(chunk, 32, 1))
    return chunk * cosine + other * sine


def pack_kernel(gate_up_ref, down_ref, packed_ref):
    packed_ref[: 2 * SHARE, :] = gate_up_ref[...]
    packed_ref[2 * SHARE :, :] = down_ref[...]


def pack_weights(gate_up, down):
    return pl.pallas_call(
        pack_kernel,
        out_shape=jax.ShapeDtypeStruct((3 * SHARE, WIDTH), BF),
        grid=(2,),
        in_specs=[
            pl.BlockSpec((None, 2 * SHARE, WIDTH // 2), lambda i: (0, 0, i)),
            pl.BlockSpec((None, SHARE, WIDTH // 2), lambda i: (0, 0, i)),
        ],
        out_specs=pl.BlockSpec((3 * SHARE, WIDTH // 2), lambda i: (0, i)),
        compiler_params=pltpu.CompilerParams(vmem_limit_bytes=VMEM_LIMIT),
        cost_estimate=cost(1.5),
        name="pack",
    )(gate_up, down)


def qkv_kernel(rank_ref, hidden_ref, gain_ref, freq_ref, w_ref, query_ref, kv_ref, normed, cos, sin):
    step = pl.program_id(0)

    @pl.when(step == 0)
    def _():
        normed[...] = norm_rows(hidden_ref[...], gain_ref[...])
        position = (sublanes((ROWS, 128)) * 4 + rank_ref[0]).astype(F32)
        cos[...], sin[...] = rope_tables(position, freq_ref[...])

    projected = jnp.dot(normed[...], w_ref[...], preferred_element_type=F32)
    chunks = [projected[:, i * 128 : (i + 1) * 128] for i in range(5)]

    @pl.when(step < 2)
    def _():
        for i in range(5):
            roped = rope(chunks[i], cos[...], sin[...]).astype(BF)
            query_ref[:, i * 128 : (i + 1) * 128] = roped * jnp.asarray(0.125, BF)

    @pl.when(step == 2)
    def _():
        low = lanes((ROWS, 128)) < HEAD
        first = rope(chunks[0], cos[...], sin[...])
        second = rope(chunks[1], cos[...], sin[...])
        third = jnp.where(low, rope(chunks[2], cos[...], sin[...]), chunks[2])
        swap = lambda value: pltpu.roll(value, 64, 1)
        out = [
            jnp.where(low, first, third),
            jnp.where(low, swap(first), swap(chunks[3])),
            jnp.where(low, second, chunks[3]),
            jnp.where(low, swap(second), swap(chunks[4])),
            jnp.where(low, third, chunks[4]),
        ]
        for i in range(5):
            kv_ref[:, i * 128 : (i + 1) * 128] = out[i].astype(BF)


def prefill_qkv(rank, hidden, gain, freq, w_qkv):
    return pl.pallas_call(
        qkv_kernel,
        out_shape=(
            jax.ShapeDtypeStruct((ROWS, QW), BF),
            jax.ShapeDtypeStruct((ROWS, KVW), BF),
        ),
        grid=(3,),
        in_specs=[
            pl.BlockSpec(memory_space=pltpu.SMEM),
            pl.BlockSpec((ROWS, WIDTH), lambda j: (0, 0)),
            pl.BlockSpec((1, WIDTH), lambda j: (0, 0)),
            pl.BlockSpec((1, 128), lambda j: (0, 0)),
            pl.BlockSpec((WIDTH, KVW), lambda j: (0, j)),
        ],
        out_specs=(
            pl.BlockSpec((ROWS, KVW), lambda j: (0, jnp.minimum(j, 1))),
            pl.BlockSpec((ROWS, KVW), lambda j: (0, 0)),
        ),
        scratch_shapes=[
            pltpu.VMEM((ROWS, WIDTH), BF),
            pltpu.VMEM((ROWS, 128), F32),
            pltpu.VMEM((ROWS, 128), F32),
        ],
        compiler_params=pltpu.CompilerParams(vmem_limit_bytes=VMEM_LIMIT),
        cost_estimate=cost(7),
        name="prefill_qkv",
    )(rank, hidden, gain, freq, w_qkv)


def column(row):
    return jnp.broadcast_to(row, (128, 128)).T


def decode_kernel(
    device_ref,
    length_ref,
    count_ref,
    slot_ref,
    index_ref,
    rows_ref,
    gain_ref,
    freq_ref,
    w_ref,
    cache_ref,
    hidden_ref,
    out_ref,
    held_ref,
    spread,
    query,
    fresh_key,
    fresh_value,
    over,
    result,
):
    tick = pl.program_id(0)
    step = tick - SLOTS
    first_slot = device_ref[0] * SLOTS

    @pl.when(tick < SLOTS)
    def _():
        normed = norm_rows(hidden_ref[...], gain_ref[...])
        projected = jnp.dot(normed, w_ref[:, QW:], preferred_element_type=F32)
        position = (index_ref[pl.ds(tick * 2, 2), :] % POSITIONS).astype(F32)
        position = jnp.concatenate([column(position[0:1]), column(position[1:2])], axis=0)
        cosine, sine = rope_tables(position, freq_ref[...])
        low = lanes((256, 128)) < HEAD
        rows = pl.ds(pl.multiple_of(tick * 256, 256), 256)
        for i in range(5):
            chunk = projected[:, i * 128 : (i + 1) * 128]
            if i < 2:
                chunk = rope(chunk, cosine, sine)
            elif i == 2:
                chunk = jnp.where(low, rope(chunk, cosine, sine), chunk)
            held_ref[rows, i * 128 : (i + 1) * 128] = chunk.astype(BF)

    index_rows = [index_ref[i : i + 1, :] for i in range(8)]

    @pl.when(step == 0)
    def _():
        spread[...] = (
            sublanes((QW, 384)) % HEAD == lanes((QW, 384)) % HEAD
        ).astype(F32).astype(BF)
        wanted = jnp.broadcast_to(slot_ref[...], (8, 256))
        slot = sublanes((8, 256))
        chosen = ((wanted == first_slot + slot) & (slot < SLOTS)).astype(F32).astype(BF)
        rows = jnp.dot(chosen, rows_ref[...], preferred_element_type=F32)
        normed = norm_rows(rows, gain_ref[...])
        projected = jnp.dot(normed, w_ref[...], preferred_element_type=F32)
        projected = projected.astype(BF).astype(F32)
        row = sublanes((8, 128))
        position = jnp.zeros((8, 128), F32)
        for j in range(SLOTS):
            position = jnp.where(row == j, length_ref[j].astype(F32), position)
        cosine, sine = rope_tables(position, freq_ref[...])
        chunks = [projected[:, i * 128 : (i + 1) * 128] for i in range(15)]
        roped = [rope(chunks[i], cosine, sine).astype(BF) for i in range(13)]
        whole = jnp.concatenate(roped[:10], axis=1).astype(F32) * 0.125
        head_of = sublanes((32, QW))
        keep = lanes((32, QW)) // HEAD == head_of
        group = sublanes((32, 384))
        block = (lanes((32, 384)) // HEAD == group // 4) & (group < QUERY_HEADS)
        for j in range(SLOTS):
            placed = jnp.where(keep, jnp.broadcast_to(whole[j : j + 1], (32, QW)), 0.0)
            turned = jnp.dot(placed.astype(BF), spread[...], preferred_element_type=F32)
            query[j * 32 : (j + 1) * 32, :] = jnp.where(block, turned, 0.0).astype(BF)
        fresh_key[...] = jnp.concatenate(roped[10:13], axis=1).astype(F32)
        fresh_value[...] = jnp.concatenate(chunks[12:15], axis=1)
        counts = jnp.zeros((32, 128), F32)
        for i in range(8):
            entry = i * 128 + lanes((32, 128))
            live = entry < count_ref[0]
            upper = jnp.broadcast_to(index_rows[i] // 128, (32, 128)) == sublanes((32, 128))
            upper = (upper & live).astype(F32).astype(BF)
            lower = jnp.broadcast_to(index_rows[i] % 128, (128, 128)) == sublanes((128, 128))
            lower = lower.astype(F32).astype(BF)
            counts = counts + lax.dot_general(upper, lower, NT, preferred_element_type=F32)
        over[...] = counts

    @pl.when(step >= 0)
    def _():
        length = length_ref[step]
        queries = query[pl.ds(pl.multiple_of(step * 32, 32), 32), :]
        taken = over[pl.ds(pl.multiple_of(step * 8, 8), 8), :]
        taken = jnp.concatenate([taken[i : i + 1, :] for i in range(8)], axis=1)
        cache_live = (lanes((1, POSITIONS)) < length) & (taken < 0.5)
        index = jnp.concatenate(index_rows, axis=1)
        held_live = (
            (lanes((1, 1024)) < count_ref[0])
            & (index // POSITIONS == step)
            & (index % POSITIONS < length)
        )
        cache_score = lax.dot_general(queries, cache_ref[:, :384], NT, preferred_element_type=F32)
        held_score = lax.dot_general(queries, held_ref[:, :384], NT, preferred_element_type=F32)
        own_score = jnp.sum(
            queries.astype(F32) * fresh_key[pl.ds(step, 1), :], axis=-1, keepdims=True
        )
        cache_live = jnp.broadcast_to(cache_live, cache_score.shape)
        held_live = jnp.broadcast_to(held_live, held_score.shape)
        cache_score = jnp.where(cache_live, cache_score, NEG)
        held_score = jnp.where(held_live, held_score, NEG)
        top = jnp.maximum(
            jnp.maximum(
                jnp.max(cache_score, axis=-1, keepdims=True), jnp.max(held_score, axis=-1, keepdims=True)
            ),
            own_score,
        )
        cache_weight = jnp.where(cache_live, jnp.exp(cache_score - top), 0.0)
        held_weight = jnp.where(held_live, jnp.exp(held_score - top), 0.0)
        own_weight = jnp.exp(own_score - top)
        total = (
            jnp.sum(cache_weight, axis=-1, keepdims=True)
            + jnp.sum(held_weight, axis=-1, keepdims=True)
            + own_weight
        )
        mixed = jnp.dot(cache_weight.astype(BF), cache_ref[:, 256:], preferred_element_type=F32)
        mixed += jnp.dot(held_weight.astype(BF), held_ref[:, 256:], preferred_element_type=F32)
        mixed += own_weight.astype(BF).astype(F32) * fresh_value[pl.ds(step, 1), :]
        group = sublanes((32, 384))
        block = (lanes((32, 384)) // HEAD == group // 4 + 1) & (group < QUERY_HEADS)
        mixed = jnp.where(block, mixed / total, 0.0).astype(BF)
        turned = lax.dot_general(mixed, spread[...], NT, preferred_element_type=F32)
        keep = lanes((32, QW)) // HEAD == sublanes((32, QW))
        result[pl.ds(step, 1), :] = jnp.sum(jnp.where(keep, turned, 0.0), axis=0, keepdims=True)

    @pl.when(step == SLOTS - 1)
    def _():
        wanted = jnp.broadcast_to(slot_ref[...], (8, 256))
        slot = sublanes((8, 256))
        chosen = ((wanted == first_slot + slot) & (slot < SLOTS)).astype(F32).astype(BF)
        good = jnp.where(sublanes((8, QW)) < SLOTS, result[...], 0.0).astype(BF)
        out_ref[...] = lax.dot_general(
            chosen, good, (((0,), (0,)), ((), ())), preferred_element_type=F32
        ).astype(BF)


def decode_attention(
    device, length, count, slots, index, rows, gain, freq, w_qkv, cache, hidden
):
    smem = pl.BlockSpec(memory_space=pltpu.SMEM)
    full = lambda shape: pl.BlockSpec(shape, lambda j: (0,) * len(shape))
    return pl.pallas_call(
        decode_kernel,
        out_shape=jax.ShapeDtypeStruct((256, QW), BF),
        grid=(2 * SLOTS,),
        in_specs=[
            smem,
            smem,
            smem,
            full((1, 256)),
            full((8, 128)),
            full((256, WIDTH)),
            full((1, WIDTH)),
            full((1, 128)),
            pl.BlockSpec(
                (WIDTH, QW + KVW), lambda j: (0, 0), pipeline_mode=pl.Buffered(1)
            ),
            pl.BlockSpec((None, POSITIONS, KVW), lambda j: (jnp.maximum(j - SLOTS, 0), 0, 0)),
            pl.BlockSpec((256, WIDTH), lambda j: (jnp.minimum(j, SLOTS - 1), 0)),
        ],
        out_specs=full((256, QW)),
        scratch_shapes=[
            pltpu.VMEM((1024, KVW), BF),
            pltpu.VMEM((QW, 384), BF),
            pltpu.VMEM((128, 384), BF),
            pltpu.VMEM((8, 384), F32),
            pltpu.VMEM((8, 384), F32),
            pltpu.VMEM((32, 128), F32),
            pltpu.VMEM((8, QW), F32),
        ],
        compiler_params=pltpu.CompilerParams(vmem_limit_bytes=VMEM_LIMIT),
        cost_estimate=cost(17),
        name="decode",
    )(device, length, count, slots, index, rows, gain, freq, w_qkv, cache, hidden)


def attention_kernel(
    rank_ref,
    query_ref,
    own_ref,
    core_ref,
    zed_ref,
    far_ref,
    w_ref,
    hidden_ref,
    gain_ref,
    resid_ref,
    lower_ref,
    upper_ref,
    total,
    mask,
):
    group = pl.program_id(0)

    @pl.when(group == 0)
    def _():
        total[...] = jnp.zeros_like(total)
        rank = rank_ref[0]
        row = sublanes((128, 128))
        col = lanes((128, 128))
        for piece in range(4):
            other = rank ^ piece
            bound = jnp.where(other <= rank, 0, 1)
            mask[:, piece * 128 : (piece + 1) * 128] = jnp.where(col + bound <= row, 0.0, NEG)

    pieces = [own_ref, core_ref, zed_ref, far_ref]
    keys = jnp.concatenate(
        [ref[h * 128 : (h + 1) * 128, :] for h in range(2) for ref in pieces], axis=0
    )
    low = lanes((1024, 128)) < HEAD
    wide = keys.astype(F32)
    values = jnp.where(low, pltpu.roll(wide, 64, 1), wide).astype(BF)
    values = jnp.concatenate([values, jnp.ones((1024, 128), BF)], axis=1)
    low = lanes((128, 128)) < HEAD
    blocked = mask[...]
    mixed = []
    for tile in range(2):
        heads = []
        for pair in range(2):
            two = query_ref[tile * 128 : (tile + 1) * 128, pair * 128 : (pair + 1) * 128].astype(F32)
            heads.append(jnp.where(low, two, 0.0).astype(BF))
            heads.append(jnp.where(low, pltpu.roll(two, 64, 1), 0.0).astype(BF))
        out = []
        for head in heads:
            count = 512 * (tile + 1)
            score = lax.dot_general(head, keys[:count], NT, preferred_element_type=F32)
            if tile == 0:
                score = score + blocked
            else:
                score = jnp.concatenate([score[:, :512], score[:, 512:] + blocked], axis=1)
            top = jnp.max(score, axis=-1, keepdims=True)
            weight = jnp.exp(score - top).astype(BF)
            both = jnp.dot(weight, values[:count], preferred_element_type=F32)
            out.append(both[:, :128] / both[:, 128:])
        mixed.append(
            jnp.concatenate(
                [jnp.where(low, out[0], out[1]), jnp.where(low, out[2], out[3])], axis=1
            ).astype(BF)
        )
    rows = jnp.concatenate(mixed, axis=0)
    total[...] += jnp.dot(rows, w_ref[...], preferred_element_type=F32)

    @pl.when(group == 4)
    def _():
        for part in range(2):
            cut = slice(part * 128, (part + 1) * 128)
            resid = (hidden_ref[cut, :].astype(F32) + total[cut, :]).astype(BF)
            resid_ref[cut, :] = resid
            (lower_ref, upper_ref)[part][:128, :] = norm_rows(resid, gain_ref[...])


def attention(rank, query, own, core, zed, far, w_out, hidden, gain):
    full = lambda shape: pl.BlockSpec(shape, lambda g: (0,) * len(shape))
    side = pl.BlockSpec((ROWS, 128), lambda g: (0, g))
    return pl.pallas_call(
        attention_kernel,
        out_shape=(
            jax.ShapeDtypeStruct((ROWS, WIDTH), BF),
            jax.ShapeDtypeStruct((HALF, WIDTH), BF),
            jax.ShapeDtypeStruct((HALF, WIDTH), BF),
        ),
        grid=(5,),
        in_specs=[
            pl.BlockSpec(memory_space=pltpu.SMEM),
            pl.BlockSpec((ROWS, 256), lambda g: (0, g)),
            side,
            side,
            side,
            side,
            pl.BlockSpec((256, WIDTH), lambda g: (g, 0)),
            full((ROWS, WIDTH)),
            full((1, WIDTH)),
        ],
        out_specs=(
            full((ROWS, WIDTH)),
            full((HALF, WIDTH)),
            full((HALF, WIDTH)),
        ),
        scratch_shapes=[
            pltpu.VMEM((ROWS, WIDTH), F32),
            pltpu.VMEM((128, 512), F32),
        ],
        compiler_params=pltpu.CompilerParams(vmem_limit_bytes=VMEM_LIMIT),
        cost_estimate=cost(12),
        name="attention",
    )(rank, query, own, core, zed, far, w_out, hidden, gain)


def decode_rows_kernel(back_ref, w_ref, decode_ref, gain_ref, lower_in, upper_in, resid_ref, lower_ref, upper_ref):
    del lower_in, upper_in
    source = lanes((32, 256)) % 2
    row = sublanes((32, 256))
    pick = ((row == 0) & (source == 0)) | ((row == 16) & (source == 1))
    pick = pick.astype(F32).astype(BF)
    mixed = jnp.dot(pick, back_ref[...], preferred_element_type=F32).astype(BF)
    projection = jnp.dot(mixed, w_ref[...], preferred_element_type=F32)
    first = sublanes((16, WIDTH)) == 0
    single = decode_ref[...].astype(F32)
    for part in range(2):
        cut = slice(part * 16, (part + 1) * 16)
        alone = jnp.where(first, jnp.broadcast_to(single[part : part + 1], (16, WIDTH)), 0.0)
        resid = (alone + projection[cut]).astype(BF)
        resid_ref[cut, :] = resid
        (lower_ref, upper_ref)[part][...] = norm_rows(resid, gain_ref[...])


def decode_rows(back, w_out, decode, gain, lower, upper):
    full = lambda shape: pl.BlockSpec(shape, lambda g: (0,) * len(shape))
    tail = pl.BlockSpec((16, WIDTH), lambda g: (8, 0))
    return pl.pallas_call(
        decode_rows_kernel,
        out_shape=(
            jax.ShapeDtypeStruct((32, WIDTH), BF),
            jax.ShapeDtypeStruct((HALF, WIDTH), BF),
            jax.ShapeDtypeStruct((HALF, WIDTH), BF),
        ),
        grid=(1,),
        in_specs=[
            full((256, WIDTH)),
            full((WIDTH, WIDTH)),
            full((2, WIDTH)),
            full((1, WIDTH)),
            tail,
            tail,
        ],
        out_specs=(full((32, WIDTH)), tail, tail),
        input_output_aliases={4: 1, 5: 2},
        compiler_params=pltpu.CompilerParams(vmem_limit_bytes=VMEM_LIMIT),
        cost_estimate=cost(3),
        name="decode_rows",
    )(back, w_out, decode, gain, lower, upper)


def feed_kernel(*refs):
    pieces, packs, far_low, far_high = refs[:2], refs[2:8], refs[8:10], refs[10:12]
    outs, act = refs[12:14], refs[14]
    cut = 3 * SHARE // 2
    rows = jnp.concatenate([ref[...] for ref in pieces], axis=0)
    downs = []
    for k in range(8):
        if k < 6:
            gate_rows = packs[k][:SHARE, :]
            up_rows = packs[k][SHARE : 2 * SHARE, :]
            downs.append(packs[k][2 * SHARE :, :])
        else:
            low, high = far_low[k - 6], far_high[k - 6]
            gate_rows = low[:SHARE, :]
            up_rows = jnp.concatenate([low[SHARE:, :], high[: 2 * SHARE - cut, :]], axis=0)
            downs.append(high[2 * SHARE - cut :, :])
        gate = lax.dot_general(rows, gate_rows, NT, preferred_element_type=F32)
        up = lax.dot_general(rows, up_rows, NT, preferred_element_type=F32)
        act[:, k * SHARE : (k + 1) * SHARE] = (gate / (1.0 + jnp.exp(-gate)) * up).astype(BF)
    down = jnp.dot(act[...], jnp.concatenate(downs, axis=0), preferred_element_type=F32)
    outs[0][...] = down[:HALF].astype(BF)
    outs[1][...] = down[HALF:].astype(BF)


def feed_forward(pieces, weights, name):
    vmem = pl.BlockSpec(memory_space=pltpu.VMEM)
    return pl.pallas_call(
        feed_kernel,
        out_shape=(jax.ShapeDtypeStruct((HALF, WIDTH), BF),) * 2,
        in_specs=[vmem] * 12,
        out_specs=(vmem,) * 2,
        scratch_shapes=[pltpu.VMEM((2 * HALF, 8 * SHARE), BF)],
        compiler_params=pltpu.CompilerParams(vmem_limit_bytes=VMEM_LIMIT),
        cost_estimate=cost(8),
        name=name,
    )(*pieces, *weights)


def start_kernel(resid_ref, extra_ref, lower_ref, upper_ref, out_ref):
    for part in range(2):
        mine_ref = (lower_ref, upper_ref)[part]
        cut = slice(part * HALF, part * HALF + 128)
        out_ref[cut, :] = resid_ref[part * 128 : (part + 1) * 128, :].astype(F32) + mine_ref[
            :128, :
        ].astype(F32)
        cut = slice(part * HALF + 128, (part + 1) * HALF)
        out_ref[cut, :] = extra_ref[part * 16 : (part + 1) * 16, :].astype(F32) + mine_ref[
            128:, :
        ].astype(F32)


def start_sum(resid, extra, mine):
    return pl.pallas_call(
        start_kernel,
        out_shape=jax.ShapeDtypeStruct((2 * HALF, WIDTH), F32),
        in_specs=[pl.BlockSpec(memory_space=pltpu.VMEM)] * 4,
        out_specs=pl.BlockSpec(memory_space=pltpu.VMEM),
        compiler_params=pltpu.CompilerParams(vmem_limit_bytes=VMEM_LIMIT),
        cost_estimate=cost(1.5),
        name="start_sum",
    )(resid, extra, *mine)


def final_kernel(start_ref, first_ref, second_ref, prefill_ref, decode_ref):
    decode = []
    for part, ref in ((0, first_ref), (1, second_ref)):
        whole = start_ref[part * HALF : (part + 1) * HALF, :] + ref[...].astype(F32)
        prefill_ref[part * 128 : (part + 1) * 128, :] = whole[:128].astype(BF)
        decode.append(whole[128:129])
    decode_ref[...] = jnp.concatenate(decode, axis=0).astype(BF)


def final_sum(start, first, second):
    return pl.pallas_call(
        final_kernel,
        out_shape=(
            jax.ShapeDtypeStruct((ROWS, WIDTH), BF),
            jax.ShapeDtypeStruct((2, WIDTH), BF),
        ),
        in_specs=[pl.BlockSpec(memory_space=pltpu.VMEM)] * 3,
        compiler_params=pltpu.CompilerParams(vmem_limit_bytes=VMEM_LIMIT),
        cost_estimate=cost(1.5),
        name="final",
    )(start, first, second)


def body(
    prefill_hidden,
    decode_hidden,
    attn_gain,
    w_qkv,
    w_out,
    ffn_gain,
    w_gate_up,
    w_down,
    key_value_cache,
    cache_len,
    slot_of_request,
    held_hidden,
    recomputed_index,
    recomp_count,
):
    device = lax.axis_index("req").astype(jnp.int32).reshape(1)
    rank = device % 4
    gain = attn_gain.reshape(1, WIDTH)
    gain2 = ffn_gain.reshape(1, WIDTH)
    exponent = np.arange(HEAD // 2) * (2.0 / HEAD)
    freq = jnp.asarray(np.tile(THETA**-exponent, 4).reshape(1, 128), F32)
    index = recomputed_index.reshape(8, 128)

    w_qkv, w_out, key_value_cache, held_hidden, prefill_hidden = in_hbm(
        w_qkv, w_out, key_value_cache, held_hidden, prefill_hidden
    )
    total = 2 * SIDE**3
    spread = jnp.broadcast_to(decode_hidden[None], (total, 2, WIDTH))
    every_row = lax.all_to_all(spread, "req", 0, 0).reshape(256, WIDTH)

    query, kv = prefill_qkv(rank, prefill_hidden, gain, freq, w_qkv)
    query, kv = in_hbm(query, kv)
    zed = send(kv, pair_z)
    core = send(kv, other_core)
    gate_up, w_down, query = lax.optimization_barrier(
        (jnp.swapaxes(w_gate_up, 1, 2), w_down, query)
    )
    packed = pack_weights(gate_up, w_down)
    below = send(packed, next_z)
    above = send(packed, last_z)
    packed_core = send(packed, other_core)
    outgoing = decode_attention(
        device,
        cache_len,
        recomp_count,
        slot_of_request.reshape(1, 256),
        index,
        every_row,
        gain,
        freq,
        w_qkv,
        key_value_cache,
        held_hidden,
    )
    outgoing, zed, core, below, above, packed_core = lax.optimization_barrier(
        (outgoing, zed, core, below, above, packed_core)
    )
    far = send(zed, other_core)
    core, zed, far = in_hbm(core, zed, far)
    cut = 3 * SHARE // 2
    far_low = send(below[:cut], next_z)
    far_high = send(above[cut:], last_z)
    below_core = send(below, other_core)
    above_core = send(above, other_core)
    back = lax.all_to_all(outgoing.reshape(total, 2, WIDTH), "req", 0, 0).reshape(256, WIDTH)

    resid, lower, upper = attention(
        rank, query, kv, core, zed, far, w_out, prefill_hidden, gain2
    )
    (resid,) = in_hbm(resid)
    lower, upper, back, far_low, far_high, below_core, above_core = lax.optimization_barrier(
        (lower, upper, back, far_low, far_high, below_core, above_core)
    )
    far_low_core = send(far_low, other_core)
    far_high_core = send(far_high, other_core)
    extra, lower, upper = decode_rows(back, w_out, decode_hidden, gain2, lower, upper)
    from_last = send(lower, next_x)
    from_next = send(upper, last_x)
    weights = (packed, packed_core, below, below_core, above, above_core)
    weights += (far_low, far_low_core, far_high, far_high_core)
    mine = feed_forward((lower, upper), weights, "feed_own")
    from_last, from_next, mine = lax.optimization_barrier((from_last, from_next, mine))
    guest = feed_forward((from_last, from_next), weights, "feed_guest")
    first = send(guest[0], last_x)
    second = send(guest[1], next_x)
    start = start_sum(resid, extra, mine)
    return final_sum(start, first, second)


def solution(mesh):
    return jax.shard_map(
        body,
        mesh=mesh,
        in_specs=(
            P("req", None),
            P("req", None),
            P(),
            P(),
            P(),
            P(),
            P("req", None, None),
            P("req", None, None),
            P("req", None, None),
            P("req"),
            P(),
            P("req", None),
            P("req"),
            P("req"),
        ),
        out_specs=(P("req", None), P("req", None)),
        check_vma=False,
    )
```

```python
import functools

import jax
import jax.numpy as jnp
import numpy as np
from jax import lax
from jax.experimental import pallas as pl
from jax.experimental.pallas import tpu as pltpu
from jax.sharding import PartitionSpec as P

WIDTH = 1280
QUERY_HEADS = 20
HEAD = 64
QW = 1280
KVW = 640
SHARE = 224
PART = 3 * SHARE // 2
GROUP = 16
SIDE = 4
SLOTS = 4
POSITIONS = 1024
ROWS = 256
HALF = 144
EPS = 1e-05
THETA = 10000.0
NEG = -1e30
F32 = jnp.float32
BF = jnp.bfloat16
NT = (((1,), (1,)), ((), ()))
VMEM_LIMIT = 24 << 20


def cost(microseconds):
    return pl.CostEstimate(
        flops=int(microseconds * 10**9), transcendentals=0, bytes_accessed=int(microseconds * 3000000)
    )


def place(y, x, z, core):
    return (((y % SIDE) * SIDE + x % SIDE) * SIDE + z % SIDE) * 2 + core


def moves(step):
    pairs = []
    for y in range(SIDE):
        for x in range(SIDE):
            for z in range(SIDE):
                for core in range(2):
                    pairs.append((place(y, x, z, core), place(*step(y, x, z, core))))
    return pairs


def send(array, step):
    return lax.ppermute(array, "req", moves(step))


def in_hbm(*arrays):
    return [pltpu.with_memory_space_constraint(a, pltpu.MemorySpace.HBM) for a in arrays]


def other_core(y, x, z, core):
    return y, x, z, 1 - core


def next_x(y, x, z, core):
    return y, x + 1, z, core


def last_x(y, x, z, core):
    return y, x - 1, z, core


def next_z(y, x, z, core):
    return y, x, z + 1, core


def last_z(y, x, z, core):
    return y, x, z - 1, core


def pair_z(y, x, z, core):
    return y, x, z ^ 1, core


def norm_rows(rows, gain):
    rows = rows.astype(F32)
    mean = jnp.mean(rows * rows, axis=-1, keepdims=True)
    return (rows * lax.rsqrt(mean + EPS) * gain).astype(BF)


def lanes(shape):
    return lax.broadcasted_iota(jnp.int32, shape, len(shape) - 1)


def sublanes(shape):
    return lax.broadcasted_iota(jnp.int32, shape, len(shape) - 2)


def sine_cosine(angle):
    turns = jnp.floor(angle * (2.0 / np.pi) + 0.5)
    rest = angle - turns * 1.5703125
    rest = rest - turns * 4.837512969970703125e-4
    rest = rest - turns * 7.54978995489188216e-8
    square = rest * rest
    sine = 8.3321608736e-3 + square * -1.9515295891e-4
    sine = rest + rest * square * (-1.6666654611e-1 + square * sine)
    cosine = -1.388731625493765e-3 + square * 2.443315711809948e-5
    cosine = 4.166664568298827e-2 + square * cosine
    cosine = 1.0 - 0.5 * square + square * square * cosine
    quarter = turns.astype(jnp.int32) & 3
    odd = (quarter & 1) == 1
    out_sine = jnp.where(odd, cosine, sine)
    out_cosine = jnp.where(odd, sine, cosine)
    out_sine = jnp.where(quarter >= 2, -out_sine, out_sine)
    out_cosine = jnp.where((quarter == 1) | (quarter == 2), -out_cosine, out_cosine)
    return out_sine, out_cosine


def rope_tables(position, frequency):
    sine, cosine = sine_cosine(position * frequency)
    low = lanes(sine.shape) % HEAD < HEAD // 2
    return cosine, jnp.where(low, -sine, sine)


def rope(chunk, cosine, sine):
    low = lanes(chunk.shape) % HEAD < HEAD // 2
    other = jnp.where(low, pltpu.roll(chunk, 96, 1), pltpu.roll(chunk, 32, 1))
    return chunk * cosine + other * sine


def pack_kernel(gate_up_ref, down_ref, low_ref, high_ref):
    low_ref[...] = gate_up_ref[:PART, :]
    high_ref[: 2 * SHARE - PART, :] = gate_up_ref[PART:, :]
    high_ref[2 * SHARE - PART :, :] = down_ref[...]


def pack_weights(gate_up, down):
    half = jax.ShapeDtypeStruct((PART, WIDTH), BF)
    block = pl.BlockSpec((PART, WIDTH // 2), lambda i: (0, i))
    return pl.pallas_call(
        pack_kernel,
        out_shape=(half, half),
        grid=(2,),
        in_specs=[
            pl.BlockSpec((None, 2 * SHARE, WIDTH // 2), lambda i: (0, 0, i)),
            pl.BlockSpec((None, SHARE, WIDTH // 2), lambda i: (0, 0, i)),
        ],
        out_specs=(block, block),
        compiler_params=pltpu.CompilerParams(vmem_limit_bytes=VMEM_LIMIT),
        cost_estimate=cost(1.5),
        name="pack",
    )(gate_up, down)


def kv_kernel(rank_ref, hidden_ref, gain_ref, freq_ref, w_ref, kv_ref):
    normed = norm_rows(hidden_ref[...], gain_ref[...])
    position = (sublanes((ROWS, 128)) * 4 + rank_ref[0]).astype(F32)
    cosine, sine = rope_tables(position, freq_ref[...])
    projected = jnp.dot(normed, w_ref[...], preferred_element_type=F32)
    chunks = [projected[:, i * 128 : (i + 1) * 128] for i in range(5)]
    low = lanes((ROWS, 128)) < HEAD
    first = rope(chunks[0], cosine, sine)
    second = rope(chunks[1], cosine, sine)
    third = jnp.where(low, rope(chunks[2], cosine, sine), chunks[2])
    swap = lambda value: pltpu.roll(value, 64, 1)
    out = [
        jnp.where(low, first, third),
        jnp.where(low, swap(first), swap(chunks[3])),
        jnp.where(low, second, chunks[3]),
        jnp.where(low, swap(second), swap(chunks[4])),
        jnp.where(low, third, chunks[4]),
    ]
    for i in range(5):
        kv_ref[:, i * 128 : (i + 1) * 128] = out[i].astype(BF)


def query_kernel(rank_ref, hidden_ref, gain_ref, freq_ref, w_ref, query_ref, normed, cos, sin):
    @pl.when(pl.program_id(0) == 0)
    def _():
        normed[...] = norm_rows(hidden_ref[...], gain_ref[...])
        position = (sublanes((ROWS, 128)) * 4 + rank_ref[0]).astype(F32)
        cos[...], sin[...] = rope_tables(position, freq_ref[...])

    projected = jnp.dot(normed[...], w_ref[...], preferred_element_type=F32)
    for i in range(5):
        roped = rope(projected[:, i * 128 : (i + 1) * 128], cos[...], sin[...]).astype(BF)
        query_ref[:, i * 128 : (i + 1) * 128] = roped * jnp.asarray(0.125, BF)


def project(rank, hidden, gain, freq, w_qkv, keys):
    steps = 1 if keys else 2
    scratch = [
        pltpu.VMEM((ROWS, WIDTH), BF),
        pltpu.VMEM((ROWS, 128), F32),
        pltpu.VMEM((ROWS, 128), F32),
    ]
    return pl.pallas_call(
        kv_kernel if keys else query_kernel,
        out_shape=jax.ShapeDtypeStruct((ROWS, KVW * steps), BF),
        grid=(steps,),
        in_specs=[
            pl.BlockSpec(memory_space=pltpu.SMEM),
            pl.BlockSpec((ROWS, WIDTH), lambda j: (0, 0)),
            pl.BlockSpec((1, WIDTH), lambda j: (0, 0)),
            pl.BlockSpec((1, 128), lambda j: (0, 0)),
            pl.BlockSpec((WIDTH, KVW), (lambda j: (0, 2)) if keys else (lambda j: (0, j))),
        ],
        out_specs=pl.BlockSpec((ROWS, KVW), lambda j: (0, j)),
        scratch_shapes=[] if keys else scratch,
        compiler_params=pltpu.CompilerParams(vmem_limit_bytes=VMEM_LIMIT),
        cost_estimate=cost(3 if keys else 5),
        name="prefill_kv" if keys else "prefill_query",
    )(rank, hidden, gain, freq, w_qkv)


def column(row):
    return jnp.broadcast_to(row, (128, 128)).T


def decode_kernel(
    device_ref,
    length_ref,
    count_ref,
    slot_ref,
    index_ref,
    rows_ref,
    gain_ref,
    freq_ref,
    w_ref,
    cache_ref,
    hidden_ref,
    out_ref,
    held_ref,
    spread,
    query,
    fresh_key,
    fresh_value,
    over,
    result,
):
    tick = pl.program_id(0)
    step = tick - SLOTS
    first_slot = device_ref[0] * SLOTS

    @pl.when(tick < SLOTS)
    def _():
        normed = norm_rows(hidden_ref[...], gain_ref[...])
        projected = jnp.dot(normed, w_ref[:, QW:], preferred_element_type=F32)
        position = (index_ref[pl.ds(tick * 2, 2), :] % POSITIONS).astype(F32)
        position = jnp.concatenate([column(position[0:1]), column(position[1:2])], axis=0)
        cosine, sine = rope_tables(position, freq_ref[...])
        low = lanes((256, 128)) < HEAD
        rows = pl.ds(pl.multiple_of(tick * 256, 256), 256)
        for i in range(5):
            chunk = projected[:, i * 128 : (i + 1) * 128]
            if i < 2:
                chunk = rope(chunk, cosine, sine)
            elif i == 2:
                chunk = jnp.where(low, rope(chunk, cosine, sine), chunk)
            held_ref[rows, i * 128 : (i + 1) * 128] = chunk.astype(BF)

    index_rows = [index_ref[i : i + 1, :] for i in range(8)]

    @pl.when(step == 0)
    def _():
        spread[...] = (
            sublanes((QW, 384)) % HEAD == lanes((QW, 384)) % HEAD
        ).astype(F32).astype(BF)
        wanted = jnp.broadcast_to(slot_ref[...], (8, 256))
        slot = sublanes((8, 256))
        chosen = ((wanted == first_slot + slot) & (slot < SLOTS)).astype(F32).astype(BF)
        rows = jnp.dot(chosen, rows_ref[...], preferred_element_type=F32)
        normed = norm_rows(rows, gain_ref[...])
        projected = jnp.dot(normed, w_ref[...], preferred_element_type=F32)
        projected = projected.astype(BF).astype(F32)
        row = sublanes((8, 128))
        position = jnp.zeros((8, 128), F32)
        for j in range(SLOTS):
            position = jnp.where(row == j, length_ref[j].astype(F32), position)
        cosine, sine = rope_tables(position, freq_ref[...])
        chunks = [projected[:, i * 128 : (i + 1) * 128] for i in range(15)]
        roped = [rope(chunks[i], cosine, sine).astype(BF) for i in range(13)]
        whole = jnp.concatenate(roped[:10], axis=1).astype(F32) * 0.125
        head_of = sublanes((32, QW))
        keep = lanes((32, QW)) // HEAD == head_of
        group = sublanes((32, 384))
        block = (lanes((32, 384)) // HEAD == group // 4) & (group < QUERY_HEADS)
        for j in range(SLOTS):
            placed = jnp.where(keep, jnp.broadcast_to(whole[j : j + 1], (32, QW)), 0.0)
            turned = jnp.dot(placed.astype(BF), spread[...], preferred_element_type=F32)
            query[j * 32 : (j + 1) * 32, :] = jnp.where(block, turned, 0.0).astype(BF)
        fresh_key[...] = jnp.concatenate(roped[10:13], axis=1).astype(F32)
        fresh_value[...] = jnp.concatenate(chunks[12:15], axis=1)
        counts = jnp.zeros((32, 128), F32)
        for i in range(8):
            entry = i * 128 + lanes((32, 128))
            live = entry < count_ref[0]
            upper = jnp.broadcast_to(index_rows[i] // 128, (32, 128)) == sublanes((32, 128))
            upper = (upper & live).astype(F32).astype(BF)
            lower = jnp.broadcast_to(index_rows[i] % 128, (128, 128)) == sublanes((128, 128))
            lower = lower.astype(F32).astype(BF)
            counts = counts + lax.dot_general(upper, lower, NT, preferred_element_type=F32)
        over[...] = counts

    @pl.when(step >= 0)
    def _():
        length = length_ref[step]
        queries = query[pl.ds(pl.multiple_of(step * 32, 32), 32), :]
        taken = over[pl.ds(pl.multiple_of(step * 8, 8), 8), :]
        taken = jnp.concatenate([taken[i : i + 1, :] for i in range(8)], axis=1)
        cache_live = (lanes((1, POSITIONS)) < length) & (taken < 0.5)
        index = jnp.concatenate(index_rows, axis=1)
        held_live = (
            (lanes((1, 1024)) < count_ref[0])
            & (index // POSITIONS == step)
            & (index % POSITIONS < length)
        )
        cache_score = lax.dot_general(queries, cache_ref[:, :384], NT, preferred_element_type=F32)
        held_score = lax.dot_general(queries, held_ref[:, :384], NT, preferred_element_type=F32)
        own_score = jnp.sum(
            queries.astype(F32) * fresh_key[pl.ds(step, 1), :], axis=-1, keepdims=True
        )
        cache_live = jnp.broadcast_to(cache_live, cache_score.shape)
        held_live = jnp.broadcast_to(held_live, held_score.shape)
        cache_score = jnp.where(cache_live, cache_score, NEG)
        held_score = jnp.where(held_live, held_score, NEG)
        top = jnp.maximum(
            jnp.maximum(
                jnp.max(cache_score, axis=-1, keepdims=True), jnp.max(held_score, axis=-1, keepdims=True)
            ),
            own_score,
        )
        cache_weight = jnp.where(cache_live, jnp.exp(cache_score - top), 0.0)
        held_weight = jnp.where(held_live, jnp.exp(held_score - top), 0.0)
        own_weight = jnp.exp(own_score - top)
        total = (
            jnp.sum(cache_weight, axis=-1, keepdims=True)
            + jnp.sum(held_weight, axis=-1, keepdims=True)
            + own_weight
        )
        mixed = jnp.dot(cache_weight.astype(BF), cache_ref[:, 256:], preferred_element_type=F32)
        mixed += jnp.dot(held_weight.astype(BF), held_ref[:, 256:], preferred_element_type=F32)
        mixed += own_weight.astype(BF).astype(F32) * fresh_value[pl.ds(step, 1), :]
        group = sublanes((32, 384))
        block = (lanes((32, 384)) // HEAD == group // 4 + 1) & (group < QUERY_HEADS)
        mixed = jnp.where(block, mixed / total, 0.0).astype(BF)
        turned = lax.dot_general(mixed, spread[...], NT, preferred_element_type=F32)
        keep = lanes((32, QW)) // HEAD == sublanes((32, QW))
        result[pl.ds(step, 1), :] = jnp.sum(jnp.where(keep, turned, 0.0), axis=0, keepdims=True)

    @pl.when(step == SLOTS - 1)
    def _():
        wanted = jnp.broadcast_to(slot_ref[...], (8, 256))
        slot = sublanes((8, 256))
        chosen = ((wanted == first_slot + slot) & (slot < SLOTS)).astype(F32).astype(BF)
        good = jnp.where(sublanes((8, QW)) < SLOTS, result[...], 0.0).astype(BF)
        out_ref[...] = lax.dot_general(
            chosen, good, (((0,), (0,)), ((), ())), preferred_element_type=F32
        ).astype(BF)


def decode_attention(
    device, length, count, slots, index, rows, gain, freq, w_qkv, cache, hidden
):
    smem = pl.BlockSpec(memory_space=pltpu.SMEM)
    full = lambda shape: pl.BlockSpec(shape, lambda j: (0,) * len(shape))
    return pl.pallas_call(
        decode_kernel,
        out_shape=jax.ShapeDtypeStruct((256, QW), BF),
        grid=(2 * SLOTS,),
        in_specs=[
            smem,
            smem,
            smem,
            full((1, 256)),
            full((8, 128)),
            full((256, WIDTH)),
            full((1, WIDTH)),
            full((1, 128)),
            pl.BlockSpec(
                (WIDTH, QW + KVW), lambda j: (0, 0), pipeline_mode=pl.Buffered(1)
            ),
            pl.BlockSpec((None, POSITIONS, KVW), lambda j: (jnp.maximum(j - SLOTS, 0), 0, 0)),
            pl.BlockSpec((256, WIDTH), lambda j: (jnp.minimum(j, SLOTS - 1), 0)),
        ],
        out_specs=full((256, QW)),
        scratch_shapes=[
            pltpu.VMEM((1024, KVW), BF),
            pltpu.VMEM((QW, 384), BF),
            pltpu.VMEM((128, 384), BF),
            pltpu.VMEM((8, 384), F32),
            pltpu.VMEM((8, 384), F32),
            pltpu.VMEM((32, 128), F32),
            pltpu.VMEM((8, QW), F32),
        ],
        compiler_params=pltpu.CompilerParams(vmem_limit_bytes=VMEM_LIMIT),
        cost_estimate=cost(17),
        name="decode",
    )(device, length, count, slots, index, rows, gain, freq, w_qkv, cache, hidden)


def attention_kernel(
    rank_ref,
    query_ref,
    own_ref,
    core_ref,
    zed_ref,
    far_ref,
    w_ref,
    hidden_ref,
    gain_ref,
    resid_ref,
    lower_ref,
    upper_ref,
    total,
    mask,
):
    group = pl.program_id(0)

    @pl.when(group == 0)
    def _():
        total[...] = jnp.zeros_like(total)
        rank = rank_ref[0]
        row = sublanes((128, 128))
        col = lanes((128, 128))
        for piece in range(4):
            other = rank ^ piece
            bound = jnp.where(other <= rank, 0, 1)
            mask[:, piece * 128 : (piece + 1) * 128] = jnp.where(col + bound <= row, 0.0, NEG)

    pieces = [own_ref, core_ref, zed_ref, far_ref]
    keys = jnp.concatenate(
        [ref[h * 128 : (h + 1) * 128, :] for h in range(2) for ref in pieces], axis=0
    )
    low = lanes((1024, 128)) < HEAD
    wide = keys.astype(F32)
    values = jnp.where(low, pltpu.roll(wide, 64, 1), wide).astype(BF)
    values = jnp.concatenate([values, jnp.ones((1024, 128), BF)], axis=1)
    low = lanes((128, 128)) < HEAD
    blocked = mask[...]
    mixed = []
    for tile in range(2):
        heads = []
        for pair in range(2):
            two = query_ref[tile * 128 : (tile + 1) * 128, pair * 128 : (pair + 1) * 128].astype(F32)
            heads.append(jnp.where(low, two, 0.0).astype(BF))
            heads.append(jnp.where(low, pltpu.roll(two, 64, 1), 0.0).astype(BF))
        out = []
        for head in heads:
            count = 512 * (tile + 1)
            score = lax.dot_general(head, keys[:count], NT, preferred_element_type=F32)
            if tile == 0:
                score = score + blocked
            else:
                score = jnp.concatenate([score[:, :512], score[:, 512:] + blocked], axis=1)
            top = jnp.max(score, axis=-1, keepdims=True)
            weight = jnp.exp(score - top).astype(BF)
            both = jnp.dot(weight, values[:count], preferred_element_type=F32)
            out.append(both[:, :128] / both[:, 128:])
        mixed.append(
            jnp.concatenate(
                [jnp.where(low, out[0], out[1]), jnp.where(low, out[2], out[3])], axis=1
            ).astype(BF)
        )
    rows = jnp.concatenate(mixed, axis=0)
    total[...] += jnp.dot(rows, w_ref[...], preferred_element_type=F32)

    @pl.when(group == 4)
    def _():
        for part in range(2):
            cut = slice(part * 128, (part + 1) * 128)
            resid = (hidden_ref[cut, :].astype(F32) + total[cut, :]).astype(BF)
            resid_ref[cut, :] = resid
            (lower_ref, upper_ref)[part][:128, :] = norm_rows(resid, gain_ref[...])


def attention(rank, query, own, core, zed, far, w_out, hidden, gain):
    full = lambda shape: pl.BlockSpec(shape, lambda g: (0,) * len(shape))
    side = pl.BlockSpec((ROWS, 128), lambda g: (0, g))
    return pl.pallas_call(
        attention_kernel,
        out_shape=(
            jax.ShapeDtypeStruct((ROWS, WIDTH), BF),
            jax.ShapeDtypeStruct((HALF, WIDTH), BF),
            jax.ShapeDtypeStruct((HALF, WIDTH), BF),
        ),
        grid=(5,),
        in_specs=[
            pl.BlockSpec(memory_space=pltpu.SMEM),
            pl.BlockSpec((ROWS, 256), lambda g: (0, g)),
            side,
            side,
            side,
            side,
            pl.BlockSpec((256, WIDTH), lambda g: (g, 0)),
            full((ROWS, WIDTH)),
            full((1, WIDTH)),
        ],
        out_specs=(
            full((ROWS, WIDTH)),
            full((HALF, WIDTH)),
            full((HALF, WIDTH)),
        ),
        scratch_shapes=[
            pltpu.VMEM((ROWS, WIDTH), F32),
            pltpu.VMEM((128, 512), F32),
        ],
        compiler_params=pltpu.CompilerParams(vmem_limit_bytes=VMEM_LIMIT),
        cost_estimate=cost(12),
        name="attention",
    )(rank, query, own, core, zed, far, w_out, hidden, gain)


def decode_rows_kernel(back_ref, w_ref, decode_ref, gain_ref, lower_in, upper_in, resid_ref, lower_ref, upper_ref):
    del lower_in, upper_in
    source = lanes((32, 256)) % 2
    row = sublanes((32, 256))
    pick = ((row == 0) & (source == 0)) | ((row == 16) & (source == 1))
    pick = pick.astype(F32).astype(BF)
    mixed = jnp.dot(pick, back_ref[...], preferred_element_type=F32).astype(BF)
    projection = jnp.dot(mixed, w_ref[...], preferred_element_type=F32)
    first = sublanes((16, WIDTH)) == 0
    single = decode_ref[...].astype(F32)
    for part in range(2):
        cut = slice(part * 16, (part + 1) * 16)
        alone = jnp.where(first, jnp.broadcast_to(single[part : part + 1], (16, WIDTH)), 0.0)
        resid = (alone + projection[cut]).astype(BF)
        resid_ref[cut, :] = resid
        (lower_ref, upper_ref)[part][...] = norm_rows(resid, gain_ref[...])


def decode_rows(back, w_out, decode, gain, lower, upper):
    full = lambda shape: pl.BlockSpec(shape, lambda g: (0,) * len(shape))
    tail = pl.BlockSpec((16, WIDTH), lambda g: (8, 0))
    return pl.pallas_call(
        decode_rows_kernel,
        out_shape=(
            jax.ShapeDtypeStruct((32, WIDTH), BF),
            jax.ShapeDtypeStruct((HALF, WIDTH), BF),
            jax.ShapeDtypeStruct((HALF, WIDTH), BF),
        ),
        grid=(1,),
        in_specs=[
            full((256, WIDTH)),
            full((WIDTH, WIDTH)),
            full((2, WIDTH)),
            full((1, WIDTH)),
            tail,
            tail,
        ],
        out_specs=(full((32, WIDTH)), tail, tail),
        input_output_aliases={4: 1, 5: 2},
        compiler_params=pltpu.CompilerParams(vmem_limit_bytes=VMEM_LIMIT),
        cost_estimate=cost(3),
        name="decode_rows",
    )(back, w_out, decode, gain, lower, upper)


def feed_kernel(*refs):
    pieces, lows, highs, outs, act = refs[:2], refs[2:10], refs[10:18], refs[18:20], refs[20]
    cut = 2 * SHARE - PART
    rows = jnp.concatenate([ref[...] for ref in pieces], axis=0)
    for k in range(8):
        gate_rows = lows[k][:SHARE, :]
        up_rows = jnp.concatenate([lows[k][SHARE:, :], highs[k][:cut, :]], axis=0)
        gate = lax.dot_general(rows, gate_rows, NT, preferred_element_type=F32)
        up = lax.dot_general(rows, up_rows, NT, preferred_element_type=F32)
        act[:, k * SHARE : (k + 1) * SHARE] = (gate / (1.0 + jnp.exp(-gate)) * up).astype(BF)
    down = jnp.concatenate([ref[cut:, :] for ref in highs], axis=0)
    down = jnp.dot(act[...], down, preferred_element_type=F32)
    outs[0][...] = down[:HALF].astype(BF)
    outs[1][...] = down[HALF:].astype(BF)


def feed_forward(pieces, lows, highs, name):
    vmem = pl.BlockSpec(memory_space=pltpu.VMEM)
    return pl.pallas_call(
        feed_kernel,
        out_shape=(jax.ShapeDtypeStruct((HALF, WIDTH), BF),) * 2,
        in_specs=[vmem] * 18,
        out_specs=(vmem,) * 2,
        scratch_shapes=[pltpu.VMEM((2 * HALF, 8 * SHARE), BF)],
        compiler_params=pltpu.CompilerParams(vmem_limit_bytes=VMEM_LIMIT),
        cost_estimate=cost(8),
        name=name,
    )(*pieces, *lows, *highs)


def start_kernel(resid_ref, extra_ref, lower_ref, upper_ref, out_ref):
    for part in range(2):
        mine_ref = (lower_ref, upper_ref)[part]
        cut = slice(part * HALF, part * HALF + 128)
        out_ref[cut, :] = resid_ref[part * 128 : (part + 1) * 128, :].astype(F32) + mine_ref[
            :128, :
        ].astype(F32)
        cut = slice(part * HALF + 128, (part + 1) * HALF)
        out_ref[cut, :] = extra_ref[part * 16 : (part + 1) * 16, :].astype(F32) + mine_ref[
            128:, :
        ].astype(F32)


def start_sum(resid, extra, mine):
    return pl.pallas_call(
        start_kernel,
        out_shape=jax.ShapeDtypeStruct((2 * HALF, WIDTH), F32),
        in_specs=[pl.BlockSpec(memory_space=pltpu.VMEM)] * 4,
        out_specs=pl.BlockSpec(memory_space=pltpu.VMEM),
        compiler_params=pltpu.CompilerParams(vmem_limit_bytes=VMEM_LIMIT),
        cost_estimate=cost(1.5),
        name="start_sum",
    )(resid, extra, *mine)


def final_kernel(start_ref, first_ref, second_ref, prefill_ref, decode_ref):
    decode = []
    for part, ref in ((0, first_ref), (1, second_ref)):
        whole = start_ref[part * HALF : (part + 1) * HALF, :] + ref[...].astype(F32)
        prefill_ref[part * 128 : (part + 1) * 128, :] = whole[:128].astype(BF)
        decode.append(whole[128:129])
    decode_ref[...] = jnp.concatenate(decode, axis=0).astype(BF)


def final_sum(start, first, second):
    return pl.pallas_call(
        final_kernel,
        out_shape=(
            jax.ShapeDtypeStruct((ROWS, WIDTH), BF),
            jax.ShapeDtypeStruct((2, WIDTH), BF),
        ),
        in_specs=[pl.BlockSpec(memory_space=pltpu.VMEM)] * 3,
        compiler_params=pltpu.CompilerParams(vmem_limit_bytes=VMEM_LIMIT),
        cost_estimate=cost(1.5),
        name="final",
    )(start, first, second)


def body(
    prefill_hidden,
    decode_hidden,
    attn_gain,
    w_qkv,
    w_out,
    ffn_gain,
    w_gate_up,
    w_down,
    key_value_cache,
    cache_len,
    slot_of_request,
    held_hidden,
    recomputed_index,
    recomp_count,
):
    device = lax.axis_index("req").astype(jnp.int32).reshape(1)
    rank = device % 4
    gain = attn_gain.reshape(1, WIDTH)
    gain2 = ffn_gain.reshape(1, WIDTH)
    exponent = np.arange(HEAD // 2) * (2.0 / HEAD)
    freq = jnp.asarray(np.tile(THETA**-exponent, 4).reshape(1, 128), F32)
    index = recomputed_index.reshape(8, 128)

    w_qkv, w_out, key_value_cache, held_hidden, prefill_hidden = in_hbm(
        w_qkv, w_out, key_value_cache, held_hidden, prefill_hidden
    )
    total = 2 * SIDE**3
    spread = jnp.broadcast_to(decode_hidden[None], (total, 2, WIDTH))
    every_row = lax.all_to_all(spread, "req", 0, 0).reshape(256, WIDTH)

    low, high = pack_weights(jnp.swapaxes(w_gate_up, 1, 2), w_down)
    (kv,) = in_hbm(project(rank, prefill_hidden, gain, freq, w_qkv, True))
    zed = send(kv, pair_z)
    core = send(kv, other_core)
    low, high, kv = lax.optimization_barrier((low, high, kv))
    below_low = send(low, next_z)
    above_high = send(high, last_z)
    below_high = send(high, next_z)
    above_low = send(low, last_z)
    low_core = send(low, other_core)
    high_core = send(high, other_core)
    (query,) = in_hbm(project(rank, prefill_hidden, gain, freq, w_qkv, False))
    outgoing = decode_attention(
        device,
        cache_len,
        recomp_count,
        slot_of_request.reshape(1, 256),
        index,
        every_row,
        gain,
        freq,
        w_qkv,
        key_value_cache,
        held_hidden,
    )
    outgoing, zed, core, below_low, above_high, low_core, high_core = lax.optimization_barrier(
        (outgoing, zed, core, below_low, above_high, low_core, high_core)
    )
    far = send(zed, other_core)
    core, zed, far = in_hbm(core, zed, far)
    far_low = send(below_low, next_z)
    far_high = send(above_high, last_z)
    below_low_core = send(below_low, other_core)
    above_high_core = send(above_high, other_core)
    back = lax.all_to_all(outgoing.reshape(total, 2, WIDTH), "req", 0, 0).reshape(256, WIDTH)

    resid, lower, upper = attention(
        rank, query, kv, core, zed, far, w_out, prefill_hidden, gain2
    )
    (resid,) = in_hbm(resid)
    lower, upper, back, below_high, above_low = lax.optimization_barrier(
        (lower, upper, back, below_high, above_low)
    )
    below_high_core = send(below_high, other_core)
    above_low_core = send(above_low, other_core)
    extra, lower, upper = decode_rows(back, w_out, decode_hidden, gain2, lower, upper)
    lower, upper, far_low, far_high = lax.optimization_barrier((lower, upper, far_low, far_high))
    far_low_core = send(far_low, other_core)
    far_high_core = send(far_high, other_core)
    from_last = send(lower, next_x)
    from_next = send(upper, last_x)
    lows = (low, low_core, below_low, below_low_core)
    lows += (above_low, above_low_core, far_low, far_low_core)
    highs = (high, high_core, below_high, below_high_core)
    highs += (above_high, above_high_core, far_high, far_high_core)
    mine = feed_forward((lower, upper), lows, highs, "feed_own")
    from_last, from_next, mine = lax.optimization_barrier((from_last, from_next, mine))
    guest = feed_forward((from_last, from_next), lows, highs, "feed_guest")
    first = send(guest[0], last_x)
    second = send(guest[1], next_x)
    start = start_sum(resid, extra, mine)
    return final_sum(start, first, second)


def solution(mesh):
    return jax.shard_map(
        body,
        mesh=mesh,
        in_specs=(
            P("req", None),
            P("req", None),
            P(),
            P(),
            P(),
            P(),
            P("req", None, None),
            P("req", None, None),
            P("req", None, None),
            P("req"),
            P(),
            P("req", None),
            P("req"),
            P("req"),
        ),
        out_specs=(P("req", None), P("req", None)),
        check_vma=False,
    )
```

```python
import functools

import jax
import jax.numpy as jnp
import numpy as np
from jax import lax
from jax.experimental import pallas as pl
from jax.experimental.pallas import tpu as pltpu
from jax.sharding import PartitionSpec as P

WIDTH = 1280
QUERY_HEADS = 20
HEAD = 64
QW = 1280
KVW = 640
SHARE = 224
PART = 3 * SHARE // 2
GROUP = 16
SIDE = 4
SLOTS = 4
POSITIONS = 1024
ROWS = 256
EPS = 1e-05
THETA = 10000.0
NEG = -1e30
F32 = jnp.float32
BF = jnp.bfloat16
NT = (((1,), (1,)), ((), ()))
VMEM_LIMIT = 24 << 20


def cost(microseconds):
    return pl.CostEstimate(
        flops=int(microseconds * 10**9), transcendentals=0, bytes_accessed=int(microseconds * 3000000)
    )


def place(y, x, z, core):
    return (((y % SIDE) * SIDE + x % SIDE) * SIDE + z % SIDE) * 2 + core


def moves(step):
    pairs = []
    for y in range(SIDE):
        for x in range(SIDE):
            for z in range(SIDE):
                for core in range(2):
                    pairs.append((place(y, x, z, core), place(*step(y, x, z, core))))
    return pairs


def send(array, step):
    return lax.ppermute(array, "req", moves(step))


def in_hbm(*arrays):
    return [pltpu.with_memory_space_constraint(a, pltpu.MemorySpace.HBM) for a in arrays]


def other_core(y, x, z, core):
    return y, x, z, 1 - core


def next_x(y, x, z, core):
    return y, x + 1, z, core


def last_x(y, x, z, core):
    return y, x - 1, z, core


def next_z(y, x, z, core):
    return y, x, z + 1, core


def last_z(y, x, z, core):
    return y, x, z - 1, core


def pair_z(y, x, z, core):
    return y, x, z ^ 1, core


def norm_rows(rows, gain):
    rows = rows.astype(F32)
    mean = jnp.mean(rows * rows, axis=-1, keepdims=True)
    return (rows * lax.rsqrt(mean + EPS) * gain.reshape(1, WIDTH)).astype(BF)


def lanes(shape):
    return lax.broadcasted_iota(jnp.int32, shape, len(shape) - 1)


def sublanes(shape):
    return lax.broadcasted_iota(jnp.int32, shape, len(shape) - 2)


def sine_cosine(angle):
    turns = jnp.floor(angle * (2.0 / np.pi) + 0.5)
    rest = angle - turns * 1.5703125
    rest = rest - turns * 4.837512969970703125e-4
    rest = rest - turns * 7.54978995489188216e-8
    square = rest * rest
    sine = 8.3321608736e-3 + square * -1.9515295891e-4
    sine = rest + rest * square * (-1.6666654611e-1 + square * sine)
    cosine = -1.388731625493765e-3 + square * 2.443315711809948e-5
    cosine = 4.166664568298827e-2 + square * cosine
    cosine = 1.0 - 0.5 * square + square * square * cosine
    quarter = turns.astype(jnp.int32) & 3
    odd = (quarter & 1) == 1
    out_sine = jnp.where(odd, cosine, sine)
    out_cosine = jnp.where(odd, sine, cosine)
    out_sine = jnp.where(quarter >= 2, -out_sine, out_sine)
    out_cosine = jnp.where((quarter == 1) | (quarter == 2), -out_cosine, out_cosine)
    return out_sine, out_cosine


def rope_tables(position):
    pair = (lanes((1, position.shape[1])) % (HEAD // 2)).astype(F32)
    frequency = jnp.exp(pair * (-2.0 * np.log(THETA) / HEAD))
    sine, cosine = sine_cosine(position * frequency)
    low = lanes(sine.shape) % HEAD < HEAD // 2
    return cosine, jnp.where(low, -sine, sine)


def rope(chunk, cosine, sine):
    low = lanes(chunk.shape) % HEAD < HEAD // 2
    other = jnp.where(low, pltpu.roll(chunk, 96, 1), pltpu.roll(chunk, 32, 1))
    return chunk * cosine + other * sine


def pack_kernel(gate_up_ref, down_ref, low_ref, high_ref):
    low_ref[...] = gate_up_ref[:PART, :]
    high_ref[: 2 * SHARE - PART, :] = gate_up_ref[PART:, :]
    high_ref[2 * SHARE - PART :, :] = down_ref[...]


def pack_weights(gate_up, down):
    half = jax.ShapeDtypeStruct((PART, WIDTH), BF)
    block = pl.BlockSpec((PART, WIDTH // 2), lambda i: (0, i))
    return pl.pallas_call(
        pack_kernel,
        out_shape=(half, half),
        grid=(2,),
        in_specs=[
            pl.BlockSpec((None, 2 * SHARE, WIDTH // 2), lambda i: (0, 0, i)),
            pl.BlockSpec((None, SHARE, WIDTH // 2), lambda i: (0, 0, i)),
        ],
        out_specs=(block, block),
        compiler_params=pltpu.CompilerParams(vmem_limit_bytes=VMEM_LIMIT),
        cost_estimate=cost(1.5),
        name="pack",
    )(gate_up, down)


def kv_kernel(rank_ref, hidden_ref, gain_ref, w_ref, kv_ref):
    normed = norm_rows(hidden_ref[...], gain_ref[...])
    position = (sublanes((ROWS, 128)) * 4 + rank_ref[0]).astype(F32)
    cosine, sine = rope_tables(position)
    projected = jnp.dot(normed, w_ref[...], preferred_element_type=F32)
    chunks = [projected[:, i * 128 : (i + 1) * 128] for i in range(5)]
    low = lanes((ROWS, 128)) < HEAD
    first = rope(chunks[0], cosine, sine)
    second = rope(chunks[1], cosine, sine)
    third = jnp.where(low, rope(chunks[2], cosine, sine), chunks[2])
    swap = lambda value: pltpu.roll(value, 64, 1)
    out = [
        jnp.where(low, first, third),
        jnp.where(low, swap(first), swap(chunks[3])),
        jnp.where(low, second, chunks[3]),
        jnp.where(low, swap(second), swap(chunks[4])),
        jnp.where(low, third, chunks[4]),
    ]
    for i in range(5):
        kv_ref[:, i * 128 : (i + 1) * 128] = out[i].astype(BF)


def query_kernel(rank_ref, hidden_ref, gain_ref, w_ref, query_ref, normed, cos, sin):
    @pl.when(pl.program_id(0) == 0)
    def _():
        normed[...] = norm_rows(hidden_ref[...], gain_ref[...])
        position = (sublanes((ROWS, 128)) * 4 + rank_ref[0]).astype(F32)
        cos[...], sin[...] = rope_tables(position)

    projected = jnp.dot(normed[...], w_ref[...], preferred_element_type=F32)
    for i in range(5):
        roped = rope(projected[:, i * 128 : (i + 1) * 128], cos[...], sin[...]).astype(BF)
        query_ref[:, i * 128 : (i + 1) * 128] = roped * jnp.asarray(0.125, BF)


def project(rank, hidden, gain, w_qkv, keys):
    steps = 1 if keys else 2
    scratch = [
        pltpu.VMEM((ROWS, WIDTH), BF),
        pltpu.VMEM((ROWS, 128), F32),
        pltpu.VMEM((ROWS, 128), F32),
    ]
    return pl.pallas_call(
        kv_kernel if keys else query_kernel,
        out_shape=jax.ShapeDtypeStruct((ROWS, KVW * steps), BF),
        grid=(steps,),
        in_specs=[
            pl.BlockSpec(memory_space=pltpu.SMEM),
            pl.BlockSpec((ROWS, WIDTH), lambda j: (0, 0)),
            pl.BlockSpec((WIDTH,), lambda j: (0,)),
            pl.BlockSpec((WIDTH, KVW), (lambda j: (0, 2)) if keys else (lambda j: (0, j))),
        ],
        out_specs=pl.BlockSpec((ROWS, KVW), lambda j: (0, j)),
        scratch_shapes=[] if keys else scratch,
        compiler_params=pltpu.CompilerParams(vmem_limit_bytes=VMEM_LIMIT),
        cost_estimate=cost(0.1),
        name="prefill_kv" if keys else "prefill_query",
    )(rank, hidden, gain, w_qkv)


def column(row):
    return jnp.broadcast_to(row, (128, 128)).T


def decode_kernel(
    device_ref,
    length_ref,
    count_ref,
    slot_ref,
    index_ref,
    rows_ref,
    gain_ref,
    w_ref,
    cache_ref,
    hidden_ref,
    out_ref,
    held_ref,
    spread,
    query,
    fresh_key,
    fresh_value,
    over,
    result,
):
    tick = pl.program_id(0)
    step = tick - SLOTS
    first_slot = device_ref[0] * SLOTS

    @pl.when(tick < SLOTS)
    def _():
        normed = norm_rows(hidden_ref[...], gain_ref[...])
        projected = jnp.dot(normed, w_ref[:, QW:], preferred_element_type=F32)
        position = (index_ref[pl.ds(tick * 2, 2), :] % POSITIONS).astype(F32)
        position = jnp.concatenate([column(position[0:1]), column(position[1:2])], axis=0)
        cosine, sine = rope_tables(position)
        low = lanes((256, 128)) < HEAD
        rows = pl.ds(pl.multiple_of(tick * 256, 256), 256)
        for i in range(5):
            chunk = projected[:, i * 128 : (i + 1) * 128]
            if i < 2:
                chunk = rope(chunk, cosine, sine)
            elif i == 2:
                chunk = jnp.where(low, rope(chunk, cosine, sine), chunk)
            held_ref[rows, i * 128 : (i + 1) * 128] = chunk.astype(BF)

    index_rows = [index_ref[i : i + 1, :] for i in range(8)]

    @pl.when(step == 0)
    def _():
        spread[...] = (
            sublanes((QW, 384)) % HEAD == lanes((QW, 384)) % HEAD
        ).astype(F32).astype(BF)
        wanted = jnp.broadcast_to(slot_ref[...], (8, 256))
        slot = sublanes((8, 256))
        chosen = ((wanted == first_slot + slot) & (slot < SLOTS)).astype(F32).astype(BF)
        rows = jnp.dot(chosen, rows_ref[...], preferred_element_type=F32)
        normed = norm_rows(rows, gain_ref[...])
        projected = jnp.dot(normed, w_ref[...], preferred_element_type=F32)
        projected = projected.astype(BF).astype(F32)
        row = sublanes((8, 128))
        position = jnp.zeros((8, 128), F32)
        for j in range(SLOTS):
            position = jnp.where(row == j, length_ref[j].astype(F32), position)
        cosine, sine = rope_tables(position)
        chunks = [projected[:, i * 128 : (i + 1) * 128] for i in range(15)]
        roped = [rope(chunks[i], cosine, sine).astype(BF) for i in range(13)]
        whole = jnp.concatenate(roped[:10], axis=1).astype(F32) * 0.125
        head_of = sublanes((32, QW))
        keep = lanes((32, QW)) // HEAD == head_of
        group = sublanes((32, 384))
        block = (lanes((32, 384)) // HEAD == group // 4) & (group < QUERY_HEADS)
        for j in range(SLOTS):
            placed = jnp.where(keep, jnp.broadcast_to(whole[j : j + 1], (32, QW)), 0.0)
            turned = jnp.dot(placed.astype(BF), spread[...], preferred_element_type=F32)
            query[j * 32 : (j + 1) * 32, :] = jnp.where(block, turned, 0.0).astype(BF)
        fresh_key[...] = jnp.concatenate(roped[10:13], axis=1).astype(F32)
        fresh_value[...] = jnp.concatenate(chunks[12:15], axis=1)
        counts = jnp.zeros((32, 128), F32)
        for i in range(8):
            entry = i * 128 + lanes((32, 128))
            live = entry < count_ref[0]
            upper = jnp.broadcast_to(index_rows[i] // 128, (32, 128)) == sublanes((32, 128))
            upper = (upper & live).astype(F32).astype(BF)
            lower = jnp.broadcast_to(index_rows[i] % 128, (128, 128)) == sublanes((128, 128))
            lower = lower.astype(F32).astype(BF)
            counts = counts + lax.dot_general(upper, lower, NT, preferred_element_type=F32)
        over[...] = counts

    @pl.when(step >= 0)
    def _():
        length = length_ref[step]
        queries = query[pl.ds(pl.multiple_of(step * 32, 32), 32), :]
        taken = over[pl.ds(pl.multiple_of(step * 8, 8), 8), :]
        taken = jnp.concatenate([taken[i : i + 1, :] for i in range(8)], axis=1)
        cache_live = (lanes((1, POSITIONS)) < length) & (taken < 0.5)
        index = jnp.concatenate(index_rows, axis=1)
        held_live = (
            (lanes((1, 1024)) < count_ref[0])
            & (index // POSITIONS == step)
            & (index % POSITIONS < length)
        )
        cache_score = lax.dot_general(queries, cache_ref[:, :384], NT, preferred_element_type=F32)
        held_score = lax.dot_general(queries, held_ref[:, :384], NT, preferred_element_type=F32)
        own_score = jnp.sum(
            queries.astype(F32) * fresh_key[pl.ds(step, 1), :], axis=-1, keepdims=True
        )
        cache_live = jnp.broadcast_to(cache_live, cache_score.shape)
        held_live = jnp.broadcast_to(held_live, held_score.shape)
        cache_score = jnp.where(cache_live, cache_score, NEG)
        held_score = jnp.where(held_live, held_score, NEG)
        top = jnp.maximum(
            jnp.maximum(
                jnp.max(cache_score, axis=-1, keepdims=True), jnp.max(held_score, axis=-1, keepdims=True)
            ),
            own_score,
        )
        cache_weight = jnp.where(cache_live, jnp.exp(cache_score - top), 0.0)
        held_weight = jnp.where(held_live, jnp.exp(held_score - top), 0.0)
        own_weight = jnp.exp(own_score - top)
        total = (
            jnp.sum(cache_weight, axis=-1, keepdims=True)
            + jnp.sum(held_weight, axis=-1, keepdims=True)
            + own_weight
        )
        mixed = jnp.dot(cache_weight.astype(BF), cache_ref[:, 256:], preferred_element_type=F32)
        mixed += jnp.dot(held_weight.astype(BF), held_ref[:, 256:], preferred_element_type=F32)
        mixed += own_weight.astype(BF).astype(F32) * fresh_value[pl.ds(step, 1), :]
        group = sublanes((32, 384))
        block = (lanes((32, 384)) // HEAD == group // 4 + 1) & (group < QUERY_HEADS)
        mixed = jnp.where(block, mixed / total, 0.0).astype(BF)
        turned = lax.dot_general(mixed, spread[...], NT, preferred_element_type=F32)
        keep = lanes((32, QW)) // HEAD == sublanes((32, QW))
        result[pl.ds(step, 1), :] = jnp.sum(jnp.where(keep, turned, 0.0), axis=0, keepdims=True)

    @pl.when(step == SLOTS - 1)
    def _():
        wanted = jnp.broadcast_to(slot_ref[...], (8, 256))
        slot = sublanes((8, 256))
        chosen = ((wanted == first_slot + slot) & (slot < SLOTS)).astype(F32).astype(BF)
        good = jnp.where(sublanes((8, QW)) < SLOTS, result[...], 0.0).astype(BF)
        out_ref[...] = lax.dot_general(
            chosen, good, (((0,), (0,)), ((), ())), preferred_element_type=F32
        ).astype(BF)


def decode_attention(
    device, length, count, slots, index, rows, gain, w_qkv, cache, hidden
):
    smem = pl.BlockSpec(memory_space=pltpu.SMEM)
    full = lambda shape: pl.BlockSpec(shape, lambda j: (0,) * len(shape))
    return pl.pallas_call(
        decode_kernel,
        out_shape=jax.ShapeDtypeStruct((256, QW), BF),
        grid=(2 * SLOTS,),
        in_specs=[
            smem,
            smem,
            smem,
            full((1, 256)),
            full((8, 128)),
            full((256, WIDTH)),
            full((WIDTH,)),
            pl.BlockSpec(
                (WIDTH, QW + KVW), lambda j: (0, 0), pipeline_mode=pl.Buffered(1)
            ),
            pl.BlockSpec((None, POSITIONS, KVW), lambda j: (jnp.maximum(j - SLOTS, 0), 0, 0)),
            pl.BlockSpec((256, WIDTH), lambda j: (jnp.minimum(j, SLOTS - 1), 0)),
        ],
        out_specs=full((256, QW)),
        scratch_shapes=[
            pltpu.VMEM((1024, KVW), BF),
            pltpu.VMEM((QW, 384), BF),
            pltpu.VMEM((128, 384), BF),
            pltpu.VMEM((8, 384), F32),
            pltpu.VMEM((8, 384), F32),
            pltpu.VMEM((32, 128), F32),
            pltpu.VMEM((8, QW), F32),
        ],
        compiler_params=pltpu.CompilerParams(vmem_limit_bytes=VMEM_LIMIT),
        cost_estimate=cost(17),
        name="decode",
    )(device, length, count, slots, index, rows, gain, w_qkv, cache, hidden)


def attention_kernel(
    rank_ref,
    query_ref,
    own_ref,
    core_ref,
    zed_ref,
    far_ref,
    w_ref,
    hidden_ref,
    gain_ref,
    resid_ref,
    lower_ref,
    upper_ref,
    total,
    mask,
):
    group = pl.program_id(0)

    @pl.when(group == 0)
    def _():
        total[...] = jnp.zeros_like(total)
        rank = rank_ref[0]
        row = sublanes((128, 128))
        col = lanes((128, 128))
        for piece in range(4):
            other = rank ^ piece
            bound = jnp.where(other <= rank, 0, 1)
            mask[:, piece * 128 : (piece + 1) * 128] = jnp.where(col + bound <= row, 0.0, NEG)

    pieces = [own_ref, core_ref, zed_ref, far_ref]
    keys = jnp.concatenate(
        [ref[h * 128 : (h + 1) * 128, :] for h in range(2) for ref in pieces], axis=0
    )
    low = lanes((1024, 128)) < HEAD
    wide = keys.astype(F32)
    values = jnp.where(low, pltpu.roll(wide, 64, 1), wide).astype(BF)
    values = jnp.concatenate([values, jnp.ones((1024, 128), BF)], axis=1)
    low = lanes((128, 128)) < HEAD
    blocked = mask[...]
    mixed = []
    for tile in range(2):
        heads = []
        for pair in range(2):
            two = query_ref[tile * 128 : (tile + 1) * 128, pair * 128 : (pair + 1) * 128].astype(F32)
            heads.append(jnp.where(low, two, 0.0).astype(BF))
            heads.append(jnp.where(low, pltpu.roll(two, 64, 1), 0.0).astype(BF))
        out = []
        for head in heads:
            count = 512 * (tile + 1)
            score = lax.dot_general(head, keys[:count], NT, preferred_element_type=F32)
            if tile == 0:
                score = score + blocked
            else:
                score = jnp.concatenate([score[:, :512], score[:, 512:] + blocked], axis=1)
            top = jnp.max(score, axis=-1, keepdims=True)
            weight = jnp.exp(score - top).astype(BF)
            both = jnp.dot(weight, values[:count], preferred_element_type=F32)
            out.append(both[:, :128] / both[:, 128:])
        mixed.append(
            jnp.concatenate(
                [jnp.where(low, out[0], out[1]), jnp.where(low, out[2], out[3])], axis=1
            ).astype(BF)
        )
    rows = jnp.concatenate(mixed, axis=0)
    total[...] += jnp.dot(rows, w_ref[...], preferred_element_type=F32)

    @pl.when(group == 4)
    def _():
        for part in range(2):
            cut = slice(part * 128, (part + 1) * 128)
            resid = (hidden_ref[cut, :].astype(F32) + total[cut, :]).astype(BF)
            resid_ref[cut, :] = resid
            (lower_ref, upper_ref)[part][...] = norm_rows(resid, gain_ref[...])


def attention(rank, query, own, core, zed, far, w_out, hidden, gain):
    full = lambda shape: pl.BlockSpec(shape, lambda g: (0,) * len(shape))
    side = pl.BlockSpec((ROWS, 128), lambda g: (0, g))
    return pl.pallas_call(
        attention_kernel,
        out_shape=(
            jax.ShapeDtypeStruct((ROWS, WIDTH), BF),
            jax.ShapeDtypeStruct((ROWS // 2, WIDTH), BF),
            jax.ShapeDtypeStruct((ROWS // 2, WIDTH), BF),
        ),
        grid=(5,),
        in_specs=[
            pl.BlockSpec(memory_space=pltpu.SMEM),
            pl.BlockSpec((ROWS, 256), lambda g: (0, g)),
            side,
            side,
            side,
            side,
            pl.BlockSpec((256, WIDTH), lambda g: (g, 0)),
            full((ROWS, WIDTH)),
            full((WIDTH,)),
        ],
        out_specs=(
            full((ROWS, WIDTH)),
            full((ROWS // 2, WIDTH)),
            full((ROWS // 2, WIDTH)),
        ),
        scratch_shapes=[
            pltpu.VMEM((ROWS, WIDTH), F32),
            pltpu.VMEM((128, 512), F32),
        ],
        compiler_params=pltpu.CompilerParams(vmem_limit_bytes=VMEM_LIMIT),
        cost_estimate=cost(0.1),
        name="attention",
    )(rank, query, own, core, zed, far, w_out, hidden, gain)


def decode_rows_kernel(back_ref, w_ref, decode_ref, gain_ref, resid_ref, normed_ref):
    mixed = jnp.sum(back_ref[...].astype(F32), axis=0)
    mixed = jnp.concatenate([mixed, jnp.zeros((14, WIDTH), F32)], axis=0).astype(BF)
    single = decode_ref[...].astype(F32)
    hidden = jnp.concatenate([single, jnp.zeros((14, WIDTH), F32)], axis=0)
    resid = (hidden + jnp.dot(mixed, w_ref[...], preferred_element_type=F32)).astype(BF)
    resid_ref[...] = resid
    normed_ref[...] = norm_rows(resid, gain_ref[...])


def decode_rows(back, w_out, decode, gain):
    vmem = pl.BlockSpec(memory_space=pltpu.VMEM)
    return pl.pallas_call(
        decode_rows_kernel,
        out_shape=(jax.ShapeDtypeStruct((16, WIDTH), BF),) * 2,
        in_specs=[vmem] * 4,
        out_specs=(vmem,) * 2,
        compiler_params=pltpu.CompilerParams(vmem_limit_bytes=VMEM_LIMIT),
        cost_estimate=cost(3),
        name="decode_rows",
    )(back, w_out, decode, gain)


def hidden_units(rows, lows, highs, act):
    cut = 2 * SHARE - PART
    for k in range(len(lows)):
        gate_rows = lows[k][:SHARE, :]
        up_rows = jnp.concatenate([lows[k][SHARE:, :], highs[k][:cut, :]], axis=0)
        gate = lax.dot_general(rows, gate_rows, NT, preferred_element_type=F32)
        up = lax.dot_general(rows, up_rows, NT, preferred_element_type=F32)
        act[:, k * SHARE : (k + 1) * SHARE] = (gate / (1.0 + jnp.exp(-gate)) * up).astype(BF)
    down = jnp.concatenate([ref[cut:, :] for ref in highs], axis=0)
    return jnp.dot(act[...], down, preferred_element_type=F32)


def first_kernel(*refs):
    rows = jnp.concatenate([refs[0][...], refs[1][...]], axis=0)
    refs[6][...] = hidden_units(rows, refs[2:4], refs[4:6], refs[7])


def second_kernel(*refs):
    rows = jnp.concatenate([refs[0][...], refs[1][...]], axis=0)
    down = hidden_units(rows, refs[2:8], refs[8:14], refs[17])
    refs[16][...] = refs[15][...].astype(F32) + (refs[14][...] + down)


def guest_kernel(*refs):
    rows = jnp.concatenate([ref[...] for ref in refs[:4]], axis=0)
    down = hidden_units(rows, refs[4:12], refs[12:20], refs[23]).astype(BF)
    for ref, start, stop in zip(refs[20:23], (0, 144, 272), (144, 272, 288)):
        ref[...] = down[start:stop]


def feed_forward(kernel, inputs, outputs, rows, shares, time, name):
    vmem = pl.BlockSpec(memory_space=pltpu.VMEM)
    return pl.pallas_call(
        kernel,
        out_shape=outputs,
        in_specs=[vmem] * len(inputs),
        out_specs=(vmem,) * len(outputs),
        scratch_shapes=[pltpu.VMEM((rows, shares * SHARE), BF)],
        compiler_params=pltpu.CompilerParams(vmem_limit_bytes=VMEM_LIMIT),
        cost_estimate=cost(time),
        name=name,
    )(*inputs)


def final_kernel(start_ref, extra_ref, mine_ref, first_ref, second_ref, prefill_ref, decode_ref):
    for part, ref in ((0, first_ref), (1, second_ref)):
        cut = slice(part * 128, (part + 1) * 128)
        prefill_ref[cut, :] = (start_ref[cut, :] + ref[:128, :].astype(F32)).astype(BF)
    alone = mine_ref[...].astype(F32) + first_ref[128:, :].astype(F32)
    decode_ref[...] = (extra_ref[...].astype(F32) + alone)[:2].astype(BF)


def final_sum(start, extra, mine, first, second):
    return pl.pallas_call(
        final_kernel,
        out_shape=(
            jax.ShapeDtypeStruct((ROWS, WIDTH), BF),
            jax.ShapeDtypeStruct((2, WIDTH), BF),
        ),
        in_specs=[pl.BlockSpec(memory_space=pltpu.VMEM)] * 5,
        compiler_params=pltpu.CompilerParams(vmem_limit_bytes=VMEM_LIMIT),
        cost_estimate=cost(1),
        name="final",
    )(start, extra, mine, first, second)


def body(
    prefill_hidden,
    decode_hidden,
    attn_gain,
    w_qkv,
    w_out,
    ffn_gain,
    w_gate_up,
    w_down,
    key_value_cache,
    cache_len,
    slot_of_request,
    held_hidden,
    recomputed_index,
    recomp_count,
):
    device = lax.axis_index("req").astype(jnp.int32).reshape(1)
    rank = device % 4
    gain, gain2 = attn_gain, ffn_gain
    index = recomputed_index.reshape(8, 128)

    w_all = w_out
    w_qkv, w_out, key_value_cache, held_hidden, prefill_hidden = in_hbm(
        w_qkv, w_out, key_value_cache, held_hidden, prefill_hidden
    )
    total = 2 * SIDE**3
    spread = jnp.broadcast_to(decode_hidden[None], (total, 2, WIDTH))
    every_row = lax.all_to_all(spread, "req", 0, 0).reshape(256, WIDTH)

    low, high = pack_weights(jnp.swapaxes(w_gate_up, 1, 2), w_down)
    (kv,) = in_hbm(project(rank, prefill_hidden, gain, w_qkv, True))
    zed = send(kv, pair_z)
    core = send(kv, other_core)
    low, high, kv = lax.optimization_barrier((low, high, kv))
    below_low = send(low, next_z)
    above_high = send(high, last_z)
    below_high = send(high, next_z)
    above_low = send(low, last_z)
    low_core = send(low, other_core)
    high_core = send(high, other_core)
    (query,) = in_hbm(project(rank, prefill_hidden, gain, w_qkv, False))
    every_row, query = lax.optimization_barrier((every_row, query))
    outgoing = decode_attention(
        device,
        cache_len,
        recomp_count,
        slot_of_request.reshape(1, 256),
        index,
        every_row,
        gain,
        w_qkv,
        key_value_cache,
        held_hidden,
    )
    outgoing, zed, core, below_low, above_high, low_core, high_core = lax.optimization_barrier(
        (outgoing, zed, core, below_low, above_high, low_core, high_core)
    )
    far = send(zed, other_core)
    core, zed, far = in_hbm(core, zed, far)
    far_low = send(below_low, next_z)
    far_high = send(above_high, last_z)
    below_low_core = send(below_low, other_core)
    above_high_core = send(above_high, other_core)
    back = lax.all_to_all(outgoing.reshape(total, 2, WIDTH), "req", 0, 0)

    resid, lower, upper = attention(
        rank, query, kv, core, zed, far, w_out, prefill_hidden, gain2
    )
    from_last = send(lower, next_x)
    from_next = send(upper, last_x)
    (mine,) = feed_forward(
        first_kernel,
        (lower, upper, low, low_core, high, high_core),
        (jax.ShapeDtypeStruct((ROWS, WIDTH), F32),),
        ROWS,
        2,
        0.1,
        "feed_first",
    )
    mine, back = lax.optimization_barrier((mine, back))
    extra, alone = decode_rows(back, w_all, decode_hidden, gain2)
    alone, far_low, far_high, from_last, from_next, below_high, above_low = (
        lax.optimization_barrier(
            (alone, far_low, far_high, from_last, from_next, below_high, above_low)
        )
    )
    far_low_core = send(far_low, other_core)
    far_high_core = send(far_high, other_core)
    below_high_core = send(below_high, other_core)
    above_low_core = send(above_low, other_core)
    guest = send(alone, next_x)
    lows = (low, low_core)
    highs = (high, high_core)
    lows_far = (below_low, below_low_core, above_low, above_low_core, far_low, far_low_core)
    highs_far = (below_high, below_high_core, above_high, above_high_core, far_high, far_high_core)
    to_last, to_next, alone = feed_forward(
        guest_kernel,
        (from_last, guest, from_next, alone) + lows + lows_far + highs + highs_far,
        tuple(jax.ShapeDtypeStruct((n, WIDTH), BF) for n in (144, 128, 16)),
        ROWS + 32,
        8,
        8,
        "feed_guest",
    )
    to_last, to_next, mine = lax.optimization_barrier((to_last, to_next, mine))
    first = send(to_last, last_x)
    second = send(to_next, next_x)
    (start,) = feed_forward(
        second_kernel,
        (lower, upper) + lows_far + highs_far + (mine, resid),
        (jax.ShapeDtypeStruct((ROWS, WIDTH), F32),),
        ROWS,
        6,
        6,
        "feed_second",
    )
    return final_sum(start, extra, alone, first, second)


def solution(mesh):
    return jax.shard_map(
        body,
        mesh=mesh,
        in_specs=(
            P("req", None),
            P("req", None),
            P(),
            P(),
            P(),
            P(),
            P("req", None, None),
            P("req", None, None),
            P("req", None, None),
            P("req"),
            P(),
            P("req", None),
            P("req"),
            P("req"),
        ),
        out_specs=(P("req", None), P("req", None)),
        check_vma=False,
    )
```

```python
import functools

import jax
import jax.numpy as jnp
import numpy as np
from jax import lax
from jax.experimental import pallas as pl
from jax.experimental.pallas import tpu as pltpu
from jax.sharding import PartitionSpec as P

WIDTH = 1280
QUERY_HEADS = 20
HEAD = 64
QW = 1280
KVW = 640
SHARE = 224
PART = 3 * SHARE // 2
GROUP = 16
SIDE = 4
SLOTS = 4
POSITIONS = 1024
ROWS = 256
EPS = 1e-05
THETA = 10000.0
NEG = -1e30
F32 = jnp.float32
BF = jnp.bfloat16
NT = (((1,), (1,)), ((), ()))
VMEM_LIMIT = 24 << 20


def cost(microseconds):
    return pl.CostEstimate(
        flops=int(microseconds * 10**9), transcendentals=0, bytes_accessed=int(microseconds * 3000000)
    )


def place(y, x, z, core):
    return (((y % SIDE) * SIDE + x % SIDE) * SIDE + z % SIDE) * 2 + core


def moves(step):
    pairs = []
    for y in range(SIDE):
        for x in range(SIDE):
            for z in range(SIDE):
                for core in range(2):
                    pairs.append((place(y, x, z, core), place(*step(y, x, z, core))))
    return pairs


def send(array, step):
    return lax.ppermute(array, "req", moves(step))


def in_hbm(*arrays):
    return [pltpu.with_memory_space_constraint(a, pltpu.MemorySpace.HBM) for a in arrays]


def other_core(y, x, z, core):
    return y, x, z, 1 - core


def next_x(y, x, z, core):
    return y, x + 1, z, core


def last_x(y, x, z, core):
    return y, x - 1, z, core


def next_z(y, x, z, core):
    return y, x, z + 1, core


def last_z(y, x, z, core):
    return y, x, z - 1, core


def pair_z(y, x, z, core):
    return y, x, z ^ 1, core


def norm_rows(rows, gain):
    rows = rows.astype(F32)
    mean = jnp.mean(rows * rows, axis=-1, keepdims=True)
    return (rows * lax.rsqrt(mean + EPS) * gain.reshape(1, WIDTH)).astype(BF)


def lanes(shape):
    return lax.broadcasted_iota(jnp.int32, shape, len(shape) - 1)


def sublanes(shape):
    return lax.broadcasted_iota(jnp.int32, shape, len(shape) - 2)


def sine_cosine(angle):
    turns = jnp.floor(angle * (2.0 / np.pi) + 0.5)
    rest = angle - turns * 1.5703125
    rest = rest - turns * 4.837512969970703125e-4
    rest = rest - turns * 7.54978995489188216e-8
    square = rest * rest
    sine = 8.3321608736e-3 + square * -1.9515295891e-4
    sine = rest + rest * square * (-1.6666654611e-1 + square * sine)
    cosine = -1.388731625493765e-3 + square * 2.443315711809948e-5
    cosine = 4.166664568298827e-2 + square * cosine
    cosine = 1.0 - 0.5 * square + square * square * cosine
    quarter = turns.astype(jnp.int32) & 3
    odd = (quarter & 1) == 1
    out_sine = jnp.where(odd, cosine, sine)
    out_cosine = jnp.where(odd, sine, cosine)
    out_sine = jnp.where(quarter >= 2, -out_sine, out_sine)
    out_cosine = jnp.where((quarter == 1) | (quarter == 2), -out_cosine, out_cosine)
    return out_sine, out_cosine


def rope_tables(position):
    pair = (lanes((1, position.shape[1])) % (HEAD // 2)).astype(F32)
    frequency = jnp.exp(pair * (-2.0 * np.log(THETA) / HEAD))
    sine, cosine = sine_cosine(position * frequency)
    low = lanes(sine.shape) % HEAD < HEAD // 2
    return cosine, jnp.where(low, -sine, sine)


def rope(chunk, cosine, sine):
    low = lanes(chunk.shape) % HEAD < HEAD // 2
    other = jnp.where(low, pltpu.roll(chunk, 96, 1), pltpu.roll(chunk, 32, 1))
    return chunk * cosine + other * sine


def pack_kernel(gate_up_ref, down_ref, low_ref, high_ref):
    low_ref[...] = gate_up_ref[:PART, :]
    high_ref[: 2 * SHARE - PART, :] = gate_up_ref[PART:, :]
    high_ref[2 * SHARE - PART :, :] = down_ref[...]


def pack_weights(gate_up, down):
    half = jax.ShapeDtypeStruct((PART, WIDTH), BF)
    block = pl.BlockSpec((PART, WIDTH // 2), lambda i: (0, i))
    return pl.pallas_call(
        pack_kernel,
        out_shape=(half, half),
        grid=(2,),
        in_specs=[
            pl.BlockSpec((None, 2 * SHARE, WIDTH // 2), lambda i: (0, 0, i)),
            pl.BlockSpec((None, SHARE, WIDTH // 2), lambda i: (0, 0, i)),
        ],
        out_specs=(block, block),
        compiler_params=pltpu.CompilerParams(vmem_limit_bytes=VMEM_LIMIT),
        cost_estimate=cost(1.5),
        name="pack",
    )(gate_up, down)


def kv_kernel(rank_ref, hidden_ref, gain_ref, w_ref, kv_ref):
    normed = norm_rows(hidden_ref[...], gain_ref[...])
    position = (sublanes((ROWS, 128)) * 4 + rank_ref[0]).astype(F32)
    cosine, sine = rope_tables(position)
    projected = jnp.dot(normed, w_ref[...], preferred_element_type=F32)
    chunks = [projected[:, i * 128 : (i + 1) * 128] for i in range(5)]
    low = lanes((ROWS, 128)) < HEAD
    first = rope(chunks[0], cosine, sine)
    second = rope(chunks[1], cosine, sine)
    third = jnp.where(low, rope(chunks[2], cosine, sine), chunks[2])
    swap = lambda value: pltpu.roll(value, 64, 1)
    out = [
        jnp.where(low, first, third),
        jnp.where(low, swap(first), swap(chunks[3])),
        jnp.where(low, second, chunks[3]),
        jnp.where(low, swap(second), swap(chunks[4])),
        jnp.where(low, third, chunks[4]),
    ]
    for i in range(5):
        kv_ref[:, i * 128 : (i + 1) * 128] = out[i].astype(BF)


def query_kernel(rank_ref, hidden_ref, gain_ref, w_ref, query_ref, normed, cos, sin):
    @pl.when(pl.program_id(0) == 0)
    def _():
        normed[...] = norm_rows(hidden_ref[...], gain_ref[...])
        position = (sublanes((ROWS, 128)) * 4 + rank_ref[0]).astype(F32)
        cos[...], sin[...] = rope_tables(position)

    projected = jnp.dot(normed[...], w_ref[...], preferred_element_type=F32)
    for i in range(5):
        roped = rope(projected[:, i * 128 : (i + 1) * 128], cos[...], sin[...]).astype(BF)
        query_ref[:, i * 128 : (i + 1) * 128] = roped * jnp.asarray(0.125, BF)


def project(rank, hidden, gain, w_qkv, keys):
    steps = 1 if keys else 2
    scratch = [
        pltpu.VMEM((ROWS, WIDTH), BF),
        pltpu.VMEM((ROWS, 128), F32),
        pltpu.VMEM((ROWS, 128), F32),
    ]
    return pl.pallas_call(
        kv_kernel if keys else query_kernel,
        out_shape=jax.ShapeDtypeStruct((ROWS, KVW * steps), BF),
        grid=(steps,),
        in_specs=[
            pl.BlockSpec(memory_space=pltpu.SMEM),
            pl.BlockSpec((ROWS, WIDTH), lambda j: (0, 0)),
            pl.BlockSpec((WIDTH,), lambda j: (0,)),
            pl.BlockSpec((WIDTH, KVW), (lambda j: (0, 2)) if keys else (lambda j: (0, j))),
        ],
        out_specs=pl.BlockSpec((ROWS, KVW), lambda j: (0, j)),
        scratch_shapes=[] if keys else scratch,
        compiler_params=pltpu.CompilerParams(vmem_limit_bytes=VMEM_LIMIT),
        cost_estimate=cost(3 if keys else 0.1),
        name="prefill_kv" if keys else "prefill_query",
    )(rank, hidden, gain, w_qkv)


def column(row):
    return jnp.broadcast_to(row, (128, 128)).T


def decode_kernel(
    device_ref,
    length_ref,
    count_ref,
    slot_ref,
    index_ref,
    rows_ref,
    gain_ref,
    w_ref,
    cache_ref,
    hidden_ref,
    out_ref,
    held_ref,
    spread,
    query,
    fresh_key,
    fresh_value,
    over,
    result,
):
    tick = pl.program_id(0)
    step = tick - SLOTS
    first_slot = device_ref[0] * SLOTS

    @pl.when(tick < SLOTS)
    def _():
        normed = norm_rows(hidden_ref[...], gain_ref[...])
        projected = jnp.dot(normed, w_ref[:, QW:], preferred_element_type=F32)
        position = (index_ref[pl.ds(tick * 2, 2), :] % POSITIONS).astype(F32)
        position = jnp.concatenate([column(position[0:1]), column(position[1:2])], axis=0)
        cosine, sine = rope_tables(position)
        low = lanes((256, 128)) < HEAD
        rows = pl.ds(pl.multiple_of(tick * 256, 256), 256)
        for i in range(5):
            chunk = projected[:, i * 128 : (i + 1) * 128]
            if i < 2:
                chunk = rope(chunk, cosine, sine)
            elif i == 2:
                chunk = jnp.where(low, rope(chunk, cosine, sine), chunk)
            held_ref[rows, i * 128 : (i + 1) * 128] = chunk.astype(BF)

    index_rows = [index_ref[i : i + 1, :] for i in range(8)]

    @pl.when(step == 0)
    def _():
        spread[...] = (
            sublanes((QW, 384)) % HEAD == lanes((QW, 384)) % HEAD
        ).astype(F32).astype(BF)
        wanted = jnp.broadcast_to(slot_ref[...], (8, 256))
        slot = sublanes((8, 256))
        chosen = ((wanted == first_slot + slot) & (slot < SLOTS)).astype(F32).astype(BF)
        rows = jnp.dot(chosen, rows_ref[...], preferred_element_type=F32)
        normed = norm_rows(rows, gain_ref[...])
        projected = jnp.dot(normed, w_ref[...], preferred_element_type=F32)
        projected = projected.astype(BF).astype(F32)
        row = sublanes((8, 128))
        position = jnp.zeros((8, 128), F32)
        for j in range(SLOTS):
            position = jnp.where(row == j, length_ref[j].astype(F32), position)
        cosine, sine = rope_tables(position)
        chunks = [projected[:, i * 128 : (i + 1) * 128] for i in range(15)]
        roped = [rope(chunks[i], cosine, sine).astype(BF) for i in range(13)]
        whole = jnp.concatenate(roped[:10], axis=1).astype(F32) * 0.125
        head_of = sublanes((32, QW))
        keep = lanes((32, QW)) // HEAD == head_of
        group = sublanes((32, 384))
        block = (lanes((32, 384)) // HEAD == group // 4) & (group < QUERY_HEADS)
        for j in range(SLOTS):
            placed = jnp.where(keep, jnp.broadcast_to(whole[j : j + 1], (32, QW)), 0.0)
            turned = jnp.dot(placed.astype(BF), spread[...], preferred_element_type=F32)
            query[j * 32 : (j + 1) * 32, :] = jnp.where(block, turned, 0.0).astype(BF)
        fresh_key[...] = jnp.concatenate(roped[10:13], axis=1).astype(F32)
        fresh_value[...] = jnp.concatenate(chunks[12:15], axis=1)
        counts = jnp.zeros((32, 128), F32)
        for i in range(8):
            entry = i * 128 + lanes((32, 128))
            live = entry < count_ref[0]
            upper = jnp.broadcast_to(index_rows[i] // 128, (32, 128)) == sublanes((32, 128))
            upper = (upper & live).astype(F32).astype(BF)
            lower = jnp.broadcast_to(index_rows[i] % 128, (128, 128)) == sublanes((128, 128))
            lower = lower.astype(F32).astype(BF)
            counts = counts + lax.dot_general(upper, lower, NT, preferred_element_type=F32)
        over[...] = counts

    @pl.when(step >= 0)
    def _():
        length = length_ref[step]
        queries = query[pl.ds(pl.multiple_of(step * 32, 32), 32), :]
        taken = over[pl.ds(pl.multiple_of(step * 8, 8), 8), :]
        taken = jnp.concatenate([taken[i : i + 1, :] for i in range(8)], axis=1)
        cache_live = (lanes((1, POSITIONS)) < length) & (taken < 0.5)
        index = jnp.concatenate(index_rows, axis=1)
        held_live = (
            (lanes((1, 1024)) < count_ref[0])
            & (index // POSITIONS == step)
            & (index % POSITIONS < length)
        )
        cache_score = lax.dot_general(queries, cache_ref[:, :384], NT, preferred_element_type=F32)
        held_score = lax.dot_general(queries, held_ref[:, :384], NT, preferred_element_type=F32)
        own_score = jnp.sum(
            queries.astype(F32) * fresh_key[pl.ds(step, 1), :], axis=-1, keepdims=True
        )
        cache_live = jnp.broadcast_to(cache_live, cache_score.shape)
        held_live = jnp.broadcast_to(held_live, held_score.shape)
        cache_score = jnp.where(cache_live, cache_score, NEG)
        held_score = jnp.where(held_live, held_score, NEG)
        top = jnp.maximum(
            jnp.maximum(
                jnp.max(cache_score, axis=-1, keepdims=True), jnp.max(held_score, axis=-1, keepdims=True)
            ),
            own_score,
        )
        cache_weight = jnp.where(cache_live, jnp.exp(cache_score - top), 0.0)
        held_weight = jnp.where(held_live, jnp.exp(held_score - top), 0.0)
        own_weight = jnp.exp(own_score - top)
        total = (
            jnp.sum(cache_weight, axis=-1, keepdims=True)
            + jnp.sum(held_weight, axis=-1, keepdims=True)
            + own_weight
        )
        mixed = jnp.dot(cache_weight.astype(BF), cache_ref[:, 256:], preferred_element_type=F32)
        mixed += jnp.dot(held_weight.astype(BF), held_ref[:, 256:], preferred_element_type=F32)
        mixed += own_weight.astype(BF).astype(F32) * fresh_value[pl.ds(step, 1), :]
        group = sublanes((32, 384))
        block = (lanes((32, 384)) // HEAD == group // 4 + 1) & (group < QUERY_HEADS)
        mixed = jnp.where(block, mixed / total, 0.0).astype(BF)
        turned = lax.dot_general(mixed, spread[...], NT, preferred_element_type=F32)
        keep = lanes((32, QW)) // HEAD == sublanes((32, QW))
        result[pl.ds(step, 1), :] = jnp.sum(jnp.where(keep, turned, 0.0), axis=0, keepdims=True)

    @pl.when(step == SLOTS - 1)
    def _():
        wanted = jnp.broadcast_to(slot_ref[...], (8, 256))
        slot = sublanes((8, 256))
        chosen = ((wanted == first_slot + slot) & (slot < SLOTS)).astype(F32).astype(BF)
        good = jnp.where(sublanes((8, QW)) < SLOTS, result[...], 0.0).astype(BF)
        out_ref[...] = lax.dot_general(
            chosen, good, (((0,), (0,)), ((), ())), preferred_element_type=F32
        ).astype(BF)


def decode_attention(
    device, length, count, slots, index, rows, gain, w_qkv, cache, hidden
):
    smem = pl.BlockSpec(memory_space=pltpu.SMEM)
    full = lambda shape: pl.BlockSpec(shape, lambda j: (0,) * len(shape))
    return pl.pallas_call(
        decode_kernel,
        out_shape=jax.ShapeDtypeStruct((256, QW), BF),
        grid=(2 * SLOTS,),
        in_specs=[
            smem,
            smem,
            smem,
            full((1, 256)),
            full((8, 128)),
            full((256, WIDTH)),
            full((WIDTH,)),
            pl.BlockSpec(
                (WIDTH, QW + KVW), lambda j: (0, 0), pipeline_mode=pl.Buffered(1)
            ),
            pl.BlockSpec((None, POSITIONS, KVW), lambda j: (jnp.maximum(j - SLOTS, 0), 0, 0)),
            pl.BlockSpec((256, WIDTH), lambda j: (jnp.minimum(j, SLOTS - 1), 0)),
        ],
        out_specs=full((256, QW)),
        scratch_shapes=[
            pltpu.VMEM((1024, KVW), BF),
            pltpu.VMEM((QW, 384), BF),
            pltpu.VMEM((128, 384), BF),
            pltpu.VMEM((8, 384), F32),
            pltpu.VMEM((8, 384), F32),
            pltpu.VMEM((32, 128), F32),
            pltpu.VMEM((8, QW), F32),
        ],
        compiler_params=pltpu.CompilerParams(vmem_limit_bytes=VMEM_LIMIT),
        cost_estimate=cost(17),
        name="decode",
    )(device, length, count, slots, index, rows, gain, w_qkv, cache, hidden)


def attention_kernel(
    rank_ref,
    query_ref,
    own_ref,
    core_ref,
    zed_ref,
    far_ref,
    w_ref,
    hidden_ref,
    gain_ref,
    resid_ref,
    lower_ref,
    upper_ref,
    total,
    mask,
):
    group = pl.program_id(0)

    @pl.when(group == 0)
    def _():
        total[...] = jnp.zeros_like(total)
        rank = rank_ref[0]
        row = sublanes((128, 128))
        col = lanes((128, 128))
        for piece in range(4):
            other = rank ^ piece
            bound = jnp.where(other <= rank, 0, 1)
            mask[:, piece * 128 : (piece + 1) * 128] = jnp.where(col + bound <= row, 0.0, NEG)

    pieces = [own_ref, core_ref, zed_ref, far_ref]
    keys = jnp.concatenate(
        [ref[h * 128 : (h + 1) * 128, :] for h in range(2) for ref in pieces], axis=0
    )
    low = lanes((1024, 128)) < HEAD
    wide = keys.astype(F32)
    values = jnp.where(low, pltpu.roll(wide, 64, 1), wide).astype(BF)
    values = jnp.concatenate([values, jnp.ones((1024, 128), BF)], axis=1)
    low = lanes((128, 128)) < HEAD
    blocked = mask[...]
    mixed = []
    for tile in range(2):
        heads = []
        for pair in range(2):
            two = query_ref[tile * 128 : (tile + 1) * 128, pair * 128 : (pair + 1) * 128].astype(F32)
            heads.append(jnp.where(low, two, 0.0).astype(BF))
            heads.append(jnp.where(low, pltpu.roll(two, 64, 1), 0.0).astype(BF))
        out = []
        for head in heads:
            count = 512 * (tile + 1)
            score = lax.dot_general(head, keys[:count], NT, preferred_element_type=F32)
            if tile == 0:
                score = score + blocked
            else:
                score = jnp.concatenate([score[:, :512], score[:, 512:] + blocked], axis=1)
            top = jnp.max(score, axis=-1, keepdims=True)
            weight = jnp.exp(score - top).astype(BF)
            both = jnp.dot(weight, values[:count], preferred_element_type=F32)
            out.append(both[:, :128] / both[:, 128:])
        mixed.append(
            jnp.concatenate(
                [jnp.where(low, out[0], out[1]), jnp.where(low, out[2], out[3])], axis=1
            ).astype(BF)
        )
    rows = jnp.concatenate(mixed, axis=0)
    total[...] += jnp.dot(rows, w_ref[...], preferred_element_type=F32)

    @pl.when(group == 4)
    def _():
        for part in range(2):
            cut = slice(part * 128, (part + 1) * 128)
            resid = (hidden_ref[cut, :].astype(F32) + total[cut, :]).astype(BF)
            resid_ref[cut, :] = resid
            (lower_ref, upper_ref)[part][...] = norm_rows(resid, gain_ref[...])


def attention(rank, query, own, core, zed, far, w_out, hidden, gain):
    full = lambda shape: pl.BlockSpec(shape, lambda g: (0,) * len(shape))
    side = pl.BlockSpec((ROWS, 128), lambda g: (0, g))
    return pl.pallas_call(
        attention_kernel,
        out_shape=(
            jax.ShapeDtypeStruct((ROWS, WIDTH), BF),
            jax.ShapeDtypeStruct((ROWS // 2, WIDTH), BF),
            jax.ShapeDtypeStruct((ROWS // 2, WIDTH), BF),
        ),
        grid=(5,),
        in_specs=[
            pl.BlockSpec(memory_space=pltpu.SMEM),
            pl.BlockSpec((ROWS, 256), lambda g: (0, g)),
            side,
            side,
            side,
            side,
            pl.BlockSpec((256, WIDTH), lambda g: (g, 0)),
            full((ROWS, WIDTH)),
            full((WIDTH,)),
        ],
        out_specs=(
            full((ROWS, WIDTH)),
            full((ROWS // 2, WIDTH)),
            full((ROWS // 2, WIDTH)),
        ),
        scratch_shapes=[
            pltpu.VMEM((ROWS, WIDTH), F32),
            pltpu.VMEM((128, 512), F32),
        ],
        compiler_params=pltpu.CompilerParams(vmem_limit_bytes=VMEM_LIMIT),
        cost_estimate=cost(0.1),
        name="attention",
    )(rank, query, own, core, zed, far, w_out, hidden, gain)


def decode_rows_kernel(back_ref, w_ref, decode_ref, gain_ref, resid_ref, normed_ref):
    mixed = jnp.sum(back_ref[...].astype(F32), axis=0)
    mixed = jnp.concatenate([mixed, jnp.zeros((14, WIDTH), F32)], axis=0).astype(BF)
    single = decode_ref[...].astype(F32)
    hidden = jnp.concatenate([single, jnp.zeros((14, WIDTH), F32)], axis=0)
    resid = (hidden + jnp.dot(mixed, w_ref[...], preferred_element_type=F32)).astype(BF)
    resid_ref[...] = resid
    normed_ref[...] = norm_rows(resid, gain_ref[...])


def decode_rows(back, w_out, decode, gain):
    vmem = pl.BlockSpec(memory_space=pltpu.VMEM)
    return pl.pallas_call(
        decode_rows_kernel,
        out_shape=(jax.ShapeDtypeStruct((16, WIDTH), BF),) * 2,
        in_specs=[vmem] * 4,
        out_specs=(vmem,) * 2,
        compiler_params=pltpu.CompilerParams(vmem_limit_bytes=VMEM_LIMIT),
        cost_estimate=cost(3),
        name="decode_rows",
    )(back, w_out, decode, gain)


def hidden_units(rows, lows, highs, act):
    cut = 2 * SHARE - PART
    for k in range(len(lows)):
        gate_rows = lows[k][:SHARE, :]
        up_rows = jnp.concatenate([lows[k][SHARE:, :], highs[k][:cut, :]], axis=0)
        gate = lax.dot_general(rows, gate_rows, NT, preferred_element_type=F32)
        up = lax.dot_general(rows, up_rows, NT, preferred_element_type=F32)
        act[:, k * SHARE : (k + 1) * SHARE] = (gate / (1.0 + jnp.exp(-gate)) * up).astype(BF)
    down = jnp.concatenate([ref[cut:, :] for ref in highs], axis=0)
    return jnp.dot(act[...], down, preferred_element_type=F32)


def first_kernel(*refs):
    rows = jnp.concatenate([refs[0][...], refs[1][...]], axis=0)
    refs[6][...] = hidden_units(rows, refs[2:4], refs[4:6], refs[7])


def second_kernel(*refs):
    rows = jnp.concatenate([refs[0][...], refs[1][...]], axis=0)
    down = hidden_units(rows, refs[2:8], refs[8:14], refs[17])
    refs[16][...] = refs[15][...].astype(F32) + (refs[14][...] + down)


def guest_kernel(*refs):
    rows = jnp.concatenate([ref[...] for ref in refs[:4]], axis=0)
    down = hidden_units(rows, refs[4:12], refs[12:20], refs[23]).astype(BF)
    for ref, start, stop in zip(refs[20:23], (0, 144, 272), (144, 272, 288)):
        ref[...] = down[start:stop]


def feed_forward(kernel, inputs, outputs, rows, shares, time, name):
    vmem = pl.BlockSpec(memory_space=pltpu.VMEM)
    return pl.pallas_call(
        kernel,
        out_shape=outputs,
        in_specs=[vmem] * len(inputs),
        out_specs=(vmem,) * len(outputs),
        scratch_shapes=[pltpu.VMEM((rows, shares * SHARE), BF)],
        compiler_params=pltpu.CompilerParams(vmem_limit_bytes=VMEM_LIMIT),
        cost_estimate=cost(time),
        name=name,
    )(*inputs)


def final_kernel(start_ref, extra_ref, mine_ref, first_ref, second_ref, prefill_ref, decode_ref):
    for part, ref in ((0, first_ref), (1, second_ref)):
        cut = slice(part * 128, (part + 1) * 128)
        prefill_ref[cut, :] = (start_ref[cut, :] + ref[:128, :].astype(F32)).astype(BF)
    alone = mine_ref[...].astype(F32) + first_ref[128:, :].astype(F32)
    decode_ref[...] = (extra_ref[...].astype(F32) + alone)[:2].astype(BF)


def final_sum(start, extra, mine, first, second):
    return pl.pallas_call(
        final_kernel,
        out_shape=(
            jax.ShapeDtypeStruct((ROWS, WIDTH), BF),
            jax.ShapeDtypeStruct((2, WIDTH), BF),
        ),
        in_specs=[pl.BlockSpec(memory_space=pltpu.VMEM)] * 5,
        compiler_params=pltpu.CompilerParams(vmem_limit_bytes=VMEM_LIMIT),
        cost_estimate=cost(1),
        name="final",
    )(start, extra, mine, first, second)


def body(
    prefill_hidden,
    decode_hidden,
    attn_gain,
    w_qkv,
    w_out,
    ffn_gain,
    w_gate_up,
    w_down,
    key_value_cache,
    cache_len,
    slot_of_request,
    held_hidden,
    recomputed_index,
    recomp_count,
):
    device = lax.axis_index("req").astype(jnp.int32).reshape(1)
    rank = device % 4
    gain, gain2 = attn_gain, ffn_gain
    index = recomputed_index.reshape(8, 128)

    w_all = w_out
    w_qkv, w_out, key_value_cache, held_hidden, prefill_hidden = in_hbm(
        w_qkv, w_out, key_value_cache, held_hidden, prefill_hidden
    )
    total = 2 * SIDE**3
    spread = jnp.broadcast_to(decode_hidden[None], (total, 2, WIDTH))
    every_row = lax.all_to_all(spread, "req", 0, 0).reshape(256, WIDTH)

    low, high = pack_weights(*in_hbm(jnp.swapaxes(w_gate_up, 1, 2), w_down))
    (kv,) = in_hbm(project(rank, prefill_hidden, gain, w_qkv, True))
    zed = send(kv, pair_z)
    core = send(kv, other_core)
    low, high, kv = lax.optimization_barrier((low, high, kv))
    below_low = send(low, next_z)
    above_high = send(high, last_z)
    (query,) = in_hbm(project(rank, prefill_hidden, gain, w_qkv, False))
    low, high, query = lax.optimization_barrier((low, high, query))
    below_high = send(high, next_z)
    above_low = send(low, last_z)
    every_row, query = lax.optimization_barrier((every_row, query))
    outgoing = decode_attention(
        device,
        cache_len,
        recomp_count,
        slot_of_request.reshape(1, 256),
        index,
        every_row,
        gain,
        w_qkv,
        key_value_cache,
        held_hidden,
    )
    outgoing, zed, core, below_low, above_high, low, high = lax.optimization_barrier(
        (outgoing, zed, core, below_low, above_high, low, high)
    )
    low_core = send(low, other_core)
    high_core = send(high, other_core)
    far = send(zed, other_core)
    core, zed, far = in_hbm(core, zed, far)
    far_low = send(below_low, next_z)
    far_high = send(above_high, last_z)
    below_low_core = send(below_low, other_core)
    above_high_core = send(above_high, other_core)
    back = lax.all_to_all(outgoing.reshape(total, 2, WIDTH), "req", 0, 0)

    resid, lower, upper = attention(
        rank, query, kv, core, zed, far, w_out, prefill_hidden, gain2
    )
    from_last = send(lower, next_x)
    from_next = send(upper, last_x)
    (mine,) = feed_forward(
        first_kernel,
        (lower, upper, low, low_core, high, high_core),
        (jax.ShapeDtypeStruct((ROWS, WIDTH), F32),),
        ROWS,
        2,
        0.1,
        "feed_first",
    )
    mine, back = lax.optimization_barrier((mine, back))
    extra, alone = decode_rows(back, w_all, decode_hidden, gain2)
    alone, far_low, far_high, from_last, from_next, below_high, above_low = (
        lax.optimization_barrier(
            (alone, far_low, far_high, from_last, from_next, below_high, above_low)
        )
    )
    far_low_core = send(far_low, other_core)
    far_high_core = send(far_high, other_core)
    below_high_core = send(below_high, other_core)
    above_low_core = send(above_low, other_core)
    guest = send(alone, next_x)
    lows = (low, low_core)
    highs = (high, high_core)
    lows_far = (below_low, below_low_core, above_low, above_low_core, far_low, far_low_core)
    highs_far = (below_high, below_high_core, above_high, above_high_core, far_high, far_high_core)
    to_last, to_next, alone = feed_forward(
        guest_kernel,
        (from_last, guest, from_next, alone) + lows + lows_far + highs + highs_far,
        tuple(jax.ShapeDtypeStruct((n, WIDTH), BF) for n in (144, 128, 16)),
        ROWS + 32,
        8,
        8,
        "feed_guest",
    )
    to_last, to_next, mine = lax.optimization_barrier((to_last, to_next, mine))
    first = send(to_last, last_x)
    second = send(to_next, next_x)
    (start,) = feed_forward(
        second_kernel,
        (lower, upper) + lows_far + highs_far + (mine, resid),
        (jax.ShapeDtypeStruct((ROWS, WIDTH), F32),),
        ROWS,
        6,
        6,
        "feed_second",
    )
    return final_sum(start, extra, alone, first, second)


def solution(mesh):
    return jax.shard_map(
        body,
        mesh=mesh,
        in_specs=(
            P("req", None),
            P("req", None),
            P(),
            P(),
            P(),
            P(),
            P("req", None, None),
            P("req", None, None),
            P("req", None, None),
            P("req"),
            P(),
            P("req", None),
            P("req"),
            P("req"),
        ),
        out_specs=(P("req", None), P("req", None)),
        check_vma=False,
    )
```

```python
import functools

import jax
import jax.numpy as jnp
import numpy as np
from jax import lax
from jax.experimental import pallas as pl
from jax.experimental.pallas import tpu as pltpu
from jax.sharding import PartitionSpec as P

WIDTH = 1280
QUERY_HEADS = 20
HEAD = 64
QW = 1280
KVW = 640
SHARE = 224
PART = 3 * SHARE // 2
GROUP = 16
SIDE = 4
SLOTS = 4
POSITIONS = 1024
ROWS = 256
EPS = 1e-05
THETA = 10000.0
NEG = -1e30
F32 = jnp.float32
BF = jnp.bfloat16
NT = (((1,), (1,)), ((), ()))
VMEM_LIMIT = 24 << 20


def cost(microseconds):
    return pl.CostEstimate(
        flops=int(microseconds * 10**9), transcendentals=0, bytes_accessed=int(microseconds * 3000000)
    )


def place(y, x, z, core):
    return (((y % SIDE) * SIDE + x % SIDE) * SIDE + z % SIDE) * 2 + core


def moves(step):
    pairs = []
    for y in range(SIDE):
        for x in range(SIDE):
            for z in range(SIDE):
                for core in range(2):
                    pairs.append((place(y, x, z, core), place(*step(y, x, z, core))))
    return pairs


def send(array, step):
    return lax.ppermute(array, "req", moves(step))


def in_hbm(*arrays):
    return [pltpu.with_memory_space_constraint(a, pltpu.MemorySpace.HBM) for a in arrays]


def other_core(y, x, z, core):
    return y, x, z, 1 - core


def next_x(y, x, z, core):
    return y, x + 1, z, core


def last_x(y, x, z, core):
    return y, x - 1, z, core


def next_z(y, x, z, core):
    return y, x, z + 1, core


def last_z(y, x, z, core):
    return y, x, z - 1, core


def pair_z(y, x, z, core):
    return y, x, z ^ 1, core


def norm_rows(rows, gain):
    rows = rows.astype(F32)
    mean = jnp.mean(rows * rows, axis=-1, keepdims=True)
    return (rows * lax.rsqrt(mean + EPS) * gain.reshape(1, WIDTH)).astype(BF)


def lanes(shape):
    return lax.broadcasted_iota(jnp.int32, shape, len(shape) - 1)


def sublanes(shape):
    return lax.broadcasted_iota(jnp.int32, shape, len(shape) - 2)


def sine_cosine(angle):
    turns = jnp.floor(angle * (2.0 / np.pi) + 0.5)
    rest = angle - turns * 1.5703125
    rest = rest - turns * 4.837512969970703125e-4
    rest = rest - turns * 7.54978995489188216e-8
    square = rest * rest
    sine = 8.3321608736e-3 + square * -1.9515295891e-4
    sine = rest + rest * square * (-1.6666654611e-1 + square * sine)
    cosine = -1.388731625493765e-3 + square * 2.443315711809948e-5
    cosine = 4.166664568298827e-2 + square * cosine
    cosine = 1.0 - 0.5 * square + square * square * cosine
    quarter = turns.astype(jnp.int32) & 3
    odd = (quarter & 1) == 1
    out_sine = jnp.where(odd, cosine, sine)
    out_cosine = jnp.where(odd, sine, cosine)
    out_sine = jnp.where(quarter >= 2, -out_sine, out_sine)
    out_cosine = jnp.where((quarter == 1) | (quarter == 2), -out_cosine, out_cosine)
    return out_sine, out_cosine


def rope_tables(position):
    pair = (lanes((1, position.shape[1])) % (HEAD // 2)).astype(F32)
    frequency = jnp.exp(pair * (-2.0 * np.log(THETA) / HEAD))
    sine, cosine = sine_cosine(position * frequency)
    low = lanes(sine.shape) % HEAD < HEAD // 2
    return cosine, jnp.where(low, -sine, sine)


def rope(chunk, cosine, sine):
    low = lanes(chunk.shape) % HEAD < HEAD // 2
    other = jnp.where(low, pltpu.roll(chunk, 96, 1), pltpu.roll(chunk, 32, 1))
    return chunk * cosine + other * sine


def pack_kernel(gate_up_ref, down_ref, packed_ref):
    packed_ref[: 2 * SHARE, :] = gate_up_ref[...]
    packed_ref[2 * SHARE :, :] = down_ref[...]


def pack_weights(gate_up, down):
    return pl.pallas_call(
        pack_kernel,
        out_shape=jax.ShapeDtypeStruct((3 * SHARE, WIDTH), BF),
        grid=(2,),
        in_specs=[
            pl.BlockSpec((None, 2 * SHARE, WIDTH // 2), lambda i: (0, 0, i)),
            pl.BlockSpec((None, SHARE, WIDTH // 2), lambda i: (0, 0, i)),
        ],
        out_specs=pl.BlockSpec((3 * SHARE, WIDTH // 2), lambda i: (0, i)),
        compiler_params=pltpu.CompilerParams(vmem_limit_bytes=VMEM_LIMIT),
        cost_estimate=cost(1.5),
        name="pack",
    )(gate_up, down)


def cut_kernel(below_ref, above_ref, low_ref, high_ref):
    low_ref[...] = below_ref[:PART, :]
    high_ref[...] = above_ref[PART:, :]


def cut_halves(below, above):
    vmem = pl.BlockSpec(memory_space=pltpu.VMEM)
    return pl.pallas_call(
        cut_kernel,
        out_shape=(jax.ShapeDtypeStruct((PART, WIDTH), BF),) * 2,
        in_specs=[vmem] * 2,
        out_specs=(vmem,) * 2,
        compiler_params=pltpu.CompilerParams(vmem_limit_bytes=VMEM_LIMIT),
        cost_estimate=cost(0.5),
        name="cut",
    )(below, above)


def kv_kernel(rank_ref, hidden_ref, gain_ref, w_ref, kv_ref):
    normed = norm_rows(hidden_ref[...], gain_ref[...])
    position = (sublanes((ROWS, 128)) * 4 + rank_ref[0]).astype(F32)
    cosine, sine = rope_tables(position)
    projected = jnp.dot(normed, w_ref[...], preferred_element_type=F32)
    chunks = [projected[:, i * 128 : (i + 1) * 128] for i in range(5)]
    low = lanes((ROWS, 128)) < HEAD
    first = rope(chunks[0], cosine, sine)
    second = rope(chunks[1], cosine, sine)
    third = jnp.where(low, rope(chunks[2], cosine, sine), chunks[2])
    swap = lambda value: pltpu.roll(value, 64, 1)
    out = [
        jnp.where(low, first, third),
        jnp.where(low, swap(first), swap(chunks[3])),
        jnp.where(low, second, chunks[3]),
        jnp.where(low, swap(second), swap(chunks[4])),
        jnp.where(low, third, chunks[4]),
    ]
    for i in range(5):
        kv_ref[:, i * 128 : (i + 1) * 128] = out[i].astype(BF)


def query_kernel(rank_ref, hidden_ref, gain_ref, w_ref, query_ref, normed, cos, sin):
    @pl.when(pl.program_id(0) == 0)
    def _():
        normed[...] = norm_rows(hidden_ref[...], gain_ref[...])
        position = (sublanes((ROWS, 128)) * 4 + rank_ref[0]).astype(F32)
        cos[...], sin[...] = rope_tables(position)

    projected = jnp.dot(normed[...], w_ref[...], preferred_element_type=F32)
    for i in range(5):
        roped = rope(projected[:, i * 128 : (i + 1) * 128], cos[...], sin[...]).astype(BF)
        query_ref[:, i * 128 : (i + 1) * 128] = roped * jnp.asarray(0.125, BF)


def project(rank, hidden, gain, w_qkv, keys):
    steps = 1 if keys else 2
    scratch = [
        pltpu.VMEM((ROWS, WIDTH), BF),
        pltpu.VMEM((ROWS, 128), F32),
        pltpu.VMEM((ROWS, 128), F32),
    ]
    return pl.pallas_call(
        kv_kernel if keys else query_kernel,
        out_shape=jax.ShapeDtypeStruct((ROWS, KVW * steps), BF),
        grid=(steps,),
        in_specs=[
            pl.BlockSpec(memory_space=pltpu.SMEM),
            pl.BlockSpec((ROWS, WIDTH), lambda j: (0, 0)),
            pl.BlockSpec((WIDTH,), lambda j: (0,)),
            pl.BlockSpec((WIDTH, KVW), (lambda j: (0, 2)) if keys else (lambda j: (0, j))),
        ],
        out_specs=pl.BlockSpec((ROWS, KVW), lambda j: (0, j)),
        scratch_shapes=[] if keys else scratch,
        compiler_params=pltpu.CompilerParams(vmem_limit_bytes=VMEM_LIMIT),
        cost_estimate=cost(3 if keys else 0.1),
        name="prefill_kv" if keys else "prefill_query",
    )(rank, hidden, gain, w_qkv)


def column(row):
    return jnp.broadcast_to(row, (128, 128)).T


def decode_kernel(
    device_ref,
    length_ref,
    count_ref,
    slot_ref,
    index_ref,
    rows_ref,
    gain_ref,
    w_ref,
    cache_ref,
    hidden_ref,
    out_ref,
    held_ref,
    spread,
    query,
    fresh_key,
    fresh_value,
    over,
    result,
):
    tick = pl.program_id(0)
    step = tick - SLOTS
    first_slot = device_ref[0] * SLOTS

    @pl.when(tick < SLOTS)
    def _():
        normed = norm_rows(hidden_ref[...], gain_ref[...])
        projected = jnp.dot(normed, w_ref[:, QW:], preferred_element_type=F32)
        position = (index_ref[pl.ds(tick * 2, 2), :] % POSITIONS).astype(F32)
        position = jnp.concatenate([column(position[0:1]), column(position[1:2])], axis=0)
        cosine, sine = rope_tables(position)
        low = lanes((256, 128)) < HEAD
        rows = pl.ds(pl.multiple_of(tick * 256, 256), 256)
        for i in range(5):
            chunk = projected[:, i * 128 : (i + 1) * 128]
            if i < 2:
                chunk = rope(chunk, cosine, sine)
            elif i == 2:
                chunk = jnp.where(low, rope(chunk, cosine, sine), chunk)
            held_ref[rows, i * 128 : (i + 1) * 128] = chunk.astype(BF)

    index_rows = [index_ref[i : i + 1, :] for i in range(8)]

    @pl.when(step == 0)
    def _():
        spread[...] = (
            sublanes((QW, 384)) % HEAD == lanes((QW, 384)) % HEAD
        ).astype(F32).astype(BF)
        wanted = jnp.broadcast_to(slot_ref[...], (8, 256))
        slot = sublanes((8, 256))
        chosen = ((wanted == first_slot + slot) & (slot < SLOTS)).astype(F32).astype(BF)
        rows = jnp.dot(chosen, rows_ref[...], preferred_element_type=F32)
        normed = norm_rows(rows, gain_ref[...])
        projected = jnp.dot(normed, w_ref[...], preferred_element_type=F32)
        projected = projected.astype(BF).astype(F32)
        row = sublanes((8, 128))
        position = jnp.zeros((8, 128), F32)
        for j in range(SLOTS):
            position = jnp.where(row == j, length_ref[j].astype(F32), position)
        cosine, sine = rope_tables(position)
        chunks = [projected[:, i * 128 : (i + 1) * 128] for i in range(15)]
        roped = [rope(chunks[i], cosine, sine).astype(BF) for i in range(13)]
        whole = jnp.concatenate(roped[:10], axis=1).astype(F32) * 0.125
        head_of = sublanes((32, QW))
        keep = lanes((32, QW)) // HEAD == head_of
        group = sublanes((32, 384))
        block = (lanes((32, 384)) // HEAD == group // 4) & (group < QUERY_HEADS)
        for j in range(SLOTS):
            placed = jnp.where(keep, jnp.broadcast_to(whole[j : j + 1], (32, QW)), 0.0)
            turned = jnp.dot(placed.astype(BF), spread[...], preferred_element_type=F32)
            query[j * 32 : (j + 1) * 32, :] = jnp.where(block, turned, 0.0).astype(BF)
        fresh_key[...] = jnp.concatenate(roped[10:13], axis=1).astype(F32)
        fresh_value[...] = jnp.concatenate(chunks[12:15], axis=1)
        counts = jnp.zeros((32, 128), F32)
        for i in range(8):
            entry = i * 128 + lanes((32, 128))
            live = entry < count_ref[0]
            upper = jnp.broadcast_to(index_rows[i] // 128, (32, 128)) == sublanes((32, 128))
            upper = (upper & live).astype(F32).astype(BF)
            lower = jnp.broadcast_to(index_rows[i] % 128, (128, 128)) == sublanes((128, 128))
            lower = lower.astype(F32).astype(BF)
            counts = counts + lax.dot_general(upper, lower, NT, preferred_element_type=F32)
        over[...] = counts

    @pl.when(step >= 0)
    def _():
        length = length_ref[step]
        queries = query[pl.ds(pl.multiple_of(step * 32, 32), 32), :]
        taken = over[pl.ds(pl.multiple_of(step * 8, 8), 8), :]
        taken = jnp.concatenate([taken[i : i + 1, :] for i in range(8)], axis=1)
        cache_live = (lanes((1, POSITIONS)) < length) & (taken < 0.5)
        index = jnp.concatenate(index_rows, axis=1)
        held_live = (
            (lanes((1, 1024)) < count_ref[0])
            & (index // POSITIONS == step)
            & (index % POSITIONS < length)
        )
        cache_score = lax.dot_general(queries, cache_ref[:, :384], NT, preferred_element_type=F32)
        held_score = lax.dot_general(queries, held_ref[:, :384], NT, preferred_element_type=F32)
        own_score = jnp.sum(
            queries.astype(F32) * fresh_key[pl.ds(step, 1), :], axis=-1, keepdims=True
        )
        cache_live = jnp.broadcast_to(cache_live, cache_score.shape)
        held_live = jnp.broadcast_to(held_live, held_score.shape)
        cache_score = jnp.where(cache_live, cache_score, NEG)
        held_score = jnp.where(held_live, held_score, NEG)
        top = jnp.maximum(
            jnp.maximum(
                jnp.max(cache_score, axis=-1, keepdims=True), jnp.max(held_score, axis=-1, keepdims=True)
            ),
            own_score,
        )
        cache_weight = jnp.where(cache_live, jnp.exp(cache_score - top), 0.0)
        held_weight = jnp.where(held_live, jnp.exp(held_score - top), 0.0)
        own_weight = jnp.exp(own_score - top)
        total = (
            jnp.sum(cache_weight, axis=-1, keepdims=True)
            + jnp.sum(held_weight, axis=-1, keepdims=True)
            + own_weight
        )
        mixed = jnp.dot(cache_weight.astype(BF), cache_ref[:, 256:], preferred_element_type=F32)
        mixed += jnp.dot(held_weight.astype(BF), held_ref[:, 256:], preferred_element_type=F32)
        mixed += own_weight.astype(BF).astype(F32) * fresh_value[pl.ds(step, 1), :]
        group = sublanes((32, 384))
        block = (lanes((32, 384)) // HEAD == group // 4 + 1) & (group < QUERY_HEADS)
        mixed = jnp.where(block, mixed / total, 0.0).astype(BF)
        turned = lax.dot_general(mixed, spread[...], NT, preferred_element_type=F32)
        keep = lanes((32, QW)) // HEAD == sublanes((32, QW))
        result[pl.ds(step, 1), :] = jnp.sum(jnp.where(keep, turned, 0.0), axis=0, keepdims=True)

    @pl.when(step == SLOTS - 1)
    def _():
        wanted = jnp.broadcast_to(slot_ref[...], (8, 256))
        slot = sublanes((8, 256))
        chosen = ((wanted == first_slot + slot) & (slot < SLOTS)).astype(F32).astype(BF)
        good = jnp.where(sublanes((8, QW)) < SLOTS, result[...], 0.0).astype(BF)
        out_ref[...] = lax.dot_general(
            chosen, good, (((0,), (0,)), ((), ())), preferred_element_type=F32
        ).astype(BF)


def decode_attention(
    device, length, count, slots, index, rows, gain, w_qkv, cache, hidden
):
    smem = pl.BlockSpec(memory_space=pltpu.SMEM)
    full = lambda shape: pl.BlockSpec(shape, lambda j: (0,) * len(shape))
    return pl.pallas_call(
        decode_kernel,
        out_shape=jax.ShapeDtypeStruct((256, QW), BF),
        grid=(2 * SLOTS,),
        in_specs=[
            smem,
            smem,
            smem,
            full((1, 256)),
            full((8, 128)),
            full((256, WIDTH)),
            full((WIDTH,)),
            pl.BlockSpec(
                (WIDTH, QW + KVW), lambda j: (0, 0), pipeline_mode=pl.Buffered(1)
            ),
            pl.BlockSpec((None, POSITIONS, KVW), lambda j: (jnp.maximum(j - SLOTS, 0), 0, 0)),
            pl.BlockSpec((256, WIDTH), lambda j: (jnp.minimum(j, SLOTS - 1), 0)),
        ],
        out_specs=full((256, QW)),
        scratch_shapes=[
            pltpu.VMEM((1024, KVW), BF),
            pltpu.VMEM((QW, 384), BF),
            pltpu.VMEM((128, 384), BF),
            pltpu.VMEM((8, 384), F32),
            pltpu.VMEM((8, 384), F32),
            pltpu.VMEM((32, 128), F32),
            pltpu.VMEM((8, QW), F32),
        ],
        compiler_params=pltpu.CompilerParams(vmem_limit_bytes=VMEM_LIMIT),
        cost_estimate=cost(17),
        name="decode",
    )(device, length, count, slots, index, rows, gain, w_qkv, cache, hidden)


def attention_kernel(
    rank_ref,
    query_ref,
    own_ref,
    core_ref,
    zed_ref,
    far_ref,
    w_ref,
    hidden_ref,
    gain_ref,
    resid_ref,
    lower_ref,
    upper_ref,
    total,
    mask,
):
    group = pl.program_id(0)

    @pl.when(group == 0)
    def _():
        total[...] = jnp.zeros_like(total)
        rank = rank_ref[0]
        row = sublanes((128, 128))
        col = lanes((128, 128))
        for piece in range(4):
            other = rank ^ piece
            bound = jnp.where(other <= rank, 0, 1)
            mask[:, piece * 128 : (piece + 1) * 128] = jnp.where(col + bound <= row, 0.0, NEG)

    pieces = [own_ref, core_ref, zed_ref, far_ref]
    keys = jnp.concatenate(
        [ref[h * 128 : (h + 1) * 128, :] for h in range(2) for ref in pieces], axis=0
    )
    low = lanes((1024, 128)) < HEAD
    wide = keys.astype(F32)
    values = jnp.where(low, pltpu.roll(wide, 64, 1), wide).astype(BF)
    values = jnp.concatenate([values, jnp.ones((1024, 128), BF)], axis=1)
    low = lanes((128, 128)) < HEAD
    blocked = mask[...]
    mixed = []
    for tile in range(2):
        heads = []
        for pair in range(2):
            two = query_ref[tile * 128 : (tile + 1) * 128, pair * 128 : (pair + 1) * 128].astype(F32)
            heads.append(jnp.where(low, two, 0.0).astype(BF))
            heads.append(jnp.where(low, pltpu.roll(two, 64, 1), 0.0).astype(BF))
        out = []
        for head in heads:
            count = 512 * (tile + 1)
            score = lax.dot_general(head, keys[:count], NT, preferred_element_type=F32)
            if tile == 0:
                score = score + blocked
            else:
                score = jnp.concatenate([score[:, :512], score[:, 512:] + blocked], axis=1)
            top = jnp.max(score, axis=-1, keepdims=True)
            weight = jnp.exp(score - top).astype(BF)
            both = jnp.dot(weight, values[:count], preferred_element_type=F32)
            out.append(both[:, :128] / both[:, 128:])
        mixed.append(
            jnp.concatenate(
                [jnp.where(low, out[0], out[1]), jnp.where(low, out[2], out[3])], axis=1
            ).astype(BF)
        )
    rows = jnp.concatenate(mixed, axis=0)
    total[...] += jnp.dot(rows, w_ref[...], preferred_element_type=F32)

    @pl.when(group == 4)
    def _():
        for part in range(2):
            cut = slice(part * 128, (part + 1) * 128)
            resid = (hidden_ref[cut, :].astype(F32) + total[cut, :]).astype(BF)
            resid_ref[cut, :] = resid
            (lower_ref, upper_ref)[part][...] = norm_rows(resid, gain_ref[...])


def attention(rank, query, own, core, zed, far, w_out, hidden, gain):
    full = lambda shape: pl.BlockSpec(shape, lambda g: (0,) * len(shape))
    side = pl.BlockSpec((ROWS, 128), lambda g: (0, g))
    return pl.pallas_call(
        attention_kernel,
        out_shape=(
            jax.ShapeDtypeStruct((ROWS, WIDTH), BF),
            jax.ShapeDtypeStruct((ROWS // 2, WIDTH), BF),
            jax.ShapeDtypeStruct((ROWS // 2, WIDTH), BF),
        ),
        grid=(5,),
        in_specs=[
            pl.BlockSpec(memory_space=pltpu.SMEM),
            pl.BlockSpec((ROWS, 256), lambda g: (0, g)),
            side,
            side,
            side,
            side,
            pl.BlockSpec((256, WIDTH), lambda g: (g, 0)),
            full((ROWS, WIDTH)),
            full((WIDTH,)),
        ],
        out_specs=(
            full((ROWS, WIDTH)),
            full((ROWS // 2, WIDTH)),
            full((ROWS // 2, WIDTH)),
        ),
        scratch_shapes=[
            pltpu.VMEM((ROWS, WIDTH), F32),
            pltpu.VMEM((128, 512), F32),
        ],
        compiler_params=pltpu.CompilerParams(vmem_limit_bytes=VMEM_LIMIT),
        cost_estimate=cost(0.1),
        name="attention",
    )(rank, query, own, core, zed, far, w_out, hidden, gain)


def decode_rows_kernel(back_ref, w_ref, decode_ref, gain_ref, resid_ref, normed_ref):
    mixed = jnp.sum(back_ref[...].astype(F32), axis=0)
    mixed = jnp.concatenate([mixed, jnp.zeros((14, WIDTH), F32)], axis=0).astype(BF)
    single = decode_ref[...].astype(F32)
    hidden = jnp.concatenate([single, jnp.zeros((14, WIDTH), F32)], axis=0)
    resid = (hidden + jnp.dot(mixed, w_ref[...], preferred_element_type=F32)).astype(BF)
    resid_ref[...] = resid
    normed_ref[...] = norm_rows(resid, gain_ref[...])


def decode_rows(back, w_out, decode, gain):
    vmem = pl.BlockSpec(memory_space=pltpu.VMEM)
    return pl.pallas_call(
        decode_rows_kernel,
        out_shape=(jax.ShapeDtypeStruct((16, WIDTH), BF),) * 2,
        in_specs=[vmem] * 4,
        out_specs=(vmem,) * 2,
        compiler_params=pltpu.CompilerParams(vmem_limit_bytes=VMEM_LIMIT),
        cost_estimate=cost(0.1),
        name="decode_rows",
    )(back, w_out, decode, gain)


def hidden_units(rows, packs, lows, highs, act):
    cut = 2 * SHARE - PART
    weights = [(ref[:SHARE, :], ref[SHARE : 2 * SHARE, :], ref[2 * SHARE :, :]) for ref in packs]
    for low, high in zip(lows, highs):
        up_rows = jnp.concatenate([low[SHARE:, :], high[:cut, :]], axis=0)
        weights.append((low[:SHARE, :], up_rows, high[cut:, :]))
    for k, (gate_rows, up_rows, _) in enumerate(weights):
        gate = lax.dot_general(rows, gate_rows, NT, preferred_element_type=F32)
        up = lax.dot_general(rows, up_rows, NT, preferred_element_type=F32)
        act[:, k * SHARE : (k + 1) * SHARE] = (gate / (1.0 + jnp.exp(-gate)) * up).astype(BF)
    down = jnp.concatenate([down_rows for _, _, down_rows in weights], axis=0)
    return jnp.dot(act[...], down, preferred_element_type=F32)


def first_kernel(*refs):
    rows = jnp.concatenate([refs[0][...], refs[1][...]], axis=0)
    refs[4][...] = hidden_units(rows, refs[2:4], (), (), refs[5])


def second_kernel(*refs):
    rows = jnp.concatenate([refs[0][...], refs[1][...]], axis=0)
    down = hidden_units(rows, refs[2:6], refs[6:8], refs[8:10], refs[13])
    refs[12][...] = refs[11][...].astype(F32) + (refs[10][...] + down)


def guest_kernel(*refs):
    rows = jnp.concatenate([ref[...] for ref in refs[:4]], axis=0)
    down = hidden_units(rows, refs[4:10], refs[10:12], refs[12:14], refs[17]).astype(BF)
    for ref, start, stop in zip(refs[14:17], (0, 144, 272), (144, 272, 288)):
        ref[...] = down[start:stop]


def feed_forward(kernel, inputs, outputs, rows, shares, time, name):
    vmem = pl.BlockSpec(memory_space=pltpu.VMEM)
    return pl.pallas_call(
        kernel,
        out_shape=outputs,
        in_specs=[vmem] * len(inputs),
        out_specs=(vmem,) * len(outputs),
        scratch_shapes=[pltpu.VMEM((rows, shares * SHARE), BF)],
        compiler_params=pltpu.CompilerParams(vmem_limit_bytes=VMEM_LIMIT),
        cost_estimate=cost(time),
        name=name,
    )(*inputs)


def final_kernel(start_ref, extra_ref, mine_ref, first_ref, second_ref, prefill_ref, decode_ref):
    for part, ref in ((0, first_ref), (1, second_ref)):
        cut = slice(part * 128, (part + 1) * 128)
        prefill_ref[cut, :] = (start_ref[cut, :] + ref[:128, :].astype(F32)).astype(BF)
    alone = mine_ref[...].astype(F32) + first_ref[128:, :].astype(F32)
    decode_ref[...] = (extra_ref[...].astype(F32) + alone)[:2].astype(BF)


def final_sum(start, extra, mine, first, second):
    return pl.pallas_call(
        final_kernel,
        out_shape=(
            jax.ShapeDtypeStruct((ROWS, WIDTH), BF),
            jax.ShapeDtypeStruct((2, WIDTH), BF),
        ),
        in_specs=[pl.BlockSpec(memory_space=pltpu.VMEM)] * 5,
        compiler_params=pltpu.CompilerParams(vmem_limit_bytes=VMEM_LIMIT),
        cost_estimate=cost(1),
        name="final",
    )(start, extra, mine, first, second)


def body(
    prefill_hidden,
    decode_hidden,
    attn_gain,
    w_qkv,
    w_out,
    ffn_gain,
    w_gate_up,
    w_down,
    key_value_cache,
    cache_len,
    slot_of_request,
    held_hidden,
    recomputed_index,
    recomp_count,
):
    device = lax.axis_index("req").astype(jnp.int32).reshape(1)
    rank = device % 4
    gain, gain2 = attn_gain, ffn_gain
    index = recomputed_index.reshape(8, 128)

    w_all = w_out
    w_qkv, w_out, key_value_cache, held_hidden, prefill_hidden = in_hbm(
        w_qkv, w_out, key_value_cache, held_hidden, prefill_hidden
    )
    total = 2 * SIDE**3
    spread = jnp.broadcast_to(decode_hidden[None], (total, 2, WIDTH))
    every_row = lax.all_to_all(spread, "req", 0, 0).reshape(256, WIDTH)

    packed = pack_weights(*in_hbm(jnp.swapaxes(w_gate_up, 1, 2), w_down))
    (kv,) = in_hbm(project(rank, prefill_hidden, gain, w_qkv, True))
    zed = send(kv, pair_z)
    core = send(kv, other_core)
    packed, kv = lax.optimization_barrier((packed, kv))
    below = send(packed, next_z)
    above = send(packed, last_z)
    packed_core = send(packed, other_core)
    (query,) = in_hbm(project(rank, prefill_hidden, gain, w_qkv, False))
    every_row, query = lax.optimization_barrier((every_row, query))
    outgoing = decode_attention(
        device,
        cache_len,
        recomp_count,
        slot_of_request.reshape(1, 256),
        index,
        every_row,
        gain,
        w_qkv,
        key_value_cache,
        held_hidden,
    )
    outgoing, zed, core, packed_core = lax.optimization_barrier(
        (outgoing, zed, core, packed_core)
    )
    far = send(zed, other_core)
    core, zed, far = in_hbm(core, zed, far)
    below, above, packed_core = lax.optimization_barrier((below, above, packed_core))
    far_low, far_high = cut_halves(below, above)
    far_low = send(far_low, next_z)
    far_high = send(far_high, last_z)
    back = lax.all_to_all(outgoing.reshape(total, 2, WIDTH), "req", 0, 0)

    resid, lower, upper = attention(
        rank, query, kv, core, zed, far, w_out, prefill_hidden, gain2
    )
    from_last = send(lower, next_x)
    from_next = send(upper, last_x)
    (mine,) = feed_forward(
        first_kernel,
        (lower, upper, packed, packed_core),
        (jax.ShapeDtypeStruct((ROWS, WIDTH), F32),),
        ROWS,
        2,
        0.1,
        "feed_first",
    )
    mine, back = lax.optimization_barrier((mine, back))
    below, above, back, from_last, from_next = lax.optimization_barrier(
        (below, above, back, from_last, from_next)
    )
    below_core = send(below, other_core)
    above_core = send(above, other_core)
    extra, alone = decode_rows(back, w_all, decode_hidden, gain2)
    guest = send(alone, next_x)
    alone, far_low, far_high = lax.optimization_barrier((alone, far_low, far_high))
    far_low_core = send(far_low, other_core)
    far_high_core = send(far_high, other_core)
    gathered = (below, below_core, above, above_core)
    distant = (far_low, far_low_core, far_high, far_high_core)
    to_last, to_next, alone = feed_forward(
        guest_kernel,
        (from_last, guest, from_next, alone, packed, packed_core) + gathered + distant,
        tuple(jax.ShapeDtypeStruct((n, WIDTH), BF) for n in (144, 128, 16)),
        ROWS + 32,
        8,
        8,
        "feed_guest",
    )
    to_last, to_next, mine = lax.optimization_barrier((to_last, to_next, mine))
    first = send(to_last, last_x)
    second = send(to_next, next_x)
    (start,) = feed_forward(
        second_kernel,
        (lower, upper) + gathered + distant + (mine, resid),
        (jax.ShapeDtypeStruct((ROWS, WIDTH), F32),),
        ROWS,
        6,
        6,
        "feed_second",
    )
    return final_sum(start, extra, alone, first, second)


def solution(mesh):
    return jax.shard_map(
        body,
        mesh=mesh,
        in_specs=(
            P("req", None),
            P("req", None),
            P(),
            P(),
            P(),
            P(),
            P("req", None, None),
            P("req", None, None),
            P("req", None, None),
            P("req"),
            P(),
            P("req", None),
            P("req"),
            P("req"),
        ),
        out_specs=(P("req", None), P("req", None)),
        check_vma=False,
    )
```

```python
import functools

import jax
import jax.numpy as jnp
import numpy as np
from jax import lax
from jax.experimental import pallas as pl
from jax.experimental.pallas import tpu as pltpu
from jax.sharding import PartitionSpec as P

WIDTH = 1280
QUERY_HEADS = 20
HEAD = 64
QW = 1280
KVW = 640
SHARE = 224
PART = 3 * SHARE // 2
GROUP = 16
SIDE = 4
SLOTS = 4
POSITIONS = 1024
ROWS = 256
EPS = 1e-05
THETA = 10000.0
NEG = -1e30
F32 = jnp.float32
BF = jnp.bfloat16
NT = (((1,), (1,)), ((), ()))
VMEM_LIMIT = 24 << 20


def cost(microseconds):
    return pl.CostEstimate(
        flops=int(microseconds * 10**9), transcendentals=0, bytes_accessed=int(microseconds * 3000000)
    )


def place(y, x, z, core):
    return (((y % SIDE) * SIDE + x % SIDE) * SIDE + z % SIDE) * 2 + core


def moves(step):
    pairs = []
    for y in range(SIDE):
        for x in range(SIDE):
            for z in range(SIDE):
                for core in range(2):
                    pairs.append((place(y, x, z, core), place(*step(y, x, z, core))))
    return pairs


def send(array, step):
    return lax.ppermute(array, "req", moves(step))


def in_hbm(*arrays):
    return [pltpu.with_memory_space_constraint(a, pltpu.MemorySpace.HBM) for a in arrays]


def other_core(y, x, z, core):
    return y, x, z, 1 - core


def next_x(y, x, z, core):
    return y, x + 1, z, core


def last_x(y, x, z, core):
    return y, x - 1, z, core


def next_z(y, x, z, core):
    return y, x, z + 1, core


def last_z(y, x, z, core):
    return y, x, z - 1, core


def pair_z(y, x, z, core):
    return y, x, z ^ 1, core


def norm_rows(rows, gain):
    rows = rows.astype(F32)
    mean = jnp.mean(rows * rows, axis=-1, keepdims=True)
    return (rows * lax.rsqrt(mean + EPS) * gain.reshape(1, WIDTH)).astype(BF)


def lanes(shape):
    return lax.broadcasted_iota(jnp.int32, shape, len(shape) - 1)


def sublanes(shape):
    return lax.broadcasted_iota(jnp.int32, shape, len(shape) - 2)


def sine_cosine(angle):
    turns = jnp.floor(angle * (2.0 / np.pi) + 0.5)
    rest = angle - turns * 1.5703125
    rest = rest - turns * 4.837512969970703125e-4
    rest = rest - turns * 7.54978995489188216e-8
    square = rest * rest
    sine = 8.3321608736e-3 + square * -1.9515295891e-4
    sine = rest + rest * square * (-1.6666654611e-1 + square * sine)
    cosine = -1.388731625493765e-3 + square * 2.443315711809948e-5
    cosine = 4.166664568298827e-2 + square * cosine
    cosine = 1.0 - 0.5 * square + square * square * cosine
    quarter = turns.astype(jnp.int32) & 3
    odd = (quarter & 1) == 1
    out_sine = jnp.where(odd, cosine, sine)
    out_cosine = jnp.where(odd, sine, cosine)
    out_sine = jnp.where(quarter >= 2, -out_sine, out_sine)
    out_cosine = jnp.where((quarter == 1) | (quarter == 2), -out_cosine, out_cosine)
    return out_sine, out_cosine


def rope_tables(position):
    pair = (lanes((1, position.shape[1])) % (HEAD // 2)).astype(F32)
    frequency = jnp.exp(pair * (-2.0 * np.log(THETA) / HEAD))
    sine, cosine = sine_cosine(position * frequency)
    low = lanes(sine.shape) % HEAD < HEAD // 2
    return cosine, jnp.where(low, -sine, sine)


def rope(chunk, cosine, sine):
    low = lanes(chunk.shape) % HEAD < HEAD // 2
    other = jnp.where(low, pltpu.roll(chunk, 96, 1), pltpu.roll(chunk, 32, 1))
    return chunk * cosine + other * sine


def pack_kernel(gate_up_ref, down_ref, packed_ref):
    packed_ref[: 2 * SHARE, :] = gate_up_ref[...]
    packed_ref[2 * SHARE :, :] = down_ref[...]


def pack_weights(gate_up, down):
    return pl.pallas_call(
        pack_kernel,
        out_shape=jax.ShapeDtypeStruct((3 * SHARE, WIDTH), BF),
        grid=(2,),
        in_specs=[
            pl.BlockSpec((None, 2 * SHARE, WIDTH // 2), lambda i: (0, 0, i)),
            pl.BlockSpec((None, SHARE, WIDTH // 2), lambda i: (0, 0, i)),
        ],
        out_specs=pl.BlockSpec((3 * SHARE, WIDTH // 2), lambda i: (0, i)),
        compiler_params=pltpu.CompilerParams(vmem_limit_bytes=VMEM_LIMIT),
        cost_estimate=cost(1.5),
        name="pack",
    )(gate_up, down)


def cut_kernel(below_ref, above_ref, low_ref, high_ref):
    low_ref[...] = below_ref[:PART, :]
    high_ref[...] = above_ref[PART:, :]


def cut_halves(below, above):
    vmem = pl.BlockSpec(memory_space=pltpu.VMEM)
    return pl.pallas_call(
        cut_kernel,
        out_shape=(jax.ShapeDtypeStruct((PART, WIDTH), BF),) * 2,
        in_specs=[vmem] * 2,
        out_specs=(vmem,) * 2,
        compiler_params=pltpu.CompilerParams(vmem_limit_bytes=VMEM_LIMIT),
        cost_estimate=cost(0.5),
        name="cut",
    )(below, above)


def kv_kernel(rank_ref, hidden_ref, gain_ref, w_ref, kv_ref):
    normed = norm_rows(hidden_ref[...], gain_ref[...])
    position = (sublanes((ROWS, 128)) * 4 + rank_ref[0]).astype(F32)
    cosine, sine = rope_tables(position)
    projected = jnp.dot(normed, w_ref[...], preferred_element_type=F32)
    chunks = [projected[:, i * 128 : (i + 1) * 128] for i in range(5)]
    low = lanes((ROWS, 128)) < HEAD
    first = rope(chunks[0], cosine, sine)
    second = rope(chunks[1], cosine, sine)
    third = jnp.where(low, rope(chunks[2], cosine, sine), chunks[2])
    swap = lambda value: pltpu.roll(value, 64, 1)
    out = [
        jnp.where(low, first, third),
        jnp.where(low, swap(first), swap(chunks[3])),
        jnp.where(low, second, chunks[3]),
        jnp.where(low, swap(second), swap(chunks[4])),
        jnp.where(low, third, chunks[4]),
    ]
    for i in range(5):
        kv_ref[:, i * 128 : (i + 1) * 128] = out[i].astype(BF)


def query_kernel(rank_ref, hidden_ref, gain_ref, w_ref, query_ref, normed, cos, sin):
    @pl.when(pl.program_id(0) == 0)
    def _():
        normed[...] = norm_rows(hidden_ref[...], gain_ref[...])
        position = (sublanes((ROWS, 128)) * 4 + rank_ref[0]).astype(F32)
        cos[...], sin[...] = rope_tables(position)

    projected = jnp.dot(normed[...], w_ref[...], preferred_element_type=F32)
    for i in range(5):
        roped = rope(projected[:, i * 128 : (i + 1) * 128], cos[...], sin[...]).astype(BF)
        query_ref[:, i * 128 : (i + 1) * 128] = roped * jnp.asarray(0.125, BF)


def project(rank, hidden, gain, w_qkv, keys):
    steps = 1 if keys else 2
    scratch = [
        pltpu.VMEM((ROWS, WIDTH), BF),
        pltpu.VMEM((ROWS, 128), F32),
        pltpu.VMEM((ROWS, 128), F32),
    ]
    return pl.pallas_call(
        kv_kernel if keys else query_kernel,
        out_shape=jax.ShapeDtypeStruct((ROWS, KVW * steps), BF),
        grid=(steps,),
        in_specs=[
            pl.BlockSpec(memory_space=pltpu.SMEM),
            pl.BlockSpec((ROWS, WIDTH), lambda j: (0, 0)),
            pl.BlockSpec((WIDTH,), lambda j: (0,)),
            pl.BlockSpec((WIDTH, KVW), (lambda j: (0, 2)) if keys else (lambda j: (0, j))),
        ],
        out_specs=pl.BlockSpec((ROWS, KVW), lambda j: (0, j)),
        scratch_shapes=[] if keys else scratch,
        compiler_params=pltpu.CompilerParams(vmem_limit_bytes=VMEM_LIMIT),
        cost_estimate=cost(3 if keys else 0.1),
        name="prefill_kv" if keys else "prefill_query",
    )(rank, hidden, gain, w_qkv)


def column(row):
    return jnp.broadcast_to(row, (128, 128)).T


def decode_kernel(
    device_ref,
    length_ref,
    count_ref,
    slot_ref,
    index_ref,
    rows_ref,
    gain_ref,
    w_ref,
    cache_ref,
    hidden_ref,
    out_ref,
    held_ref,
    spread,
    query,
    fresh_key,
    fresh_value,
    over,
    result,
    held_score,
    held_weight,
    mixture,
    totals,
):
    tick = pl.program_id(0)
    step = tick - SLOTS
    first_slot = device_ref[0] * SLOTS

    @pl.when(tick < SLOTS)
    def _():
        normed = norm_rows(hidden_ref[...], gain_ref[...])
        projected = jnp.dot(normed, w_ref[:, QW:], preferred_element_type=F32)
        position = (index_ref[pl.ds(tick * 2, 2), :] % POSITIONS).astype(F32)
        position = jnp.concatenate([column(position[0:1]), column(position[1:2])], axis=0)
        cosine, sine = rope_tables(position)
        low = lanes((256, 128)) < HEAD
        rows = pl.ds(pl.multiple_of(tick * 256, 256), 256)
        for i in range(5):
            chunk = projected[:, i * 128 : (i + 1) * 128]
            if i < 2:
                chunk = rope(chunk, cosine, sine)
            elif i == 2:
                chunk = jnp.where(low, rope(chunk, cosine, sine), chunk)
            held_ref[rows, i * 128 : (i + 1) * 128] = chunk.astype(BF)

    index_rows = [index_ref[i : i + 1, :] for i in range(8)]

    @pl.when(step == 0)
    def _():
        spread[...] = (
            sublanes((QW, 384)) % HEAD == lanes((QW, 384)) % HEAD
        ).astype(F32).astype(BF)
        wanted = jnp.broadcast_to(slot_ref[...], (8, 256))
        slot = sublanes((8, 256))
        chosen = ((wanted == first_slot + slot) & (slot < SLOTS)).astype(F32).astype(BF)
        rows = jnp.dot(chosen, rows_ref[...], preferred_element_type=F32)
        normed = norm_rows(rows, gain_ref[...])
        projected = jnp.dot(normed, w_ref[...], preferred_element_type=F32)
        projected = projected.astype(BF).astype(F32)
        row = sublanes((8, 128))
        position = jnp.zeros((8, 128), F32)
        for j in range(SLOTS):
            position = jnp.where(row == j, length_ref[j].astype(F32), position)
        cosine, sine = rope_tables(position)
        chunks = [projected[:, i * 128 : (i + 1) * 128] for i in range(15)]
        roped = [rope(chunks[i], cosine, sine).astype(BF) for i in range(13)]
        whole = jnp.concatenate(roped[:10], axis=1).astype(F32) * 0.125
        head_of = sublanes((32, QW))
        keep = lanes((32, QW)) // HEAD == head_of
        group = sublanes((32, 384))
        block = (lanes((32, 384)) // HEAD == group // 4) & (group < QUERY_HEADS)
        for j in range(SLOTS):
            placed = jnp.where(keep, jnp.broadcast_to(whole[j : j + 1], (32, QW)), 0.0)
            turned = jnp.dot(placed.astype(BF), spread[...], preferred_element_type=F32)
            query[j * 32 : (j + 1) * 32, :] = jnp.where(block, turned, 0.0).astype(BF)
        fresh_key[...] = jnp.concatenate(roped[10:13], axis=1).astype(F32)
        fresh_value[...] = jnp.concatenate(chunks[12:15], axis=1)
        counts = jnp.zeros((32, 128), F32)
        for i in range(8):
            entry = i * 128 + lanes((32, 128))
            live = entry < count_ref[0]
            upper = jnp.broadcast_to(index_rows[i] // 128, (32, 128)) == sublanes((32, 128))
            upper = (upper & live).astype(F32).astype(BF)
            lower = jnp.broadcast_to(index_rows[i] % 128, (128, 128)) == sublanes((128, 128))
            lower = lower.astype(F32).astype(BF)
            counts = counts + lax.dot_general(upper, lower, NT, preferred_element_type=F32)
        over[...] = counts

    index = jnp.concatenate(index_rows, axis=1)

    @pl.when(step == 0)
    def _():
        score = lax.dot_general(query[...], held_ref[:, :384], NT, preferred_element_type=F32)
        slot = sublanes((128, 1)) // 32
        length = jnp.zeros((128, 1), jnp.int32)
        for j in range(SLOTS):
            length = jnp.where(slot == j, length_ref[j], length)
        live = lanes((128, 1024)) < count_ref[0]
        live &= jnp.broadcast_to(index // POSITIONS, (128, 1024)) == slot
        live &= jnp.broadcast_to(index % POSITIONS, (128, 1024)) < length
        held_score[...] = jnp.where(live, score, NEG)

    @pl.when(step >= 0)
    def _():
        length = length_ref[step]
        part = pl.ds(pl.multiple_of(step * 32, 32), 32)
        queries = query[part, :]
        taken = over[pl.ds(pl.multiple_of(step * 8, 8), 8), :]
        taken = jnp.concatenate([taken[i : i + 1, :] for i in range(8)], axis=1)
        cache_live = (lanes((1, POSITIONS)) < length) & (taken < 0.5)
        cache_score = lax.dot_general(queries, cache_ref[:, :384], NT, preferred_element_type=F32)
        own_score = jnp.sum(
            queries.astype(F32) * fresh_key[pl.ds(step, 1), :], axis=-1, keepdims=True
        )
        cache_live = jnp.broadcast_to(cache_live, cache_score.shape)
        cache_score = jnp.where(cache_live, cache_score, NEG)
        kept_score = held_score[part, :]
        top = jnp.maximum(
            jnp.maximum(
                jnp.max(cache_score, axis=-1, keepdims=True),
                jnp.max(kept_score, axis=-1, keepdims=True),
            ),
            own_score,
        )
        cache_weight = jnp.where(cache_live, jnp.exp(cache_score - top), 0.0)
        kept_weight = jnp.where(kept_score > NEG, jnp.exp(kept_score - top), 0.0)
        own_weight = jnp.exp(own_score - top)
        total = (
            jnp.sum(cache_weight, axis=-1, keepdims=True)
            + jnp.sum(kept_weight, axis=-1, keepdims=True)
            + own_weight
        )
        held_weight[part, :] = kept_weight.astype(BF)
        mixed = jnp.dot(cache_weight.astype(BF), cache_ref[:, 256:], preferred_element_type=F32)
        mixed += own_weight.astype(BF).astype(F32) * fresh_value[pl.ds(step, 1), :]
        mixture[part, :] = mixed
        totals[part, :] = jnp.broadcast_to(total, (32, 128))

    @pl.when(step == SLOTS - 1)
    def _():
        mixed = mixture[...] + jnp.dot(
            held_weight[...], held_ref[:, 256:], preferred_element_type=F32
        )
        total = jnp.concatenate([totals[...]] * 3, axis=1)
        head = sublanes((128, 384)) % 32
        block = (lanes((128, 384)) // HEAD == head // 4 + 1) & (head < QUERY_HEADS)
        mixed = jnp.where(block, mixed / total, 0.0).astype(BF)
        turned = lax.dot_general(mixed, spread[...], NT, preferred_element_type=F32)
        keep = lanes((32, QW)) // HEAD == sublanes((32, QW))
        rows = [
            jnp.sum(jnp.where(keep, turned[j * 32 : (j + 1) * 32], 0.0), axis=0, keepdims=True)
            for j in range(SLOTS)
        ]
        result[:SLOTS, :] = jnp.concatenate(rows, axis=0)

    @pl.when(step == SLOTS - 1)
    def _():
        wanted = jnp.broadcast_to(slot_ref[...], (8, 256))
        slot = sublanes((8, 256))
        chosen = ((wanted == first_slot + slot) & (slot < SLOTS)).astype(F32).astype(BF)
        good = jnp.where(sublanes((8, QW)) < SLOTS, result[...], 0.0).astype(BF)
        out_ref[...] = lax.dot_general(
            chosen, good, (((0,), (0,)), ((), ())), preferred_element_type=F32
        ).astype(BF)


def decode_attention(
    device, length, count, slots, index, rows, gain, w_qkv, cache, hidden
):
    smem = pl.BlockSpec(memory_space=pltpu.SMEM)
    full = lambda shape: pl.BlockSpec(shape, lambda j: (0,) * len(shape))
    return pl.pallas_call(
        decode_kernel,
        out_shape=jax.ShapeDtypeStruct((256, QW), BF),
        grid=(2 * SLOTS,),
        in_specs=[
            smem,
            smem,
            smem,
            full((1, 256)),
            full((8, 128)),
            full((256, WIDTH)),
            full((WIDTH,)),
            pl.BlockSpec(
                (WIDTH, QW + KVW), lambda j: (0, 0), pipeline_mode=pl.Buffered(1)
            ),
            pl.BlockSpec((None, POSITIONS, KVW), lambda j: (jnp.maximum(j - SLOTS, 0), 0, 0)),
            pl.BlockSpec((256, WIDTH), lambda j: (jnp.minimum(j, SLOTS - 1), 0)),
        ],
        out_specs=full((256, QW)),
        scratch_shapes=[
            pltpu.VMEM((1024, KVW), BF),
            pltpu.VMEM((QW, 384), BF),
            pltpu.VMEM((128, 384), BF),
            pltpu.VMEM((8, 384), F32),
            pltpu.VMEM((8, 384), F32),
            pltpu.VMEM((32, 128), F32),
            pltpu.VMEM((8, QW), F32),
            pltpu.VMEM((128, 1024), F32),
            pltpu.VMEM((128, 1024), BF),
            pltpu.VMEM((128, 384), F32),
            pltpu.VMEM((128, 128), F32),
        ],
        compiler_params=pltpu.CompilerParams(vmem_limit_bytes=VMEM_LIMIT),
        cost_estimate=cost(17),
        name="decode",
    )(device, length, count, slots, index, rows, gain, w_qkv, cache, hidden)


def attention_kernel(
    rank_ref,
    query_ref,
    own_ref,
    core_ref,
    zed_ref,
    far_ref,
    w_ref,
    hidden_ref,
    gain_ref,
    resid_ref,
    lower_ref,
    upper_ref,
    total,
    mask,
):
    group = pl.program_id(0)

    @pl.when(group == 0)
    def _():
        total[...] = jnp.zeros_like(total)
        rank = rank_ref[0]
        row = sublanes((128, 128))
        col = lanes((128, 128))
        for piece in range(4):
            other = rank ^ piece
            bound = jnp.where(other <= rank, 0, 1)
            mask[:, piece * 128 : (piece + 1) * 128] = jnp.where(col + bound <= row, 0.0, NEG)

    pieces = [own_ref, core_ref, zed_ref, far_ref]
    keys = jnp.concatenate(
        [ref[h * 128 : (h + 1) * 128, :] for h in range(2) for ref in pieces], axis=0
    )
    low = lanes((1024, 128)) < HEAD
    wide = keys.astype(F32)
    values = jnp.where(low, pltpu.roll(wide, 64, 1), wide).astype(BF)
    values = jnp.concatenate([values, jnp.ones((1024, 128), BF)], axis=1)
    low = lanes((128, 128)) < HEAD
    blocked = mask[...]
    mixed = []
    for tile in range(2):
        heads = []
        for pair in range(2):
            two = query_ref[tile * 128 : (tile + 1) * 128, pair * 128 : (pair + 1) * 128].astype(F32)
            heads.append(jnp.where(low, two, 0.0).astype(BF))
            heads.append(jnp.where(low, pltpu.roll(two, 64, 1), 0.0).astype(BF))
        out = []
        for head in heads:
            count = 512 * (tile + 1)
            score = lax.dot_general(head, keys[:count], NT, preferred_element_type=F32)
            if tile == 0:
                score = score + blocked
            else:
                score = jnp.concatenate([score[:, :512], score[:, 512:] + blocked], axis=1)
            top = jnp.max(score, axis=-1, keepdims=True)
            weight = jnp.exp(score - top).astype(BF)
            both = jnp.dot(weight, values[:count], preferred_element_type=F32)
            out.append(both[:, :128] / both[:, 128:])
        mixed.append(
            jnp.concatenate(
                [jnp.where(low, out[0], out[1]), jnp.where(low, out[2], out[3])], axis=1
            ).astype(BF)
        )
    rows = jnp.concatenate(mixed, axis=0)
    total[...] += jnp.dot(rows, w_ref[...], preferred_element_type=F32)

    @pl.when(group == 4)
    def _():
        for part in range(2):
            cut = slice(part * 128, (part + 1) * 128)
            resid = (hidden_ref[cut, :].astype(F32) + total[cut, :]).astype(BF)
            resid_ref[cut, :] = resid
            (lower_ref, upper_ref)[part][...] = norm_rows(resid, gain_ref[...])


def attention(rank, query, own, core, zed, far, w_out, hidden, gain):
    full = lambda shape: pl.BlockSpec(shape, lambda g: (0,) * len(shape))
    side = pl.BlockSpec((ROWS, 128), lambda g: (0, g))
    return pl.pallas_call(
        attention_kernel,
        out_shape=(
            jax.ShapeDtypeStruct((ROWS, WIDTH), BF),
            jax.ShapeDtypeStruct((ROWS // 2, WIDTH), BF),
            jax.ShapeDtypeStruct((ROWS // 2, WIDTH), BF),
        ),
        grid=(5,),
        in_specs=[
            pl.BlockSpec(memory_space=pltpu.SMEM),
            pl.BlockSpec((ROWS, 256), lambda g: (0, g)),
            side,
            side,
            side,
            side,
            pl.BlockSpec((256, WIDTH), lambda g: (g, 0)),
            full((ROWS, WIDTH)),
            full((WIDTH,)),
        ],
        out_specs=(
            full((ROWS, WIDTH)),
            full((ROWS // 2, WIDTH)),
            full((ROWS // 2, WIDTH)),
        ),
        scratch_shapes=[
            pltpu.VMEM((ROWS, WIDTH), F32),
            pltpu.VMEM((128, 512), F32),
        ],
        compiler_params=pltpu.CompilerParams(vmem_limit_bytes=VMEM_LIMIT),
        cost_estimate=cost(0.1),
        name="attention",
    )(rank, query, own, core, zed, far, w_out, hidden, gain)


def decode_rows_kernel(back_ref, w_ref, decode_ref, gain_ref, resid_ref, normed_ref):
    mixed = jnp.sum(back_ref[...].astype(F32), axis=0)
    mixed = jnp.concatenate([mixed, jnp.zeros((14, WIDTH), F32)], axis=0).astype(BF)
    single = decode_ref[...].astype(F32)
    hidden = jnp.concatenate([single, jnp.zeros((14, WIDTH), F32)], axis=0)
    resid = (hidden + jnp.dot(mixed, w_ref[...], preferred_element_type=F32)).astype(BF)
    resid_ref[...] = resid
    normed_ref[...] = norm_rows(resid, gain_ref[...])


def decode_rows(back, w_out, decode, gain):
    vmem = pl.BlockSpec(memory_space=pltpu.VMEM)
    return pl.pallas_call(
        decode_rows_kernel,
        out_shape=(jax.ShapeDtypeStruct((16, WIDTH), BF),) * 2,
        in_specs=[vmem] * 4,
        out_specs=(vmem,) * 2,
        compiler_params=pltpu.CompilerParams(vmem_limit_bytes=VMEM_LIMIT),
        cost_estimate=cost(0.1),
        name="decode_rows",
    )(back, w_out, decode, gain)


def hidden_units(rows, packs, lows, highs, act):
    cut = 2 * SHARE - PART
    weights = [(ref[:SHARE, :], ref[SHARE : 2 * SHARE, :], ref[2 * SHARE :, :]) for ref in packs]
    for low, high in zip(lows, highs):
        up_rows = jnp.concatenate([low[SHARE:, :], high[:cut, :]], axis=0)
        weights.append((low[:SHARE, :], up_rows, high[cut:, :]))
    for k, (gate_rows, up_rows, _) in enumerate(weights):
        gate = lax.dot_general(rows, gate_rows, NT, preferred_element_type=F32)
        up = lax.dot_general(rows, up_rows, NT, preferred_element_type=F32)
        act[:, k * SHARE : (k + 1) * SHARE] = (gate / (1.0 + jnp.exp(-gate)) * up).astype(BF)
    down = jnp.concatenate([down_rows for _, _, down_rows in weights], axis=0)
    return jnp.dot(act[...], down, preferred_element_type=F32)


def first_kernel(*refs):
    rows = jnp.concatenate([refs[0][...], refs[1][...]], axis=0)
    refs[4][...] = hidden_units(rows, refs[2:4], (), (), refs[5])


def second_kernel(*refs):
    rows = jnp.concatenate([refs[0][...], refs[1][...]], axis=0)
    down = hidden_units(rows, refs[2:6], refs[6:8], refs[8:10], refs[13])
    refs[12][...] = refs[11][...].astype(F32) + (refs[10][...] + down)


def guest_kernel(*refs):
    rows = jnp.concatenate([ref[...] for ref in refs[:4]], axis=0)
    down = hidden_units(rows, refs[4:10], refs[10:12], refs[12:14], refs[17]).astype(BF)
    for ref, start, stop in zip(refs[14:17], (0, 144, 272), (144, 272, 288)):
        ref[...] = down[start:stop]


def feed_forward(kernel, inputs, outputs, rows, shares, time, name):
    vmem = pl.BlockSpec(memory_space=pltpu.VMEM)
    return pl.pallas_call(
        kernel,
        out_shape=outputs,
        in_specs=[vmem] * len(inputs),
        out_specs=(vmem,) * len(outputs),
        scratch_shapes=[pltpu.VMEM((rows, shares * SHARE), BF)],
        compiler_params=pltpu.CompilerParams(vmem_limit_bytes=VMEM_LIMIT),
        cost_estimate=cost(time),
        name=name,
    )(*inputs)


def final_kernel(start_ref, extra_ref, mine_ref, first_ref, second_ref, prefill_ref, decode_ref):
    for part, ref in ((0, first_ref), (1, second_ref)):
        cut = slice(part * 128, (part + 1) * 128)
        prefill_ref[cut, :] = (start_ref[cut, :] + ref[:128, :].astype(F32)).astype(BF)
    alone = mine_ref[...].astype(F32) + first_ref[128:, :].astype(F32)
    decode_ref[...] = (extra_ref[...].astype(F32) + alone)[:2].astype(BF)


def final_sum(start, extra, mine, first, second):
    return pl.pallas_call(
        final_kernel,
        out_shape=(
            jax.ShapeDtypeStruct((ROWS, WIDTH), BF),
            jax.ShapeDtypeStruct((2, WIDTH), BF),
        ),
        in_specs=[pl.BlockSpec(memory_space=pltpu.VMEM)] * 5,
        compiler_params=pltpu.CompilerParams(vmem_limit_bytes=VMEM_LIMIT),
        cost_estimate=cost(1),
        name="final",
    )(start, extra, mine, first, second)


def body(
    prefill_hidden,
    decode_hidden,
    attn_gain,
    w_qkv,
    w_out,
    ffn_gain,
    w_gate_up,
    w_down,
    key_value_cache,
    cache_len,
    slot_of_request,
    held_hidden,
    recomputed_index,
    recomp_count,
):
    device = lax.axis_index("req").astype(jnp.int32).reshape(1)
    rank = device % 4
    gain, gain2 = attn_gain, ffn_gain
    index = recomputed_index.reshape(8, 128)

    w_all = w_out
    w_qkv, w_out, key_value_cache, held_hidden, prefill_hidden = in_hbm(
        w_qkv, w_out, key_value_cache, held_hidden, prefill_hidden
    )
    total = 2 * SIDE**3
    spread = jnp.broadcast_to(decode_hidden[None], (total, 2, WIDTH))
    every_row = lax.all_to_all(spread, "req", 0, 0).reshape(256, WIDTH)

    packed = pack_weights(*in_hbm(jnp.swapaxes(w_gate_up, 1, 2), w_down))
    (kv,) = in_hbm(project(rank, prefill_hidden, gain, w_qkv, True))
    zed = send(kv, pair_z)
    core = send(kv, other_core)
    packed, kv = lax.optimization_barrier((packed, kv))
    below = send(packed, next_z)
    above = send(packed, last_z)
    packed_core = send(packed, other_core)
    (query,) = in_hbm(project(rank, prefill_hidden, gain, w_qkv, False))
    every_row, query = lax.optimization_barrier((every_row, query))
    outgoing = decode_attention(
        device,
        cache_len,
        recomp_count,
        slot_of_request.reshape(1, 256),
        index,
        every_row,
        gain,
        w_qkv,
        key_value_cache,
        held_hidden,
    )
    outgoing, zed, core, packed_core = lax.optimization_barrier(
        (outgoing, zed, core, packed_core)
    )
    far = send(zed, other_core)
    core, zed, far = in_hbm(core, zed, far)
    below, above, packed_core = lax.optimization_barrier((below, above, packed_core))
    far_low, far_high = cut_halves(below, above)
    far_low = send(far_low, next_z)
    far_high = send(far_high, last_z)
    back = lax.all_to_all(outgoing.reshape(total, 2, WIDTH), "req", 0, 0)

    resid, lower, upper = attention(
        rank, query, kv, core, zed, far, w_out, prefill_hidden, gain2
    )
    from_last = send(lower, next_x)
    from_next = send(upper, last_x)
    (mine,) = feed_forward(
        first_kernel,
        (lower, upper, packed, packed_core),
        (jax.ShapeDtypeStruct((ROWS, WIDTH), F32),),
        ROWS,
        2,
        0.1,
        "feed_first",
    )
    mine, back = lax.optimization_barrier((mine, back))
    below, above, back, from_last, from_next = lax.optimization_barrier(
        (below, above, back, from_last, from_next)
    )
    below_core = send(below, other_core)
    above_core = send(above, other_core)
    extra, alone = decode_rows(back, w_all, decode_hidden, gain2)
    guest = send(alone, next_x)
    alone, far_low, far_high = lax.optimization_barrier((alone, far_low, far_high))
    far_low_core = send(far_low, other_core)
    far_high_core = send(far_high, other_core)
    gathered = (below, below_core, above, above_core)
    distant = (far_low, far_low_core, far_high, far_high_core)
    to_last, to_next, alone = feed_forward(
        guest_kernel,
        (from_last, guest, from_next, alone, packed, packed_core) + gathered + distant,
        tuple(jax.ShapeDtypeStruct((n, WIDTH), BF) for n in (144, 128, 16)),
        ROWS + 32,
        8,
        8,
        "feed_guest",
    )
    to_last, to_next, mine = lax.optimization_barrier((to_last, to_next, mine))
    first = send(to_last, last_x)
    second = send(to_next, next_x)
    (start,) = feed_forward(
        second_kernel,
        (lower, upper) + gathered + distant + (mine, resid),
        (jax.ShapeDtypeStruct((ROWS, WIDTH), F32),),
        ROWS,
        6,
        6,
        "feed_second",
    )
    return final_sum(start, extra, alone, first, second)


def solution(mesh):
    return jax.shard_map(
        body,
        mesh=mesh,
        in_specs=(
            P("req", None),
            P("req", None),
            P(),
            P(),
            P(),
            P(),
            P("req", None, None),
            P("req", None, None),
            P("req", None, None),
            P("req"),
            P(),
            P("req", None),
            P("req"),
            P("req"),
        ),
        out_specs=(P("req", None), P("req", None)),
        check_vma=False,
    )
```

```python
import functools

import jax
import jax.numpy as jnp
import numpy as np
from jax import lax
from jax.experimental import pallas as pl
from jax.experimental.pallas import tpu as pltpu
from jax.sharding import PartitionSpec as P

WIDTH = 1280
QUERY_HEADS = 20
HEAD = 64
QW = 1280
KVW = 640
SHARE = 224
PART = 3 * SHARE // 2
GROUP = 16
SIDE = 4
SLOTS = 4
POSITIONS = 1024
ROWS = 256
EPS = 1e-05
THETA = 10000.0
NEG = -1e30
F32 = jnp.float32
BF = jnp.bfloat16
NT = (((1,), (1,)), ((), ()))
VMEM_LIMIT = 24 << 20


def cost(microseconds):
    return pl.CostEstimate(
        flops=int(microseconds * 10**9), transcendentals=0, bytes_accessed=int(microseconds * 3000000)
    )


def place(y, x, z, core):
    return (((y % SIDE) * SIDE + x % SIDE) * SIDE + z % SIDE) * 2 + core


def moves(step):
    pairs = []
    for y in range(SIDE):
        for x in range(SIDE):
            for z in range(SIDE):
                for core in range(2):
                    pairs.append((place(y, x, z, core), place(*step(y, x, z, core))))
    return pairs


def send(array, step):
    return lax.ppermute(array, "req", moves(step))


def in_hbm(*arrays):
    return [pltpu.with_memory_space_constraint(a, pltpu.MemorySpace.HBM) for a in arrays]


def other_core(y, x, z, core):
    return y, x, z, 1 - core


def next_x(y, x, z, core):
    return y, x + 1, z, core


def last_x(y, x, z, core):
    return y, x - 1, z, core


def next_z(y, x, z, core):
    return y, x, z + 1, core


def last_z(y, x, z, core):
    return y, x, z - 1, core


def pair_z(y, x, z, core):
    return y, x, z ^ 1, core


def norm_rows(rows, gain):
    rows = rows.astype(F32)
    mean = jnp.mean(rows * rows, axis=-1, keepdims=True)
    return (rows * lax.rsqrt(mean + EPS) * gain.reshape(1, WIDTH)).astype(BF)


def lanes(shape):
    return lax.broadcasted_iota(jnp.int32, shape, len(shape) - 1)


def sublanes(shape):
    return lax.broadcasted_iota(jnp.int32, shape, len(shape) - 2)


def sine_cosine(angle):
    turns = jnp.floor(angle * (2.0 / np.pi) + 0.5)
    rest = angle - turns * 1.5703125
    rest = rest - turns * 4.837512969970703125e-4
    rest = rest - turns * 7.54978995489188216e-8
    square = rest * rest
    sine = 8.3321608736e-3 + square * -1.9515295891e-4
    sine = rest + rest * square * (-1.6666654611e-1 + square * sine)
    cosine = -1.388731625493765e-3 + square * 2.443315711809948e-5
    cosine = 4.166664568298827e-2 + square * cosine
    cosine = 1.0 - 0.5 * square + square * square * cosine
    quarter = turns.astype(jnp.int32) & 3
    odd = (quarter & 1) == 1
    out_sine = jnp.where(odd, cosine, sine)
    out_cosine = jnp.where(odd, sine, cosine)
    out_sine = jnp.where(quarter >= 2, -out_sine, out_sine)
    out_cosine = jnp.where((quarter == 1) | (quarter == 2), -out_cosine, out_cosine)
    return out_sine, out_cosine


def rope_tables(position):
    pair = (lanes((1, position.shape[1])) % (HEAD // 2)).astype(F32)
    frequency = jnp.exp(pair * (-2.0 * np.log(THETA) / HEAD))
    sine, cosine = sine_cosine(position * frequency)
    low = lanes(sine.shape) % HEAD < HEAD // 2
    return cosine, jnp.where(low, -sine, sine)


def rope(chunk, cosine, sine):
    low = lanes(chunk.shape) % HEAD < HEAD // 2
    other = jnp.where(low, pltpu.roll(chunk, 96, 1), pltpu.roll(chunk, 32, 1))
    return chunk * cosine + other * sine


def pack_kernel(gate_up_ref, down_ref, packed_ref):
    packed_ref[: 2 * SHARE, :] = gate_up_ref[...]
    packed_ref[2 * SHARE :, :] = down_ref[...]


def pack_weights(gate_up, down):
    return pl.pallas_call(
        pack_kernel,
        out_shape=jax.ShapeDtypeStruct((3 * SHARE, WIDTH), BF),
        grid=(2,),
        in_specs=[
            pl.BlockSpec((None, 2 * SHARE, WIDTH // 2), lambda i: (0, 0, i)),
            pl.BlockSpec((None, SHARE, WIDTH // 2), lambda i: (0, 0, i)),
        ],
        out_specs=pl.BlockSpec((3 * SHARE, WIDTH // 2), lambda i: (0, i)),
        compiler_params=pltpu.CompilerParams(vmem_limit_bytes=VMEM_LIMIT),
        cost_estimate=cost(1.5),
        name="pack",
    )(gate_up, down)


def cut_kernel(below_ref, above_ref, low_ref, high_ref):
    low_ref[...] = below_ref[:PART, :]
    high_ref[...] = above_ref[PART:, :]


def cut_halves(below, above):
    vmem = pl.BlockSpec(memory_space=pltpu.VMEM)
    return pl.pallas_call(
        cut_kernel,
        out_shape=(jax.ShapeDtypeStruct((PART, WIDTH), BF),) * 2,
        in_specs=[vmem] * 2,
        out_specs=(vmem,) * 2,
        compiler_params=pltpu.CompilerParams(vmem_limit_bytes=VMEM_LIMIT),
        cost_estimate=cost(0.5),
        name="cut",
    )(below, above)


def kv_kernel(rank_ref, hidden_ref, gain_ref, w_ref, kv_ref):
    normed = norm_rows(hidden_ref[...], gain_ref[...])
    position = (sublanes((ROWS, 128)) * 4 + rank_ref[0]).astype(F32)
    cosine, sine = rope_tables(position)
    projected = jnp.dot(normed, w_ref[...], preferred_element_type=F32)
    chunks = [projected[:, i * 128 : (i + 1) * 128] for i in range(5)]
    low = lanes((ROWS, 128)) < HEAD
    first = rope(chunks[0], cosine, sine)
    second = rope(chunks[1], cosine, sine)
    third = jnp.where(low, rope(chunks[2], cosine, sine), chunks[2])
    swap = lambda value: pltpu.roll(value, 64, 1)
    out = [
        jnp.where(low, first, third),
        jnp.where(low, swap(first), swap(chunks[3])),
        jnp.where(low, second, chunks[3]),
        jnp.where(low, swap(second), swap(chunks[4])),
        jnp.where(low, third, chunks[4]),
    ]
    for i in range(5):
        kv_ref[:, i * 128 : (i + 1) * 128] = out[i].astype(BF)


def query_kernel(rank_ref, hidden_ref, gain_ref, w_ref, query_ref, normed, cos, sin):
    @pl.when(pl.program_id(0) == 0)
    def _():
        normed[...] = norm_rows(hidden_ref[...], gain_ref[...])
        position = (sublanes((ROWS, 128)) * 4 + rank_ref[0]).astype(F32)
        cos[...], sin[...] = rope_tables(position)

    projected = jnp.dot(normed[...], w_ref[...], preferred_element_type=F32)
    for i in range(5):
        roped = rope(projected[:, i * 128 : (i + 1) * 128], cos[...], sin[...]).astype(BF)
        query_ref[:, i * 128 : (i + 1) * 128] = roped * jnp.asarray(0.125, BF)


def project(rank, hidden, gain, w_qkv, keys):
    steps = 1 if keys else 2
    scratch = [
        pltpu.VMEM((ROWS, WIDTH), BF),
        pltpu.VMEM((ROWS, 128), F32),
        pltpu.VMEM((ROWS, 128), F32),
    ]
    return pl.pallas_call(
        kv_kernel if keys else query_kernel,
        out_shape=jax.ShapeDtypeStruct((ROWS, KVW * steps), BF),
        grid=(steps,),
        in_specs=[
            pl.BlockSpec(memory_space=pltpu.SMEM),
            pl.BlockSpec((ROWS, WIDTH), lambda j: (0, 0)),
            pl.BlockSpec((WIDTH,), lambda j: (0,)),
            pl.BlockSpec((WIDTH, KVW), (lambda j: (0, 2)) if keys else (lambda j: (0, j))),
        ],
        out_specs=pl.BlockSpec((ROWS, KVW), lambda j: (0, j)),
        scratch_shapes=[] if keys else scratch,
        compiler_params=pltpu.CompilerParams(vmem_limit_bytes=VMEM_LIMIT),
        cost_estimate=cost(3 if keys else 0.1),
        name="prefill_kv" if keys else "prefill_query",
    )(rank, hidden, gain, w_qkv)


def column(row):
    return jnp.broadcast_to(row, (128, 128)).T


def decode_kernel(
    device_ref,
    length_ref,
    count_ref,
    slot_ref,
    index_ref,
    rows_ref,
    gain_ref,
    w_ref,
    cache_ref,
    hidden_ref,
    out_ref,
    held_ref,
    spread,
    query,
    fresh_key,
    fresh_value,
    over,
    result,
    held_score,
    held_weight,
    mixture,
    totals,
):
    tick = pl.program_id(0)
    step = tick - SLOTS
    first_slot = device_ref[0] * SLOTS

    @pl.when(tick < SLOTS)
    def _():
        normed = norm_rows(hidden_ref[...], gain_ref[...])
        projected = jnp.dot(normed, w_ref[:, QW:], preferred_element_type=F32)
        position = (index_ref[pl.ds(tick * 2, 2), :] % POSITIONS).astype(F32)
        position = jnp.concatenate([column(position[0:1]), column(position[1:2])], axis=0)
        cosine, sine = rope_tables(position)
        low = lanes((256, 128)) < HEAD
        rows = pl.ds(pl.multiple_of(tick * 256, 256), 256)
        for i in range(5):
            chunk = projected[:, i * 128 : (i + 1) * 128]
            if i < 2:
                chunk = rope(chunk, cosine, sine)
            elif i == 2:
                chunk = jnp.where(low, rope(chunk, cosine, sine), chunk)
            held_ref[rows, i * 128 : (i + 1) * 128] = chunk.astype(BF)

    index_rows = [index_ref[i : i + 1, :] for i in range(8)]

    def chosen(k):
        wanted = jnp.broadcast_to(slot_ref[k : k + 1, :], (8, 128))
        slot = sublanes((8, 128))
        return ((wanted == first_slot + slot) & (slot < SLOTS)).astype(F32).astype(BF)

    @pl.when(step == 0)
    def _():
        spread[...] = (
            sublanes((QW, 384)) % HEAD == lanes((QW, 384)) % HEAD
        ).astype(F32).astype(BF)
        rows = jnp.dot(chosen(0), rows_ref[:, 0, :], preferred_element_type=F32)
        rows += jnp.dot(chosen(1), rows_ref[:, 1, :], preferred_element_type=F32)
        normed = norm_rows(rows, gain_ref[...])
        projected = jnp.dot(normed, w_ref[...], preferred_element_type=F32)
        projected = projected.astype(BF).astype(F32)
        row = sublanes((8, 128))
        position = jnp.zeros((8, 128), F32)
        for j in range(SLOTS):
            position = jnp.where(row == j, length_ref[j].astype(F32), position)
        cosine, sine = rope_tables(position)
        chunks = [projected[:, i * 128 : (i + 1) * 128] for i in range(15)]
        roped = [rope(chunks[i], cosine, sine).astype(BF) for i in range(13)]
        whole = jnp.concatenate(roped[:10], axis=1).astype(F32) * 0.125
        head_of = sublanes((32, QW))
        keep = lanes((32, QW)) // HEAD == head_of
        group = sublanes((32, 384))
        block = (lanes((32, 384)) // HEAD == group // 4) & (group < QUERY_HEADS)
        for j in range(SLOTS):
            placed = jnp.where(keep, jnp.broadcast_to(whole[j : j + 1], (32, QW)), 0.0)
            turned = jnp.dot(placed.astype(BF), spread[...], preferred_element_type=F32)
            query[j * 32 : (j + 1) * 32, :] = jnp.where(block, turned, 0.0).astype(BF)
        fresh_key[...] = jnp.concatenate(roped[10:13], axis=1).astype(F32)
        fresh_value[...] = jnp.concatenate(chunks[12:15], axis=1)
        counts = jnp.zeros((32, 128), F32)
        for i in range(8):
            entry = i * 128 + lanes((32, 128))
            live = entry < count_ref[0]
            upper = jnp.broadcast_to(index_rows[i] // 128, (32, 128)) == sublanes((32, 128))
            upper = (upper & live).astype(F32).astype(BF)
            lower = jnp.broadcast_to(index_rows[i] % 128, (128, 128)) == sublanes((128, 128))
            lower = lower.astype(F32).astype(BF)
            counts = counts + lax.dot_general(upper, lower, NT, preferred_element_type=F32)
        over[...] = counts

    index = jnp.concatenate(index_rows, axis=1)

    @pl.when(step == 0)
    def _():
        score = lax.dot_general(query[...], held_ref[:, :384], NT, preferred_element_type=F32)
        slot = sublanes((128, 1)) // 32
        length = jnp.zeros((128, 1), jnp.int32)
        for j in range(SLOTS):
            length = jnp.where(slot == j, length_ref[j], length)
        live = lanes((128, 1024)) < count_ref[0]
        live &= jnp.broadcast_to(index // POSITIONS, (128, 1024)) == slot
        live &= jnp.broadcast_to(index % POSITIONS, (128, 1024)) < length
        held_score[...] = jnp.where(live, score, NEG)

    @pl.when(step >= 0)
    def _():
        length = length_ref[step]
        part = pl.ds(pl.multiple_of(step * 32, 32), 32)
        queries = query[part, :]
        taken = over[pl.ds(pl.multiple_of(step * 8, 8), 8), :]
        taken = jnp.concatenate([taken[i : i + 1, :] for i in range(8)], axis=1)
        cache_live = (lanes((1, POSITIONS)) < length) & (taken < 0.5)
        cache_score = lax.dot_general(queries, cache_ref[:, :384], NT, preferred_element_type=F32)
        own_score = jnp.sum(
            queries.astype(F32) * fresh_key[pl.ds(step, 1), :], axis=-1, keepdims=True
        )
        cache_live = jnp.broadcast_to(cache_live, cache_score.shape)
        cache_score = jnp.where(cache_live, cache_score, NEG)
        kept_score = held_score[part, :]
        top = jnp.maximum(
            jnp.maximum(
                jnp.max(cache_score, axis=-1, keepdims=True),
                jnp.max(kept_score, axis=-1, keepdims=True),
            ),
            own_score,
        )
        cache_weight = jnp.where(cache_live, jnp.exp(cache_score - top), 0.0)
        kept_weight = jnp.where(kept_score > NEG, jnp.exp(kept_score - top), 0.0)
        own_weight = jnp.exp(own_score - top)
        total = (
            jnp.sum(cache_weight, axis=-1, keepdims=True)
            + jnp.sum(kept_weight, axis=-1, keepdims=True)
            + own_weight
        )
        held_weight[part, :] = kept_weight.astype(BF)
        mixed = jnp.dot(cache_weight.astype(BF), cache_ref[:, 256:], preferred_element_type=F32)
        mixed += own_weight.astype(BF).astype(F32) * fresh_value[pl.ds(step, 1), :]
        mixture[part, :] = mixed
        totals[part, :] = jnp.broadcast_to(total, (32, 128))

    @pl.when(step == SLOTS - 1)
    def _():
        mixed = mixture[...] + jnp.dot(
            held_weight[...], held_ref[:, 256:], preferred_element_type=F32
        )
        total = jnp.concatenate([totals[...]] * 3, axis=1)
        head = sublanes((128, 384)) % 32
        block = (lanes((128, 384)) // HEAD == head // 4 + 1) & (head < QUERY_HEADS)
        mixed = jnp.where(block, mixed / total, 0.0).astype(BF)
        turned = lax.dot_general(mixed, spread[...], NT, preferred_element_type=F32)
        keep = lanes((32, QW)) // HEAD == sublanes((32, QW))
        rows = [
            jnp.sum(jnp.where(keep, turned[j * 32 : (j + 1) * 32], 0.0), axis=0, keepdims=True)
            for j in range(SLOTS)
        ]
        result[:SLOTS, :] = jnp.concatenate(rows, axis=0)

    @pl.when(step == SLOTS - 1)
    def _():
        good = jnp.where(sublanes((8, QW)) < SLOTS, result[...], 0.0).astype(BF)
        for k in range(2):
            out_ref[:, k, :] = lax.dot_general(
                chosen(k), good, (((0,), (0,)), ((), ())), preferred_element_type=F32
            ).astype(BF)


def decode_attention(
    device, length, count, slots, index, rows, gain, w_qkv, cache, hidden
):
    smem = pl.BlockSpec(memory_space=pltpu.SMEM)
    full = lambda shape: pl.BlockSpec(shape, lambda j: (0,) * len(shape))
    return pl.pallas_call(
        decode_kernel,
        out_shape=jax.ShapeDtypeStruct((128, 2, QW), BF),
        grid=(2 * SLOTS,),
        in_specs=[
            smem,
            smem,
            smem,
            full((2, 128)),
            full((8, 128)),
            full((128, 2, WIDTH)),
            full((WIDTH,)),
            pl.BlockSpec(
                (WIDTH, QW + KVW), lambda j: (0, 0), pipeline_mode=pl.Buffered(1)
            ),
            pl.BlockSpec((None, POSITIONS, KVW), lambda j: (jnp.maximum(j - SLOTS, 0), 0, 0)),
            pl.BlockSpec((256, WIDTH), lambda j: (jnp.minimum(j, SLOTS - 1), 0)),
        ],
        out_specs=full((128, 2, QW)),
        scratch_shapes=[
            pltpu.VMEM((1024, KVW), BF),
            pltpu.VMEM((QW, 384), BF),
            pltpu.VMEM((128, 384), BF),
            pltpu.VMEM((8, 384), F32),
            pltpu.VMEM((8, 384), F32),
            pltpu.VMEM((32, 128), F32),
            pltpu.VMEM((8, QW), F32),
            pltpu.VMEM((128, 1024), F32),
            pltpu.VMEM((128, 1024), BF),
            pltpu.VMEM((128, 384), F32),
            pltpu.VMEM((128, 128), F32),
        ],
        compiler_params=pltpu.CompilerParams(vmem_limit_bytes=VMEM_LIMIT),
        cost_estimate=cost(17),
        name="decode",
    )(device, length, count, slots, index, rows, gain, w_qkv, cache, hidden)


def attention_kernel(
    rank_ref,
    query_ref,
    own_ref,
    core_ref,
    zed_ref,
    far_ref,
    w_ref,
    hidden_ref,
    gain_ref,
    resid_ref,
    lower_ref,
    upper_ref,
    total,
    mask,
):
    group = pl.program_id(0)

    @pl.when(group == 0)
    def _():
        total[...] = jnp.zeros_like(total)
        rank = rank_ref[0]
        row = sublanes((128, 128))
        col = lanes((128, 128))
        for piece in range(4):
            other = rank ^ piece
            bound = jnp.where(other <= rank, 0, 1)
            mask[:, piece * 128 : (piece + 1) * 128] = jnp.where(col + bound <= row, 0.0, NEG)

    pieces = [own_ref, core_ref, zed_ref, far_ref]
    keys = jnp.concatenate(
        [ref[h * 128 : (h + 1) * 128, :] for h in range(2) for ref in pieces], axis=0
    )
    low = lanes((1024, 128)) < HEAD
    wide = keys.astype(F32)
    values = jnp.where(low, pltpu.roll(wide, 64, 1), wide).astype(BF)
    values = jnp.concatenate([values, jnp.ones((1024, 128), BF)], axis=1)
    low = lanes((128, 128)) < HEAD
    blocked = mask[...]
    mixed = []
    for tile in range(2):
        heads = []
        for pair in range(2):
            two = query_ref[tile * 128 : (tile + 1) * 128, pair * 128 : (pair + 1) * 128].astype(F32)
            heads.append(jnp.where(low, two, 0.0).astype(BF))
            heads.append(jnp.where(low, pltpu.roll(two, 64, 1), 0.0).astype(BF))
        out = []
        for head in heads:
            count = 512 * (tile + 1)
            score = lax.dot_general(head, keys[:count], NT, preferred_element_type=F32)
            if tile == 0:
                score = score + blocked
            else:
                score = jnp.concatenate([score[:, :512], score[:, 512:] + blocked], axis=1)
            top = jnp.max(score, axis=-1, keepdims=True)
            weight = jnp.exp(score - top).astype(BF)
            both = jnp.dot(weight, values[:count], preferred_element_type=F32)
            out.append(both[:, :128] / both[:, 128:])
        mixed.append(
            jnp.concatenate(
                [jnp.where(low, out[0], out[1]), jnp.where(low, out[2], out[3])], axis=1
            ).astype(BF)
        )
    rows = jnp.concatenate(mixed, axis=0)
    total[...] += jnp.dot(rows, w_ref[...], preferred_element_type=F32)

    @pl.when(group == 4)
    def _():
        for part in range(2):
            cut = slice(part * 128, (part + 1) * 128)
            resid = (hidden_ref[cut, :].astype(F32) + total[cut, :]).astype(BF)
            resid_ref[cut, :] = resid
            (lower_ref, upper_ref)[part][...] = norm_rows(resid, gain_ref[...])


def attention(rank, query, own, core, zed, far, w_out, hidden, gain):
    full = lambda shape: pl.BlockSpec(shape, lambda g: (0,) * len(shape))
    side = pl.BlockSpec((ROWS, 128), lambda g: (0, g))
    return pl.pallas_call(
        attention_kernel,
        out_shape=(
            jax.ShapeDtypeStruct((ROWS, WIDTH), BF),
            jax.ShapeDtypeStruct((ROWS // 2, WIDTH), BF),
            jax.ShapeDtypeStruct((ROWS // 2, WIDTH), BF),
        ),
        grid=(5,),
        in_specs=[
            pl.BlockSpec(memory_space=pltpu.SMEM),
            pl.BlockSpec((ROWS, 256), lambda g: (0, g)),
            side,
            side,
            side,
            side,
            pl.BlockSpec((256, WIDTH), lambda g: (g, 0)),
            full((ROWS, WIDTH)),
            full((WIDTH,)),
        ],
        out_specs=(
            full((ROWS, WIDTH)),
            full((ROWS // 2, WIDTH)),
            full((ROWS // 2, WIDTH)),
        ),
        scratch_shapes=[
            pltpu.VMEM((ROWS, WIDTH), F32),
            pltpu.VMEM((128, 512), F32),
        ],
        compiler_params=pltpu.CompilerParams(vmem_limit_bytes=VMEM_LIMIT),
        cost_estimate=cost(0.1),
        name="attention",
    )(rank, query, own, core, zed, far, w_out, hidden, gain)


def decode_rows_kernel(back_ref, w_ref, decode_ref, gain_ref, resid_ref, normed_ref):
    mixed = jnp.sum(back_ref[...].astype(F32), axis=0)
    mixed = jnp.concatenate([mixed, jnp.zeros((14, WIDTH), F32)], axis=0).astype(BF)
    single = decode_ref[...].astype(F32)
    hidden = jnp.concatenate([single, jnp.zeros((14, WIDTH), F32)], axis=0)
    resid = (hidden + jnp.dot(mixed, w_ref[...], preferred_element_type=F32)).astype(BF)
    resid_ref[...] = resid
    normed_ref[...] = norm_rows(resid, gain_ref[...])


def decode_rows(back, w_out, decode, gain):
    vmem = pl.BlockSpec(memory_space=pltpu.VMEM)
    return pl.pallas_call(
        decode_rows_kernel,
        out_shape=(jax.ShapeDtypeStruct((16, WIDTH), BF),) * 2,
        in_specs=[vmem] * 4,
        out_specs=(vmem,) * 2,
        compiler_params=pltpu.CompilerParams(vmem_limit_bytes=VMEM_LIMIT),
        cost_estimate=cost(0.1),
        name="decode_rows",
    )(back, w_out, decode, gain)


def hidden_units(rows, packs, lows, highs, act):
    cut = 2 * SHARE - PART
    weights = [(ref[:SHARE, :], ref[SHARE : 2 * SHARE, :], ref[2 * SHARE :, :]) for ref in packs]
    for low, high in zip(lows, highs):
        up_rows = jnp.concatenate([low[SHARE:, :], high[:cut, :]], axis=0)
        weights.append((low[:SHARE, :], up_rows, high[cut:, :]))
    for k, (gate_rows, up_rows, _) in enumerate(weights):
        gate = lax.dot_general(rows, gate_rows, NT, preferred_element_type=F32)
        up = lax.dot_general(rows, up_rows, NT, preferred_element_type=F32)
        act[:, k * SHARE : (k + 1) * SHARE] = (gate / (1.0 + jnp.exp(-gate)) * up).astype(BF)
    down = jnp.concatenate([down_rows for _, _, down_rows in weights], axis=0)
    return jnp.dot(act[...], down, preferred_element_type=F32)


def first_kernel(*refs):
    rows = jnp.concatenate([refs[0][...], refs[1][...]], axis=0)
    refs[4][...] = hidden_units(rows, refs[2:4], (), (), refs[5])


def second_kernel(*refs):
    rows = jnp.concatenate([refs[0][...], refs[1][...]], axis=0)
    down = hidden_units(rows, refs[2:6], refs[6:8], refs[8:10], refs[13])
    refs[12][...] = refs[11][...].astype(F32) + (refs[10][...] + down)


def guest_kernel(*refs):
    rows = jnp.concatenate([ref[...] for ref in refs[:4]], axis=0)
    down = hidden_units(rows, refs[4:10], refs[10:12], refs[12:14], refs[17]).astype(BF)
    for ref, start, stop in zip(refs[14:17], (0, 144, 272), (144, 272, 288)):
        ref[...] = down[start:stop]


def feed_forward(kernel, inputs, outputs, rows, shares, time, name):
    vmem = pl.BlockSpec(memory_space=pltpu.VMEM)
    return pl.pallas_call(
        kernel,
        out_shape=outputs,
        in_specs=[vmem] * len(inputs),
        out_specs=(vmem,) * len(outputs),
        scratch_shapes=[pltpu.VMEM((rows, shares * SHARE), BF)],
        compiler_params=pltpu.CompilerParams(vmem_limit_bytes=VMEM_LIMIT),
        cost_estimate=cost(time),
        name=name,
    )(*inputs)


def final_kernel(start_ref, extra_ref, mine_ref, first_ref, second_ref, prefill_ref, decode_ref):
    for part, ref in ((0, first_ref), (1, second_ref)):
        cut = slice(part * 128, (part + 1) * 128)
        prefill_ref[cut, :] = (start_ref[cut, :] + ref[:128, :].astype(F32)).astype(BF)
    alone = mine_ref[...].astype(F32) + first_ref[128:, :].astype(F32)
    decode_ref[...] = (extra_ref[...].astype(F32) + alone)[:2].astype(BF)


def final_sum(start, extra, mine, first, second):
    return pl.pallas_call(
        final_kernel,
        out_shape=(
            jax.ShapeDtypeStruct((ROWS, WIDTH), BF),
            jax.ShapeDtypeStruct((2, WIDTH), BF),
        ),
        in_specs=[pl.BlockSpec(memory_space=pltpu.VMEM)] * 5,
        compiler_params=pltpu.CompilerParams(vmem_limit_bytes=VMEM_LIMIT),
        cost_estimate=cost(1),
        name="final",
    )(start, extra, mine, first, second)


def body(
    prefill_hidden,
    decode_hidden,
    attn_gain,
    w_qkv,
    w_out,
    ffn_gain,
    w_gate_up,
    w_down,
    key_value_cache,
    cache_len,
    slot_of_request,
    held_hidden,
    recomputed_index,
    recomp_count,
):
    device = lax.axis_index("req").astype(jnp.int32).reshape(1)
    rank = device % 4
    gain, gain2 = attn_gain, ffn_gain
    index = recomputed_index.reshape(8, 128)

    w_all = w_out
    w_qkv, w_out, key_value_cache, held_hidden, prefill_hidden = in_hbm(
        w_qkv, w_out, key_value_cache, held_hidden, prefill_hidden
    )
    total = 2 * SIDE**3
    spread = jnp.broadcast_to(decode_hidden[None], (total, 2, WIDTH))
    every_row = lax.all_to_all(spread, "req", 0, 0)

    packed = pack_weights(*in_hbm(jnp.swapaxes(w_gate_up, 1, 2), w_down))
    (kv,) = in_hbm(project(rank, prefill_hidden, gain, w_qkv, True))
    zed = send(kv, pair_z)
    core = send(kv, other_core)
    packed, kv = lax.optimization_barrier((packed, kv))
    below = send(packed, next_z)
    above = send(packed, last_z)
    packed_core = send(packed, other_core)
    (query,) = in_hbm(project(rank, prefill_hidden, gain, w_qkv, False))
    every_row, query = lax.optimization_barrier((every_row, query))
    outgoing = decode_attention(
        device,
        cache_len,
        recomp_count,
        slot_of_request.reshape(128, 2).T,
        index,
        every_row,
        gain,
        w_qkv,
        key_value_cache,
        held_hidden,
    )
    outgoing, zed, core, packed_core = lax.optimization_barrier(
        (outgoing, zed, core, packed_core)
    )
    far = send(zed, other_core)
    core, zed, far = in_hbm(core, zed, far)
    below, above, packed_core = lax.optimization_barrier((below, above, packed_core))
    far_low, far_high = cut_halves(below, above)
    far_low = send(far_low, next_z)
    far_high = send(far_high, last_z)
    back = lax.all_to_all(outgoing, "req", 0, 0)

    resid, lower, upper = attention(
        rank, query, kv, core, zed, far, w_out, prefill_hidden, gain2
    )
    from_last = send(lower, next_x)
    from_next = send(upper, last_x)
    (mine,) = feed_forward(
        first_kernel,
        (lower, upper, packed, packed_core),
        (jax.ShapeDtypeStruct((ROWS, WIDTH), F32),),
        ROWS,
        2,
        0.1,
        "feed_first",
    )
    mine, back = lax.optimization_barrier((mine, back))
    below, above, back, from_last, from_next = lax.optimization_barrier(
        (below, above, back, from_last, from_next)
    )
    below_core = send(below, other_core)
    above_core = send(above, other_core)
    extra, alone = decode_rows(back, w_all, decode_hidden, gain2)
    guest = send(alone, next_x)
    alone, far_low, far_high = lax.optimization_barrier((alone, far_low, far_high))
    far_low_core = send(far_low, other_core)
    far_high_core = send(far_high, other_core)
    gathered = (below, below_core, above, above_core)
    distant = (far_low, far_low_core, far_high, far_high_core)
    to_last, to_next, alone = feed_forward(
        guest_kernel,
        (from_last, guest, from_next, alone, packed, packed_core) + gathered + distant,
        tuple(jax.ShapeDtypeStruct((n, WIDTH), BF) for n in (144, 128, 16)),
        ROWS + 32,
        8,
        8,
        "feed_guest",
    )
    to_last, to_next, mine = lax.optimization_barrier((to_last, to_next, mine))
    first = send(to_last, last_x)
    second = send(to_next, next_x)
    (start,) = feed_forward(
        second_kernel,
        (lower, upper) + gathered + distant + (mine, resid),
        (jax.ShapeDtypeStruct((ROWS, WIDTH), F32),),
        ROWS,
        6,
        6,
        "feed_second",
    )
    return final_sum(start, extra, alone, first, second)


def solution(mesh):
    return jax.shard_map(
        body,
        mesh=mesh,
        in_specs=(
            P("req", None),
            P("req", None),
            P(),
            P(),
            P(),
            P(),
            P("req", None, None),
            P("req", None, None),
            P("req", None, None),
            P("req"),
            P(),
            P("req", None),
            P("req"),
            P("req"),
        ),
        out_specs=(P("req", None), P("req", None)),
        check_vma=False,
    )
```

```python
import functools

import jax
import jax.numpy as jnp
import numpy as np
from jax import lax
from jax.experimental import pallas as pl
from jax.experimental.pallas import tpu as pltpu
from jax.sharding import PartitionSpec as P

WIDTH = 1280
QUERY_HEADS = 20
HEAD = 64
QW = 1280
KVW = 640
SHARE = 224
PART = 3 * SHARE // 2
GROUP = 16
SIDE = 4
SLOTS = 4
POSITIONS = 1024
ROWS = 256
EPS = 1e-05
THETA = 10000.0
NEG = -1e30
F32 = jnp.float32
BF = jnp.bfloat16
NT = (((1,), (1,)), ((), ()))
VMEM_LIMIT = 24 << 20


def cost(microseconds):
    return pl.CostEstimate(
        flops=int(microseconds * 10**9), transcendentals=0, bytes_accessed=int(microseconds * 3000000)
    )


def place(y, x, z, core):
    return (((y % SIDE) * SIDE + x % SIDE) * SIDE + z % SIDE) * 2 + core


def moves(step):
    pairs = []
    for y in range(SIDE):
        for x in range(SIDE):
            for z in range(SIDE):
                for core in range(2):
                    pairs.append((place(y, x, z, core), place(*step(y, x, z, core))))
    return pairs


def send(array, step):
    return lax.ppermute(array, "req", moves(step))


def in_hbm(*arrays):
    return [pltpu.with_memory_space_constraint(a, pltpu.MemorySpace.HBM) for a in arrays]


def other_core(y, x, z, core):
    return y, x, z, 1 - core


def next_x(y, x, z, core):
    return y, x + 1, z, core


def last_x(y, x, z, core):
    return y, x - 1, z, core


def next_z(y, x, z, core):
    return y, x, z + 1, core


def last_z(y, x, z, core):
    return y, x, z - 1, core


def pair_z(y, x, z, core):
    return y, x, z ^ 1, core


def norm_rows(rows, gain):
    rows = rows.astype(F32)
    mean = jnp.mean(rows * rows, axis=-1, keepdims=True)
    return (rows * lax.rsqrt(mean + EPS) * gain.reshape(1, WIDTH)).astype(BF)


def lanes(shape):
    return lax.broadcasted_iota(jnp.int32, shape, len(shape) - 1)


def sublanes(shape):
    return lax.broadcasted_iota(jnp.int32, shape, len(shape) - 2)


def sine_cosine(angle):
    turns = jnp.floor(angle * (2.0 / np.pi) + 0.5)
    rest = angle - turns * 1.5703125
    rest = rest - turns * 4.837512969970703125e-4
    rest = rest - turns * 7.54978995489188216e-8
    square = rest * rest
    sine = 8.3321608736e-3 + square * -1.9515295891e-4
    sine = rest + rest * square * (-1.6666654611e-1 + square * sine)
    cosine = -1.388731625493765e-3 + square * 2.443315711809948e-5
    cosine = 4.166664568298827e-2 + square * cosine
    cosine = 1.0 - 0.5 * square + square * square * cosine
    quarter = turns.astype(jnp.int32) & 3
    odd = (quarter & 1) == 1
    out_sine = jnp.where(odd, cosine, sine)
    out_cosine = jnp.where(odd, sine, cosine)
    out_sine = jnp.where(quarter >= 2, -out_sine, out_sine)
    out_cosine = jnp.where((quarter == 1) | (quarter == 2), -out_cosine, out_cosine)
    return out_sine, out_cosine


def rope_tables(position):
    pair = (lanes((1, position.shape[1])) % (HEAD // 2)).astype(F32)
    frequency = jnp.exp(pair * (-2.0 * np.log(THETA) / HEAD))
    sine, cosine = sine_cosine(position * frequency)
    low = lanes(sine.shape) % HEAD < HEAD // 2
    return cosine, jnp.where(low, -sine, sine)


def rope(chunk, cosine, sine):
    low = lanes(chunk.shape) % HEAD < HEAD // 2
    other = jnp.where(low, pltpu.roll(chunk, 96, 1), pltpu.roll(chunk, 32, 1))
    return chunk * cosine + other * sine


def pack_kernel(gate_up_ref, down_ref, packed_ref):
    packed_ref[: 2 * SHARE, :] = gate_up_ref[...]
    packed_ref[2 * SHARE :, :] = down_ref[...]


def pack_weights(gate_up, down):
    return pl.pallas_call(
        pack_kernel,
        out_shape=jax.ShapeDtypeStruct((3 * SHARE, WIDTH), BF),
        grid=(2,),
        in_specs=[
            pl.BlockSpec((None, 2 * SHARE, WIDTH // 2), lambda i: (0, 0, i)),
            pl.BlockSpec((None, SHARE, WIDTH // 2), lambda i: (0, 0, i)),
        ],
        out_specs=pl.BlockSpec((3 * SHARE, WIDTH // 2), lambda i: (0, i)),
        compiler_params=pltpu.CompilerParams(vmem_limit_bytes=VMEM_LIMIT),
        cost_estimate=cost(1.5),
        name="pack",
    )(gate_up, down)


def cut_kernel(below_ref, above_ref, low_ref, high_ref):
    low_ref[...] = below_ref[:PART, :]
    high_ref[...] = above_ref[PART:, :]


def cut_halves(below, above):
    vmem = pl.BlockSpec(memory_space=pltpu.VMEM)
    return pl.pallas_call(
        cut_kernel,
        out_shape=(jax.ShapeDtypeStruct((PART, WIDTH), BF),) * 2,
        in_specs=[vmem] * 2,
        out_specs=(vmem,) * 2,
        compiler_params=pltpu.CompilerParams(vmem_limit_bytes=VMEM_LIMIT),
        cost_estimate=cost(0.5),
        name="cut",
    )(below, above)


def kv_kernel(rank_ref, hidden_ref, gain_ref, w_ref, kv_ref):
    normed = norm_rows(hidden_ref[...], gain_ref[...])
    position = (sublanes((ROWS, 128)) * 4 + rank_ref[0]).astype(F32)
    cosine, sine = rope_tables(position)
    projected = jnp.dot(normed, w_ref[...], preferred_element_type=F32)
    chunks = [projected[:, i * 128 : (i + 1) * 128] for i in range(5)]
    low = lanes((ROWS, 128)) < HEAD
    first = rope(chunks[0], cosine, sine)
    second = rope(chunks[1], cosine, sine)
    third = jnp.where(low, rope(chunks[2], cosine, sine), chunks[2])
    swap = lambda value: pltpu.roll(value, 64, 1)
    out = [
        jnp.where(low, first, third),
        jnp.where(low, swap(first), swap(chunks[3])),
        jnp.where(low, second, chunks[3]),
        jnp.where(low, swap(second), swap(chunks[4])),
        jnp.where(low, third, chunks[4]),
    ]
    for i in range(5):
        kv_ref[:, i * 128 : (i + 1) * 128] = out[i].astype(BF)


def query_kernel(rank_ref, hidden_ref, gain_ref, w_ref, query_ref, normed, cos, sin):
    @pl.when(pl.program_id(0) == 0)
    def _():
        normed[...] = norm_rows(hidden_ref[...], gain_ref[...])
        position = (sublanes((ROWS, 128)) * 4 + rank_ref[0]).astype(F32)
        cos[...], sin[...] = rope_tables(position)

    projected = jnp.dot(normed[...], w_ref[...], preferred_element_type=F32)
    for i in range(5):
        roped = rope(projected[:, i * 128 : (i + 1) * 128], cos[...], sin[...]).astype(BF)
        query_ref[:, i * 128 : (i + 1) * 128] = roped * jnp.asarray(0.125, BF)


def project(rank, hidden, gain, w_qkv, keys):
    steps = 1 if keys else 2
    scratch = [
        pltpu.VMEM((ROWS, WIDTH), BF),
        pltpu.VMEM((ROWS, 128), F32),
        pltpu.VMEM((ROWS, 128), F32),
    ]
    return pl.pallas_call(
        kv_kernel if keys else query_kernel,
        out_shape=jax.ShapeDtypeStruct((ROWS, KVW * steps), BF),
        grid=(steps,),
        in_specs=[
            pl.BlockSpec(memory_space=pltpu.SMEM),
            pl.BlockSpec((ROWS, WIDTH), lambda j: (0, 0)),
            pl.BlockSpec((WIDTH,), lambda j: (0,)),
            pl.BlockSpec((WIDTH, KVW), (lambda j: (0, 2)) if keys else (lambda j: (0, j))),
        ],
        out_specs=pl.BlockSpec((ROWS, KVW), lambda j: (0, j)),
        scratch_shapes=[] if keys else scratch,
        compiler_params=pltpu.CompilerParams(vmem_limit_bytes=VMEM_LIMIT),
        cost_estimate=cost(3 if keys else 0.1),
        name="prefill_kv" if keys else "prefill_query",
    )(rank, hidden, gain, w_qkv)


def column(row):
    return jnp.broadcast_to(row, (128, 128)).T


def decode_kernel(
    device_ref,
    length_ref,
    count_ref,
    slot_ref,
    index_ref,
    rows_ref,
    gain_ref,
    w_ref,
    cache_ref,
    hidden_ref,
    out_ref,
    held_ref,
    spread,
    query,
    fresh_key,
    fresh_value,
    over,
    result,
    held_score,
    held_weight,
    mixture,
    totals,
):
    tick = pl.program_id(0)
    step = tick - SLOTS
    first_slot = device_ref[0] * SLOTS

    @pl.when(tick < SLOTS)
    def _():
        normed = norm_rows(hidden_ref[...], gain_ref[...])
        projected = jnp.dot(normed, w_ref[:, QW:], preferred_element_type=F32)
        position = (index_ref[pl.ds(tick * 2, 2), :] % POSITIONS).astype(F32)
        position = jnp.concatenate([column(position[0:1]), column(position[1:2])], axis=0)
        cosine, sine = rope_tables(position)
        low = lanes((256, 128)) < HEAD
        rows = pl.ds(pl.multiple_of(tick * 256, 256), 256)
        for i in range(5):
            chunk = projected[:, i * 128 : (i + 1) * 128]
            if i < 2:
                chunk = rope(chunk, cosine, sine)
            elif i == 2:
                chunk = jnp.where(low, rope(chunk, cosine, sine), chunk)
            held_ref[rows, i * 128 : (i + 1) * 128] = chunk.astype(BF)

    index_rows = [index_ref[i : i + 1, :] for i in range(8)]

    def chosen(k):
        wanted = jnp.broadcast_to(slot_ref[k : k + 1, :], (8, 128))
        slot = sublanes((8, 128))
        return ((wanted == first_slot + slot) & (slot < SLOTS)).astype(F32).astype(BF)

    @pl.when(step == 0)
    def _():
        spread[...] = (
            sublanes((QW, 384)) % HEAD == lanes((QW, 384)) % HEAD
        ).astype(F32).astype(BF)
        rows = jnp.dot(chosen(0), rows_ref[:, 0, :], preferred_element_type=F32)
        rows += jnp.dot(chosen(1), rows_ref[:, 1, :], preferred_element_type=F32)
        normed = norm_rows(rows, gain_ref[...])
        projected = jnp.dot(normed, w_ref[...], preferred_element_type=F32)
        projected = projected.astype(BF).astype(F32)
        row = sublanes((8, 128))
        position = jnp.zeros((8, 128), F32)
        for j in range(SLOTS):
            position = jnp.where(row == j, length_ref[j].astype(F32), position)
        cosine, sine = rope_tables(position)
        chunks = [projected[:, i * 128 : (i + 1) * 128] for i in range(15)]
        roped = [rope(chunks[i], cosine, sine).astype(BF) for i in range(13)]
        whole = jnp.concatenate(roped[:10], axis=1).astype(F32) * 0.125
        head_of = sublanes((32, QW))
        keep = lanes((32, QW)) // HEAD == head_of
        group = sublanes((32, 384))
        block = (lanes((32, 384)) // HEAD == group // 4) & (group < QUERY_HEADS)
        for j in range(SLOTS):
            placed = jnp.where(keep, jnp.broadcast_to(whole[j : j + 1], (32, QW)), 0.0)
            turned = jnp.dot(placed.astype(BF), spread[...], preferred_element_type=F32)
            query[j * 32 : (j + 1) * 32, :] = jnp.where(block, turned, 0.0).astype(BF)
        fresh_key[...] = jnp.concatenate(roped[10:13], axis=1).astype(F32)
        fresh_value[...] = jnp.concatenate(chunks[12:15], axis=1)
        counts = jnp.zeros((32, 128), F32)
        for i in range(8):
            entry = i * 128 + lanes((32, 128))
            live = entry < count_ref[0]
            upper = jnp.broadcast_to(index_rows[i] // 128, (32, 128)) == sublanes((32, 128))
            upper = (upper & live).astype(F32).astype(BF)
            lower = jnp.broadcast_to(index_rows[i] % 128, (128, 128)) == sublanes((128, 128))
            lower = lower.astype(F32).astype(BF)
            counts = counts + lax.dot_general(upper, lower, NT, preferred_element_type=F32)
        over[...] = counts

    index = jnp.concatenate(index_rows, axis=1)

    @pl.when(step == 0)
    def _():
        score = lax.dot_general(query[...], held_ref[:, :384], NT, preferred_element_type=F32)
        slot = sublanes((128, 1)) // 32
        length = jnp.zeros((128, 1), jnp.int32)
        for j in range(SLOTS):
            length = jnp.where(slot == j, length_ref[j], length)
        live = lanes((128, 1024)) < count_ref[0]
        live &= jnp.broadcast_to(index // POSITIONS, (128, 1024)) == slot
        live &= jnp.broadcast_to(index % POSITIONS, (128, 1024)) < length
        held_score[...] = jnp.where(live, score, NEG)

    @pl.when(step >= 0)
    def _():
        length = length_ref[step]
        part = pl.ds(pl.multiple_of(step * 32, 32), 32)
        queries = query[part, :]
        taken = over[pl.ds(pl.multiple_of(step * 8, 8), 8), :]
        taken = jnp.concatenate([taken[i : i + 1, :] for i in range(8)], axis=1)
        cache_live = (lanes((1, POSITIONS)) < length) & (taken < 0.5)
        cache_score = lax.dot_general(queries, cache_ref[:, :384], NT, preferred_element_type=F32)
        own_score = jnp.sum(
            queries.astype(F32) * fresh_key[pl.ds(step, 1), :], axis=-1, keepdims=True
        )
        cache_live = jnp.broadcast_to(cache_live, cache_score.shape)
        cache_score = jnp.where(cache_live, cache_score, NEG)
        kept_score = held_score[part, :]
        top = jnp.maximum(
            jnp.maximum(
                jnp.max(cache_score, axis=-1, keepdims=True),
                jnp.max(kept_score, axis=-1, keepdims=True),
            ),
            own_score,
        )
        cache_weight = jnp.where(cache_live, jnp.exp(cache_score - top), 0.0)
        kept_weight = jnp.where(kept_score > NEG, jnp.exp(kept_score - top), 0.0)
        own_weight = jnp.exp(own_score - top)
        total = (
            jnp.sum(cache_weight, axis=-1, keepdims=True)
            + jnp.sum(kept_weight, axis=-1, keepdims=True)
            + own_weight
        )
        held_weight[part, :] = kept_weight.astype(BF)
        mixed = jnp.dot(cache_weight.astype(BF), cache_ref[:, 256:], preferred_element_type=F32)
        mixed += own_weight.astype(BF).astype(F32) * fresh_value[pl.ds(step, 1), :]
        mixture[part, :] = mixed
        totals[part, :] = jnp.broadcast_to(total, (32, 128))

    @pl.when(step == SLOTS - 1)
    def _():
        mixed = mixture[...] + jnp.dot(
            held_weight[...], held_ref[:, 256:], preferred_element_type=F32
        )
        total = jnp.concatenate([totals[...]] * 3, axis=1)
        head = sublanes((128, 384)) % 32
        block = (lanes((128, 384)) // HEAD == head // 4 + 1) & (head < QUERY_HEADS)
        mixed = jnp.where(block, mixed / total, 0.0).astype(BF)
        turned = lax.dot_general(mixed, spread[...], NT, preferred_element_type=F32)
        keep = lanes((32, QW)) // HEAD == sublanes((32, QW))
        rows = [
            jnp.sum(jnp.where(keep, turned[j * 32 : (j + 1) * 32], 0.0), axis=0, keepdims=True)
            for j in range(SLOTS)
        ]
        result[:SLOTS, :] = jnp.concatenate(rows, axis=0)

    @pl.when(step == SLOTS - 1)
    def _():
        good = jnp.where(sublanes((8, QW)) < SLOTS, result[...], 0.0).astype(BF)
        for k in range(2):
            out_ref[:, k, :] = lax.dot_general(
                chosen(k), good, (((0,), (0,)), ((), ())), preferred_element_type=F32
            ).astype(BF)


def decode_attention(
    device, length, count, slots, index, rows, gain, w_qkv, cache, hidden
):
    smem = pl.BlockSpec(memory_space=pltpu.SMEM)
    full = lambda shape: pl.BlockSpec(shape, lambda j: (0,) * len(shape))
    return pl.pallas_call(
        decode_kernel,
        out_shape=jax.ShapeDtypeStruct((128, 2, QW), BF),
        grid=(2 * SLOTS,),
        in_specs=[
            smem,
            smem,
            smem,
            full((2, 128)),
            full((8, 128)),
            full((128, 2, WIDTH)),
            full((WIDTH,)),
            pl.BlockSpec(
                (WIDTH, QW + KVW), lambda j: (0, 0), pipeline_mode=pl.Buffered(1)
            ),
            pl.BlockSpec((None, POSITIONS, KVW), lambda j: (jnp.maximum(j - SLOTS, 0), 0, 0)),
            pl.BlockSpec((256, WIDTH), lambda j: (jnp.minimum(j, SLOTS - 1), 0)),
        ],
        out_specs=full((128, 2, QW)),
        scratch_shapes=[
            pltpu.VMEM((1024, KVW), BF),
            pltpu.VMEM((QW, 384), BF),
            pltpu.VMEM((128, 384), BF),
            pltpu.VMEM((8, 384), F32),
            pltpu.VMEM((8, 384), F32),
            pltpu.VMEM((32, 128), F32),
            pltpu.VMEM((8, QW), F32),
            pltpu.VMEM((128, 1024), F32),
            pltpu.VMEM((128, 1024), BF),
            pltpu.VMEM((128, 384), F32),
            pltpu.VMEM((128, 128), F32),
        ],
        compiler_params=pltpu.CompilerParams(vmem_limit_bytes=VMEM_LIMIT),
        cost_estimate=cost(17),
        name="decode",
    )(device, length, count, slots, index, rows, gain, w_qkv, cache, hidden)


def attention_kernel(
    rank_ref,
    query_ref,
    own_ref,
    core_ref,
    zed_ref,
    far_ref,
    w_ref,
    hidden_ref,
    gain_ref,
    resid_ref,
    lower_ref,
    upper_ref,
    total,
    mask,
):
    group = pl.program_id(0)

    @pl.when(group == 0)
    def _():
        total[...] = jnp.zeros_like(total)
        rank = rank_ref[0]
        row = sublanes((128, 128))
        col = lanes((128, 128))
        for piece in range(4):
            other = rank ^ piece
            bound = jnp.where(other <= rank, 0, 1)
            mask[:, piece * 128 : (piece + 1) * 128] = jnp.where(col + bound <= row, 0.0, NEG)

    pieces = [own_ref, core_ref, zed_ref, far_ref]
    keys = jnp.concatenate(
        [ref[h * 128 : (h + 1) * 128, :] for h in range(2) for ref in pieces], axis=0
    )
    low = lanes((1024, 128)) < HEAD
    wide = keys.astype(F32)
    values = jnp.where(low, pltpu.roll(wide, 64, 1), wide).astype(BF)
    values = jnp.concatenate([values, jnp.ones((1024, 128), BF)], axis=1)
    low = lanes((128, 128)) < HEAD
    blocked = mask[...]
    mixed = []
    for tile in range(2):
        heads = []
        for pair in range(2):
            two = query_ref[tile * 128 : (tile + 1) * 128, pair * 128 : (pair + 1) * 128].astype(F32)
            heads.append(jnp.where(low, two, 0.0).astype(BF))
            heads.append(jnp.where(low, pltpu.roll(two, 64, 1), 0.0).astype(BF))
        out = []
        for head in heads:
            count = 512 * (tile + 1)
            score = lax.dot_general(head, keys[:count], NT, preferred_element_type=F32)
            if tile == 0:
                score = score + blocked
            else:
                score = jnp.concatenate([score[:, :512], score[:, 512:] + blocked], axis=1)
            top = jnp.max(score, axis=-1, keepdims=True)
            weight = jnp.exp(score - top).astype(BF)
            both = jnp.dot(weight, values[:count], preferred_element_type=F32)
            out.append(both[:, :128] / both[:, 128:])
        mixed.append(
            jnp.concatenate(
                [jnp.where(low, out[0], out[1]), jnp.where(low, out[2], out[3])], axis=1
            ).astype(BF)
        )
    rows = jnp.concatenate(mixed, axis=0)
    total[...] += jnp.dot(rows, w_ref[...], preferred_element_type=F32)

    @pl.when(group == 4)
    def _():
        for part in range(2):
            cut = slice(part * 128, (part + 1) * 128)
            resid = (hidden_ref[cut, :].astype(F32) + total[cut, :]).astype(BF)
            resid_ref[cut, :] = resid
            (lower_ref, upper_ref)[part][...] = norm_rows(resid, gain_ref[...])


def attention(rank, query, own, core, zed, far, w_out, hidden, gain):
    full = lambda shape: pl.BlockSpec(shape, lambda g: (0,) * len(shape))
    side = pl.BlockSpec((ROWS, 128), lambda g: (0, g))
    return pl.pallas_call(
        attention_kernel,
        out_shape=(
            jax.ShapeDtypeStruct((ROWS, WIDTH), BF),
            jax.ShapeDtypeStruct((ROWS // 2, WIDTH), BF),
            jax.ShapeDtypeStruct((ROWS // 2, WIDTH), BF),
        ),
        grid=(5,),
        in_specs=[
            pl.BlockSpec(memory_space=pltpu.SMEM),
            pl.BlockSpec((ROWS, 256), lambda g: (0, g)),
            side,
            side,
            side,
            side,
            pl.BlockSpec((256, WIDTH), lambda g: (g, 0)),
            full((ROWS, WIDTH)),
            full((WIDTH,)),
        ],
        out_specs=(
            full((ROWS, WIDTH)),
            full((ROWS // 2, WIDTH)),
            full((ROWS // 2, WIDTH)),
        ),
        scratch_shapes=[
            pltpu.VMEM((ROWS, WIDTH), F32),
            pltpu.VMEM((128, 512), F32),
        ],
        compiler_params=pltpu.CompilerParams(vmem_limit_bytes=VMEM_LIMIT),
        cost_estimate=cost(0.1),
        name="attention",
    )(rank, query, own, core, zed, far, w_out, hidden, gain)


def decode_rows_kernel(back_ref, w_ref, decode_ref, gain_ref, resid_ref, normed_ref):
    mixed = jnp.sum(back_ref[...].astype(F32), axis=0)
    mixed = jnp.concatenate([mixed, jnp.zeros((14, WIDTH), F32)], axis=0).astype(BF)
    single = decode_ref[...].astype(F32)
    hidden = jnp.concatenate([single, jnp.zeros((14, WIDTH), F32)], axis=0)
    resid = (hidden + jnp.dot(mixed, w_ref[...], preferred_element_type=F32)).astype(BF)
    resid_ref[...] = resid
    normed_ref[...] = norm_rows(resid, gain_ref[...])


def decode_rows(back, w_out, decode, gain):
    vmem = pl.BlockSpec(memory_space=pltpu.VMEM)
    return pl.pallas_call(
        decode_rows_kernel,
        out_shape=(jax.ShapeDtypeStruct((16, WIDTH), BF),) * 2,
        in_specs=[vmem] * 4,
        out_specs=(vmem,) * 2,
        compiler_params=pltpu.CompilerParams(vmem_limit_bytes=VMEM_LIMIT),
        cost_estimate=cost(0.1),
        name="decode_rows",
    )(back, w_out, decode, gain)


def hidden_units(rows, packs, lows, highs, act):
    cut = 2 * SHARE - PART
    weights = [(ref[:SHARE, :], ref[SHARE : 2 * SHARE, :], ref[2 * SHARE :, :]) for ref in packs]
    for low, high in zip(lows, highs):
        up_rows = jnp.concatenate([low[SHARE:, :], high[:cut, :]], axis=0)
        weights.append((low[:SHARE, :], up_rows, high[cut:, :]))
    for k, (gate_rows, up_rows, _) in enumerate(weights):
        gate = lax.dot_general(rows, gate_rows, NT, preferred_element_type=F32)
        up = lax.dot_general(rows, up_rows, NT, preferred_element_type=F32)
        act[:, k * SHARE : (k + 1) * SHARE] = (gate / (1.0 + jnp.exp(-gate)) * up).astype(BF)
    down = jnp.concatenate([down_rows for _, _, down_rows in weights], axis=0)
    return jnp.dot(act[...], down, preferred_element_type=F32)


def first_kernel(*refs):
    rows = jnp.concatenate([refs[0][...], refs[1][...]], axis=0)
    refs[4][...] = hidden_units(rows, refs[2:4], (), (), refs[5])


def second_kernel(*refs):
    rows = jnp.concatenate([refs[0][...], refs[1][...]], axis=0)
    down = hidden_units(rows, refs[2:6], refs[6:8], refs[8:10], refs[13])
    refs[12][...] = refs[11][...].astype(F32) + (refs[10][...] + down)


def guest_kernel(*refs):
    rows = jnp.concatenate([ref[...] for ref in refs[:4]], axis=0)
    down = hidden_units(rows, refs[4:10], refs[10:12], refs[12:14], refs[17]).astype(BF)
    for ref, start, stop in zip(refs[14:17], (0, 144, 272), (144, 272, 288)):
        ref[...] = down[start:stop]


def feed_forward(kernel, inputs, outputs, rows, shares, time, name):
    vmem = pl.BlockSpec(memory_space=pltpu.VMEM)
    return pl.pallas_call(
        kernel,
        out_shape=outputs,
        in_specs=[vmem] * len(inputs),
        out_specs=(vmem,) * len(outputs),
        scratch_shapes=[pltpu.VMEM((rows, shares * SHARE), BF)],
        compiler_params=pltpu.CompilerParams(vmem_limit_bytes=VMEM_LIMIT),
        cost_estimate=cost(time),
        name=name,
    )(*inputs)


def final_kernel(start_ref, extra_ref, mine_ref, first_ref, second_ref, prefill_ref, decode_ref):
    for part, ref in ((0, first_ref), (1, second_ref)):
        cut = slice(part * 128, (part + 1) * 128)
        prefill_ref[cut, :] = (start_ref[cut, :] + ref[:128, :].astype(F32)).astype(BF)
    alone = mine_ref[...].astype(F32) + first_ref[128:, :].astype(F32)
    decode_ref[...] = (extra_ref[...].astype(F32) + alone)[:2].astype(BF)


def final_sum(start, extra, mine, first, second):
    return pl.pallas_call(
        final_kernel,
        out_shape=(
            jax.ShapeDtypeStruct((ROWS, WIDTH), BF),
            jax.ShapeDtypeStruct((2, WIDTH), BF),
        ),
        in_specs=[pl.BlockSpec(memory_space=pltpu.VMEM)] * 5,
        compiler_params=pltpu.CompilerParams(vmem_limit_bytes=VMEM_LIMIT),
        cost_estimate=cost(1),
        name="final",
    )(start, extra, mine, first, second)


def body(
    prefill_hidden,
    decode_hidden,
    attn_gain,
    w_qkv,
    w_out,
    ffn_gain,
    w_gate_up,
    w_down,
    key_value_cache,
    cache_len,
    slot_of_request,
    held_hidden,
    recomputed_index,
    recomp_count,
):
    device = lax.axis_index("req").astype(jnp.int32).reshape(1)
    rank = device % 4
    gain, gain2 = attn_gain, ffn_gain
    index = recomputed_index.reshape(8, 128)

    w_all = w_out
    w_qkv, w_out, key_value_cache, held_hidden, prefill_hidden = in_hbm(
        w_qkv, w_out, key_value_cache, held_hidden, prefill_hidden
    )
    total = 2 * SIDE**3
    spread = jnp.broadcast_to(decode_hidden[None], (total, 2, WIDTH))
    every_row = lax.all_to_all(spread, "req", 0, 0)

    packed = pack_weights(*in_hbm(jnp.swapaxes(w_gate_up, 1, 2), w_down))
    (kv,) = in_hbm(project(rank, prefill_hidden, gain, w_qkv, True))
    zed = send(kv, pair_z)
    core = send(kv, other_core)
    packed, kv = lax.optimization_barrier((packed, kv))
    below = send(packed, next_z)
    above = send(packed, last_z)
    packed_core = send(packed, other_core)
    query = project(rank, prefill_hidden, gain, w_qkv, False)
    every_row, query = lax.optimization_barrier((every_row, query))
    outgoing = decode_attention(
        device,
        cache_len,
        recomp_count,
        slot_of_request.reshape(128, 2).T,
        index,
        every_row,
        gain,
        w_qkv,
        key_value_cache,
        held_hidden,
    )
    outgoing, zed, core, packed_core = lax.optimization_barrier(
        (outgoing, zed, core, packed_core)
    )
    far = send(zed, other_core)
    core, zed, far = in_hbm(core, zed, far)
    below, above, packed_core = lax.optimization_barrier((below, above, packed_core))
    far_low, far_high = cut_halves(below, above)
    far_low = send(far_low, next_z)
    far_high = send(far_high, last_z)
    back = lax.all_to_all(outgoing, "req", 0, 0)

    resid, lower, upper = attention(
        rank, query, kv, core, zed, far, w_out, prefill_hidden, gain2
    )
    from_last = send(lower, next_x)
    from_next = send(upper, last_x)
    (mine,) = feed_forward(
        first_kernel,
        (lower, upper, packed, packed_core),
        (jax.ShapeDtypeStruct((ROWS, WIDTH), F32),),
        ROWS,
        2,
        0.1,
        "feed_first",
    )
    mine, back = lax.optimization_barrier((mine, back))
    below, above, back, from_last, from_next = lax.optimization_barrier(
        (below, above, back, from_last, from_next)
    )
    below_core = send(below, other_core)
    above_core = send(above, other_core)
    extra, alone = decode_rows(back, w_all, decode_hidden, gain2)
    guest = send(alone, next_x)
    alone, far_low, far_high = lax.optimization_barrier((alone, far_low, far_high))
    far_low_core = send(far_low, other_core)
    far_high_core = send(far_high, other_core)
    gathered = (below, below_core, above, above_core)
    distant = (far_low, far_low_core, far_high, far_high_core)
    to_last, to_next, alone = feed_forward(
        guest_kernel,
        (from_last, guest, from_next, alone, packed, packed_core) + gathered + distant,
        tuple(jax.ShapeDtypeStruct((n, WIDTH), BF) for n in (144, 128, 16)),
        ROWS + 32,
        8,
        8,
        "feed_guest",
    )
    to_last, to_next, mine = lax.optimization_barrier((to_last, to_next, mine))
    first = send(to_last, last_x)
    second = send(to_next, next_x)
    (start,) = feed_forward(
        second_kernel,
        (lower, upper) + gathered + distant + (mine, resid),
        (jax.ShapeDtypeStruct((ROWS, WIDTH), F32),),
        ROWS,
        6,
        6,
        "feed_second",
    )
    return final_sum(start, extra, alone, first, second)


def solution(mesh):
    return jax.shard_map(
        body,
        mesh=mesh,
        in_specs=(
            P("req", None),
            P("req", None),
            P(),
            P(),
            P(),
            P(),
            P("req", None, None),
            P("req", None, None),
            P("req", None, None),
            P("req"),
            P(),
            P("req", None),
            P("req"),
            P("req"),
        ),
        out_specs=(P("req", None), P("req", None)),
        check_vma=False,
    )
```
